32 devices in a mesh: dp: 8 (over z, core), fsdp: 4 (over y, x).
Axes of the slice: x: 2, y: 2, z: 4, core: 2. Of those that a mesh axis runs over, the one named last changes fastest.
Arguments:
- tokens: bfloat16 [160, 196, 768], P(('dp', 'fsdp')), may hold values from -6 to 6
- mask: int32 [160, 196], P(('dp', 'fsdp')), may hold values from 0 to 1, as said below
- cotangent: bfloat16 [160, 196, 768], P(('dp', 'fsdp')), may hold values from -6 to 6
- ln1_gain: bfloat16 [768], P('fsdp'), may hold values from 0.099609375 to 1.8984375
- ln1_bias: bfloat16 [768], P('fsdp'), may hold values from -4 to 4
- w_qkv: bfloat16 [768, 2304], P('fsdp'), may hold values from -0.21875 to 0.21875
- qv_bias: bfloat16 [1536], P('fsdp'), may hold values from -1.5 to 1.5
- w_out: bfloat16 [768, 768], P('fsdp'), may hold values from -1.75 to 1.75
- out_bias: bfloat16 [768], P('fsdp'), may hold values from -4 to 4
- ln2_gain: bfloat16 [768], P('fsdp'), may hold values from 0.099609375 to 1.8984375
- ln2_bias: bfloat16 [768], P('fsdp'), may hold values from -4 to 4
- w_up: bfloat16 [768, 3072], P('fsdp'), may hold values from -0.21875 to 0.21875
- up_bias: bfloat16 [3072], P('fsdp'), may hold values from -4 to 4
- w_down: bfloat16 [3072, 768], P('fsdp'), may hold values from -0.109375 to 0.109375
- down_bias: bfloat16 [768], P('fsdp'), may hold values from -4 to 4
Outputs:
- layer_out: bfloat16 [160, 196, 768], P(('dp', 'fsdp'))
- grad_tokens: bfloat16 [160, 196, 768], P(('dp', 'fsdp'))
- grad_ln1_gain: float32 [768], P('fsdp')
- grad_ln1_bias: float32 [768], P('fsdp')
- grad_w_qkv: float32 [768, 2304], P('fsdp')
- grad_qv_bias: float32 [1536], P('fsdp')
- grad_w_out: float32 [768, 768], P('fsdp')
- grad_out_bias: float32 [768], P('fsdp')
- grad_ln2_gain: float32 [768], P('fsdp')
- grad_ln2_bias: float32 [768], P('fsdp')
- grad_w_up: float32 [768, 3072], P('fsdp')
- grad_up_bias: float32 [3072], P('fsdp')
- grad_w_down: float32 [3072, 768], P('fsdp')
- grad_down_bias: float32 [768], P('fsdp')
The draws below stay inside these ranges and needn't reach their ends.
Inputs may be any that keep to these rules, and one draw needn't show every extreme that they name: `mask`: each image keeps at least one of its 196 patch slots.
All inputs are finite; a program needn't handle non-finite values.
Results may differ from the reference program's by a relative error of at most 0.013.
Values may be sent and summed in bfloat16 or wider, within the bound.
No kernel may reach another device: no remote copies, remote signals or barrier semaphores. Data moves between devices by JAX's collectives and lax.ppermute only.
A program may use at most 256 MiB of HBM per device.

```python
import jax
import jax.numpy as jnp
from jax import lax

D = 768
HD = 64
FF = 3072
S = 196
IMG_DEV = 5
IMAGES = 160


def draw_mask(key, part):
    first_key, second_key, third_key = jax.random.split(key, 3)
    keep_share = jax.random.randint(first_key, (IMAGES, 1), 300, 1001)
    ticket_draw = jax.random.randint(second_key, (IMAGES, S), 0, 1000)
    chosen_slot = jax.random.randint(third_key, (IMAGES, 1), 0, S)
    slot_index = jnp.arange(S, dtype=jnp.int32)[None, :]
    return jnp.logical_or(ticket_draw < keep_share, slot_index == chosen_slot).astype(jnp.int32)


def raised(entries, stream_key, source, target, blocks, factor):
    def block_of(position):
        return (jnp.arange(entries.shape[position]) // (entries.shape[position] // blocks)).reshape((-1,) + (1,) * (entries.ndim - 1 - position))

    first = jax.random.permutation(stream_key, blocks)[block_of(target)]
    far = (block_of(target) + blocks // 2) % blocks
    return jnp.where((block_of(source) == first) | (block_of(source) == far), factor * entries, entries)


def levels(own_key, shape, pieces, least, high):
    factor_of, own = 1.0, jax.random.fold_in(own_key, 6)
    for dim, shards_of in pieces:
        draws = jnp.exp(jax.random.uniform(jax.random.fold_in(own, dim), (shards_of,), jnp.float32, least / len(pieces), high / len(pieces)))
        factor_of = factor_of * jnp.repeat(draws, shape[dim] // shards_of).reshape([-1 if axis == dim else 1 for axis in range(len(shape))])
    return factor_of


def bell_draw(stream_key, extent, deviation, reach, cuts=(), kind=jnp.bfloat16):
    values = jax.random.normal(stream_key, extent, jnp.float32) * deviation
    if len(cuts) > 0:
        values = levels(stream_key, extent, cuts, -0.22, 0.18) * values
    return jnp.clip(values, min=-reach, max=reach).astype(kind)


def heavy_noise(own_key, dims, deviation, limit, shards, heavy, held_as=jnp.bfloat16):
    drawn = deviation * jax.random.normal(own_key, dims, jnp.float32)
    if shards:
        drawn = drawn * levels(own_key, dims, shards, -0.22, 0.18)
    return jnp.clip(raised(drawn, jax.random.fold_in(own_key, 3), *heavy), -limit, limit).astype(held_as)


def setup_inputs(seed: int = 0) -> dict:
    key_list = jax.random.split(jax.random.key(seed), 16)
    tokens = bell_draw(key_list[0], (IMAGES, S, D), 1.0, 6.0, ((0, 32),))
    mask = draw_mask(jax.random.fold_in(key_list[15], 71), 0)
    cotangent = heavy_noise(key_list[2], (IMAGES, S, D), 1.0, 6.0, ((0, 32),), (0, 2, 32, 2.75))
    ln1_gain = jnp.clip(1.0 + 0.18 * jax.random.normal(key_list[3], (D,), jnp.float32), 0.099609375, 1.8984375).astype(jnp.bfloat16)
    ln1_bias = bell_draw(key_list[4], (D,), 0.3, 4.0, ((0, 4),))
    w_qkv = bell_draw(key_list[5], (D, 3 * D), D ** -0.5, 0.21875, ((0, 4),))
    qv_bias = bell_draw(key_list[6], (2 * D,), 0.1, 1.5, ((0, 4),))
    w_out = bell_draw(key_list[7], (D, D), (D // 64) ** -0.5, 1.75, ((0, 4),))
    out_bias = bell_draw(key_list[8], (D,), 0.3, 4.0, ((0, 4),))
    ln2_gain = jnp.clip(1.0 + 0.18 * jax.random.normal(key_list[9], (D,), jnp.float32), 0.099609375, 1.8984375).astype(jnp.bfloat16)
    ln2_bias = bell_draw(key_list[10], (D,), 0.3, 4.0, ((0, 4),))
    w_up = bell_draw(key_list[11], (D, FF), D ** -0.5, 0.21875, ((0, 4),))
    up_bias = bell_draw(key_list[12], (FF,), 0.3, 4.0, ((0, 4),))
    w_down = bell_draw(key_list[13], (FF, D), FF ** -0.5, 0.109375, ((0, 4),))
    down_bias = bell_draw(key_list[14], (D,), 0.3, 4.0, ((0, 4),))
    return {"tokens": tokens, "mask": mask, "cotangent": cotangent, "ln1_gain": ln1_gain, "ln1_bias": ln1_bias, "w_qkv": w_qkv, "qv_bias": qv_bias, "w_out": w_out, "out_bias": out_bias, "ln2_gain": ln2_gain, "ln2_bias": ln2_bias, "w_up": w_up, "up_bias": up_bias, "w_down": w_down, "down_bias": down_bias}


EPS = 1e-06
HIGH = lax.Precision.HIGHEST

@jax.custom_vjp
def low(v):
    return lax.optimization_barrier(v.astype(jnp.bfloat16)).astype(jnp.float32)

@jax.custom_vjp
def low_back(v):
    return v

def low_keep(v):
    return (low(v), None)

def low_pass(kept, grad):
    return (grad,)

def back_keep(v):
    return (v, None)

def back_low(kept, grad):
    return (low(grad),)
low.defvjp(low_keep, low_pass)
low_back.defvjp(back_keep, back_low)

def norm(values, gain, shift):
    mean_value = lax.optimization_barrier(jnp.mean(values, axis=-1, keepdims=True))
    centred = values - mean_value
    variance = lax.optimization_barrier(jnp.mean(centred * centred, axis=-1, keepdims=True))
    return centred * lax.rsqrt(variance + EPS) * gain + shift

def layer(inputs, keep, params):
    ln1_gain, ln1_bias, w_qkv, qv_bias, w_out, out_bias, ln2_gain, ln2_bias, w_up, up_bias, w_down, down_bias = params
    image_count, slot_count, width = inputs.shape
    heads = width // HD
    normed_one = low(norm(inputs, ln1_gain, ln1_bias))
    full_bias = jnp.concatenate([qv_bias[:width], jnp.zeros((width,), jnp.float32), qv_bias[width:]])
    projected = jnp.einsum('gsd,de->gse', normed_one, w_qkv, precision=HIGH) + full_bias
    projected = low(low_back(projected))
    query = projected[..., :width].reshape(image_count, slot_count, heads, HD)
    key_part = projected[..., width:2 * width].reshape(image_count, slot_count, heads, HD)
    value = projected[..., 2 * width:].reshape(image_count, slot_count, heads, HD)
    scores = jnp.einsum('gqhe,gkhe->ghqk', query, key_part, precision=HIGH) * HD ** (-0.5)
    scores = low_back(scores)
    valid = keep[:, None, None, :] > 0.5
    scores = jnp.where(valid, scores, -1e+30)
    top = lax.optimization_barrier(jnp.max(scores, axis=-1, keepdims=True))
    lse = top + jnp.log(lax.optimization_barrier(jnp.sum(jnp.exp(scores - top), axis=-1, keepdims=True)))
    probs = low(jnp.exp(scores - lse))
    mixed = jnp.einsum('ghqk,gkhe->gqhe', probs, value, precision=HIGH).reshape(image_count, slot_count, width)
    mixed = low(low_back(mixed))
    attended = low_back(jnp.einsum('gsd,de->gse', mixed, w_out, precision=HIGH) + out_bias)
    middle = inputs + attended
    normed_two = low(norm(middle, ln2_gain, ln2_bias))
    upward = low_back(jnp.einsum('gsd,df->gsf', normed_two, w_up, precision=HIGH) + up_bias)
    active = low(jax.nn.gelu(upward, approximate=False))
    downward = low_back(jnp.einsum('gsf,fd->gsd', active, w_down, precision=HIGH) + down_bias)
    return keep[..., None] * (middle + downward)

def reference(tokens, mask, cotangent, ln1_gain, ln1_bias, w_qkv, qv_bias, w_out, out_bias, ln2_gain, ln2_bias, w_up, up_bias, w_down, down_bias):
    params = tuple((item.astype(jnp.float32) for item in (ln1_gain, ln1_bias, w_qkv, qv_bias, w_out, out_bias, ln2_gain, ln2_bias, w_up, up_bias, w_down, down_bias)))
    group = 4 * IMG_DEV
    blocks = IMAGES // group
    inputs = tokens.astype(jnp.float32).reshape(blocks, group, S, D)
    keep = mask.astype(jnp.float32).reshape(blocks, group, S)
    seed_grad = cotangent.astype(jnp.float32).reshape(blocks, group, S, D)

    def forward(all_inputs, weights):

        def one_block(pair):
            return layer(pair[0], pair[1], weights)
        return lax.map(jax.checkpoint(one_block), (all_inputs, keep))
    result, pullback = jax.vjp(forward, inputs, params)
    grad_inputs, grads = pullback(seed_grad)
    return (result.reshape(IMAGES, S, D).astype(jnp.bfloat16), grad_inputs.reshape(IMAGES, S, D).astype(jnp.bfloat16), grads[0], grads[1], grads[2], grads[3], grads[4], grads[5], grads[6], grads[7], grads[8], grads[9], grads[10], grads[11])
```

```python
import functools

import jax
import jax.numpy as jnp
import numpy as np
from jax import lax
from jax.experimental import pallas as pl
from jax.experimental.pallas import tpu as pltpu
from jax.sharding import PartitionSpec as P

HD = 64
EPS = 1e-06
F32 = jnp.float32
BF = jnp.bfloat16
MB = 2**20
SCORE_SCALE = np.float32(np.log2(np.e) * HD ** (-0.5))
MASKED = np.float32(-1e30)
SD = jax.ShapeDtypeStruct
ANY = pl.BlockSpec(memory_space=pl.ANY)
VM = pl.BlockSpec(memory_space=pltpu.VMEM)


def dot(a, b, ca, cb):
    return lax.dot_general(a, b, (((ca,), (cb,)), ((), ())), preferred_element_type=F32)


def params(mb=58):
    return pltpu.CompilerParams(vmem_limit_bytes=mb * MB)


def cost(flops, moved):
    return pl.CostEstimate(flops=int(flops), bytes_accessed=int(moved), transcendentals=0)


def normalized(values):
    mean = jnp.mean(values, axis=-1, keepdims=True)
    centred = values - mean
    rsq = lax.rsqrt(jnp.mean(centred * centred, axis=-1, keepdims=True) + EPS)
    return centred * rsq, rsq


def norm_back(e, xhat, rsq):
    return rsq * (
        e
        - jnp.mean(e, axis=-1, keepdims=True)
        - xhat * jnp.mean(e * xhat, axis=-1, keepdims=True)
    )


def run_copies(pairs, sems, base=0):
    copies = [
        pltpu.make_async_copy(src, dst, sems.at[base + n]) for n, (src, dst) in enumerate(pairs)
    ]
    return copies


G1, B1, QB, VB, OB, G2, B2, DB, UB = range(9)


def pack_first_kernel(sc, wqkv, wout, small, sp, sq, sems):
    width = wout.shape[1]
    half = wout.shape[0] // 2
    at = pl.multiple_of(sc[1] * half, 16)
    rows = pl.ds(at, half)
    copies = run_copies(
        [
            (wqkv.at[rows, pl.ds(0, 2 * width)], sp.at[pl.ds(0, half), :]),
            (small, sp.at[pl.ds(half, 16), pl.ds(0, small.shape[1])]),
            (wqkv.at[rows, pl.ds(2 * width, width)], sq.at[:, pl.ds(0, width)]),
            (wout.at[rows, :], sq.at[:, pl.ds(width, width)]),
        ],
        sems,
    )
    for c in copies:
        c.start()
    for c in copies:
        c.wait()


def pack_first(sc, wqkv, wout, small):
    half, width = wout.shape[0] // 2, wout.shape[1]
    return pl.pallas_call(
        pack_first_kernel,
        grid_spec=pltpu.PrefetchScalarGridSpec(
            num_scalar_prefetch=1,
            in_specs=[ANY] * 3,
            out_specs=[ANY] * 2,
            scratch_shapes=[pltpu.SemaphoreType.DMA((4,))],
        ),
        out_shape=[SD((half + 16, 2 * width), BF), SD((half, 2 * width), BF)],
        compiler_params=params(2),
        name="pack_first",
    )(sc, wqkv, wout, small)


def pack_mlp_kernel(sc, wup, wdown, sp0, sq0, sp1, sq1, sems):
    half = wup.shape[0] // 2
    width = wdown.shape[1]
    part = wdown.shape[0] // 2
    rows = pl.ds(pl.multiple_of(sc[1] * half, 16), half)
    pairs = []
    for k, (sp, sq) in enumerate(((sp0, sq0), (sp1, sq1))):
        for b in range(4):
            at = pl.multiple_of((sc[0] ^ b) * width + k * part, 128)
            pairs.append((wup.at[rows, pl.ds(at, part)], sp.at[b]))
        at = pl.multiple_of(k * part + sc[1] * (part // 2), 16)
        pairs.append((wdown.at[pl.ds(at, part // 2), :], sq))
    copies = run_copies(pairs, sems)
    for c in copies:
        c.start()
    for c in copies:
        c.wait()


def pack_mlp(sc, wup, wdown):
    half, width = wup.shape[0] // 2, wdown.shape[1]
    part = wdown.shape[0] // 2
    return pl.pallas_call(
        pack_mlp_kernel,
        grid_spec=pltpu.PrefetchScalarGridSpec(
            num_scalar_prefetch=1,
            in_specs=[ANY] * 2,
            out_specs=[ANY] * 4,
            scratch_shapes=[pltpu.SemaphoreType.DMA((10,))],
        ),
        out_shape=[SD((4, half, part), BF), SD((part // 2, width), BF)] * 2,
        compiler_params=params(2),
        name="pack_mlp",
    )(sc, wup, wdown)


def place_rows(dst, sc, own, pieces, cols, src_cols, height):
    half = height // 2
    shard, core = sc[0], sc[1]
    pairs = []
    if own is not None:
        src, take = own
        pairs.append((src.at[:, take], dst.at[pl.ds(pl.multiple_of(shard * height, 16), height), cols]))
    for side in range(2):
        which = core if side == 0 else 1 - core
        for r in range(1, 4):
            at = pl.multiple_of((shard ^ r) * height + which * half, 16)
            pairs.append(
                (pieces[side * 3 + r - 1].at[pl.ds(0, half), src_cols], dst.at[pl.ds(at, half), cols])
            )
    return pairs


def fill_small(sc, pieces, sm, height):
    shard = sc[0]
    vals = [pieces[r].astype(F32) for r in range(4)]

    def of(j):
        got = vals[3]
        for r in range(3):
            got = jnp.where(shard == (j ^ r), vals[r], got)
        return got[:, :height]

    by = [of(j) for j in range(4)]
    sm[...] = jnp.zeros_like(sm)
    for j in range(4):
        cols = slice(j * height, (j + 1) * height)
        sm[G1 : B1 + 1, cols] = by[j][0:2]
        sm[OB : DB + 1, cols] = by[j][4:8]
        for n in range(2):
            at = (2 * j + n) % 4 * height
            row = QB if j < 2 else VB
            sm[row : row + 1, at : at + height] = by[j][2 + n : 3 + n]
        for n in range(4):
            sm[UB + j : UB + j + 1, n * height : (n + 1) * height] = by[j][8 + n : 9 + n]


def project_kernel(sc, tok, small, own, *rest, slots):
    pp, pq = rest[:6], rest[6:12]
    h1, qkv, sm, wbuf, sbuf, sems, ssems = rest[12:]
    images, count, width = tok.shape
    height = own.shape[0]
    step = pl.program_id(0)
    two = pl.ds(0, 2 * width)
    third = pl.ds(2 * width, width)
    first = run_copies(place_rows(wbuf, sc, (own, two), pp, two, two, height), sems)
    last = run_copies(
        place_rows(wbuf, sc, (own, third), pq, third, pl.ds(0, width), height), sems, len(first)
    )

    rows = pl.ds(height // 2, 16)
    lanes = pl.ds(0, small.shape[1])
    table = [(small, sbuf.at[0])]
    table += [(pp[r - 1].at[rows, lanes], sbuf.at[r]) for r in range(1, 4)]
    table = run_copies(table, ssems)

    @pl.when(step == 0)
    def _():
        for c in table + first + last:
            c.start()
        for c in table:
            c.wait()
        fill_small(sc, sbuf, sm, height)
        for i in range(images):
            xhat, _ = normalized(tok[i].astype(F32))
            low = (xhat * sm[G1 : G1 + 1, :] + sm[B1 : B1 + 1, :]).astype(BF)
            tail = count // 8 * 8
            h1[i * slots + tail : (i + 1) * slots, :] = jnp.zeros((slots - tail, width), BF)
            h1[i * slots : i * slots + count, :] = low
        for c in first:
            c.wait()

    @pl.when(step == 2)
    def _():
        for c in last:
            c.wait()

    row = jnp.where(step == 0, sm[QB : QB + 1, :], sm[VB : VB + 1, :])
    row = jnp.where(step == 1, jnp.zeros_like(row), row)
    weight = wbuf[:, pl.ds(pl.multiple_of(step * width, 128), width)]
    qkv[...] = (dot(h1[...], weight, 1, 0) + row).astype(BF)


def project(sc, tok, small, own, pieces, slots):
    images, _, width = tok.shape
    rows = images * slots
    full = lambda *s: pl.BlockSpec(s, lambda j, sc: (0,) * len(s))
    return pl.pallas_call(
        functools.partial(project_kernel, slots=slots),
        grid_spec=pltpu.PrefetchScalarGridSpec(
            num_scalar_prefetch=1,
            grid=(3,),
            in_specs=[full(*tok.shape)] + [ANY] * 14,
            out_specs=[
                full(rows, width),
                pl.BlockSpec((rows, width), lambda j, sc: (0, j)),
                full(16, width),
            ],
            scratch_shapes=[
                pltpu.VMEM((width, 3 * width), BF),
                pltpu.VMEM((4,) + small.shape, BF),
                pltpu.SemaphoreType.DMA((14,)),
                pltpu.SemaphoreType.DMA((4,)),
            ],
        ),
        out_shape=[SD((rows, width), BF), SD((rows, 3 * width), BF), SD((16, width), F32)],
        compiler_params=params(),
        cost_estimate=cost(6 * rows * width * width, 14 * MB),
        name="project",
    )(sc, tok, small, own, *pieces)


def head_lanes():
    return lax.broadcasted_iota(jnp.int32, (1, 2 * HD), 1) < HD


def attend_kernel(q, k, v, mask, o, *, pairs):
    low_half = head_lanes()
    keep = mask[0] > 0
    zero = jnp.zeros((), BF)
    for p in range(pairs):
        sl = slice(p * 2 * HD, (p + 1) * 2 * HD)
        qp, kp, vp = q[:, sl], k[:, sl], v[:, sl]
        outs = []
        for a in range(2):
            mine = low_half if a == 0 else jnp.logical_not(low_half)
            s = dot(jnp.where(mine, qp, zero), kp, 1, 1)
            s = jnp.where(keep, s * SCORE_SCALE, MASKED)
            e = jnp.exp2(s - jnp.max(s, axis=-1, keepdims=True))
            prob = (e * (1.0 / jnp.sum(e, axis=-1, keepdims=True))).astype(BF)
            outs.append(dot(prob, jnp.where(mine, vp, zero), 1, 0))
        o[:, sl] = (outs[0] + outs[1]).astype(BF)


def attend(qkv, mask_row, slots):
    rows, three = qkv.shape
    width, images = three // 3, rows // slots
    block = lambda n: pl.BlockSpec((slots, width), lambda i: (i, n))
    return pl.pallas_call(
        functools.partial(attend_kernel, pairs=width // (2 * HD)),
        grid=(images,),
        in_specs=[block(0), block(1), block(2), pl.BlockSpec((1, 1, slots), lambda i: (i, 0, 0))],
        out_specs=block(0),
        out_shape=SD((rows, width), BF),
        compiler_params=params(),
        cost_estimate=cost(11e9, 6 * MB),
        name="attend",
    )(qkv, qkv, qkv, mask_row)


def attend_back_kernel(q, k, v, do, mask, dx, *, pairs):
    low_half = head_lanes()
    keep = mask[...] > 0
    zero = jnp.zeros((), BF)
    scale = np.float32(HD ** (-0.5))
    wide = pairs * 2 * HD
    for p in range(pairs):
        sl = slice(p * 2 * HD, (p + 1) * 2 * HD)
        qp, kp, vp, dop = q[:, sl], k[:, sl], v[:, sl], do[:, sl]
        gq, gk, gv = [], [], []
        for a in range(2):
            mine = low_half if a == 0 else jnp.logical_not(low_half)
            qm, km, dm = (jnp.where(mine, t, zero) for t in (qp, kp, dop))
            s = dot(km, qp, 1, 1)
            s = jnp.where(keep, s * SCORE_SCALE, MASKED)
            e = jnp.exp2(s - jnp.max(s, axis=0, keepdims=True))
            prob = e * (1.0 / jnp.sum(e, axis=0, keepdims=True))
            gv.append(dot(prob.astype(BF), dm, 1, 0))
            weighed = prob * dot(vp, dm, 1, 1)
            inner = jnp.sum(weighed, axis=0, keepdims=True)
            ds = (weighed - prob * inner).astype(BF)
            gk.append(dot(ds, qm, 1, 0))
            gq.append(dot(ds, km, 0, 0))
        at = p * 2 * HD
        dx[:, at : at + 2 * HD] = ((gq[0] + gq[1]) * scale).astype(BF)
        dx[:, wide + at : wide + at + 2 * HD] = ((gk[0] + gk[1]) * scale).astype(BF)
        dx[:, 2 * wide + at : 2 * wide + at + 2 * HD] = (gv[0] + gv[1]).astype(BF)


def attend_back(qkv, do, mask_col, slots, group):
    rows, three = qkv.shape
    part, images = three // 6, rows // slots
    block = lambda n: pl.BlockSpec((slots, part), lambda i: (i, n + group))
    return pl.pallas_call(
        functools.partial(attend_back_kernel, pairs=part // (2 * HD)),
        grid=(images,),
        in_specs=[block(0), block(2), block(4), block(0), pl.BlockSpec((slots, 1), lambda i: (i, 0))],
        out_specs=pl.BlockSpec((slots, 3 * part), lambda i: (i, 0)),
        out_shape=SD((rows, 3 * part), BF),
        compiler_params=params(),
        cost_estimate=cost(10e9, 6 * MB),
        name="attend_back%d" % group,
    )(qkv, qkv, qkv, do, mask_col)


def middle_kernel(sc, tok, o, sm, cot, keep, own, *rest, slots):
    pieces = rest[:6]
    mid, h2, dm, wbuf, sems = rest[6:]
    images, count, width = tok.shape
    every = pl.ds(0, width)
    copies = run_copies(
        place_rows(wbuf, sc, (own, every), pieces, every, pl.ds(width, width), own.shape[0]), sems
    )
    for c in copies:
        c.start()
    tail = count // 8 * 8
    for i in range(images):
        sl = slice(i * slots, i * slots + count)
        dm[i * slots + tail : (i + 1) * slots, :] = jnp.zeros((slots - tail, width), BF)
        dm[sl, :] = (cot[i].astype(F32) * keep[sl, :]).astype(BF)
    for c in copies:
        c.wait()
    mid[...] = dot(o[...], wbuf[...], 1, 0) + sm[OB : OB + 1, :]
    for i in range(images):
        sl = slice(i * slots, i * slots + count)
        mid[sl, :] += tok[i].astype(F32)
    xhat, _ = normalized(mid[...])
    h2[...] = (xhat * sm[G2 : G2 + 1, :] + sm[B2 : B2 + 1, :]).astype(BF)


def middle_part(sc, tok, o, sm, cot, keep, own, pieces, slots):
    rows, width = o.shape
    full = lambda a: pl.BlockSpec(a.shape, lambda j, sc: (0,) * a.ndim)
    whole = pl.BlockSpec((rows, width), lambda j, sc: (0, 0))
    return pl.pallas_call(
        functools.partial(middle_kernel, slots=slots),
        grid_spec=pltpu.PrefetchScalarGridSpec(
            num_scalar_prefetch=1,
            grid=(1,),
            in_specs=[full(a) for a in (tok, o, sm, cot, keep)] + [ANY] * 7,
            out_specs=[whole] * 3,
            scratch_shapes=[pltpu.VMEM((width, width), BF), pltpu.SemaphoreType.DMA((7,))],
        ),
        out_shape=[SD((rows, width), F32), SD((rows, width), BF), SD((rows, width), BF)],
        compiler_params=params(),
        cost_estimate=cost(4 * rows * width * width, 14 * MB),
        name="middle",
    )(sc, tok, o, sm, cot, keep, own, *pieces)


def store_halves(core, own_ref, send_ref, index, first, second):
    @pl.when(core == 0)
    def _():
        own_ref[index] = first
        send_ref[index] = second

    @pl.when(core != 0)
    def _():
        own_ref[index] = second
        send_ref[index] = first


def mlp_kernel(sc, h2, dm, sm, wup, wdown, *rest, k, last):
    pp, pq = rest[:6], rest[6:12]
    rest = rest[12:]
    if last:
        old_down, old_dh2 = rest[:2]
        rest = rest[2:]
    down, dh2, up_own, up_send, dn_own, dn_send, gub, ubuf, dbuf, sems = rest
    shard, core = sc[0], sc[1]
    step = pl.program_id(0)
    width = h2.shape[1]
    height = wup.shape[0]
    half, part = height // 2, wdown.shape[0] // 2
    pairs = []
    for r in range(4):
        at = pl.multiple_of(shard * height, 16)
        take = pl.multiple_of((shard ^ r) * width + k * part, 128)
        pairs.append(
            (wup.at[:, pl.ds(take, part)], ubuf.at[pl.ds(at, height), pl.ds(r * part, part)])
        )
    pairs.append((wdown.at[pl.ds(k * part, part), :], dbuf.at[pl.ds(0, part), :]))
    for side in range(2):
        which = core if side == 0 else 1 - core
        for m in range(1, 4):
            at = pl.multiple_of((shard ^ m) * height + which * half, 16)
            for r in range(4):
                pairs.append(
                    (
                        pp[side * 3 + m - 1].at[r ^ m],
                        ubuf.at[pl.ds(at, half), pl.ds(r * part, part)],
                    )
                )
            at = pl.multiple_of(m * part + which * (part // 2), 16)
            pairs.append((pq[side * 3 + m - 1], dbuf.at[pl.ds(at, part // 2), :]))
    copies = run_copies(pairs, sems)

    @pl.when(step == 0)
    def _():
        for c in copies:
            c.start()
        for c in copies:
            c.wait()

    cols = pl.ds(pl.multiple_of(step * width, 128), width)
    uw, dw = ubuf[:, cols], dbuf[cols, :]
    x, g = h2[...], dm[...]
    take = slice(k * part, (k + 1) * part)
    first = shard ^ (2 * step)
    bias = jnp.concatenate(
        [sm[pl.ds(UB + first, 1), take], sm[pl.ds(UB + (first ^ 1), 1), take]], axis=1
    )
    u = dot(x, uw, 1, 0) + bias
    dact = dot(g, dw, 1, 1)
    cdf = 0.5 * (1.0 + lax.erf(u * np.float32(np.sqrt(0.5))))
    act = (u * cdf).astype(BF)
    slope = cdf + u * (jnp.exp(-0.5 * u * u) * np.float32(1.0 / np.sqrt(2.0 * np.pi)))
    du = (dact * slope).astype(BF)
    bsum = jnp.sum(du.astype(F32), axis=0, keepdims=True)
    gd = dot(act, g, 0, 0).astype(BF)
    quarter = part // 4
    for r in range(2):
        gub[(shard & 1) ^ r] = bsum[:, r * part : (r + 1) * part]
        for i in range(2):
            for j in range(2):
                span = slice(j * part, (j + 1) * part)
                at = r * part + i * quarter
                store_halves(
                    core,
                    dn_own,
                    dn_send,
                    (r, 2 * i + j),
                    gd[at : at + quarter, span],
                    gd[at + part // 2 : at + part // 2 + quarter, span],
                )
    gu = dot(x, du, 0, 0).astype(BF)
    for m in range(4):
        at = m * height
        for r in range(2):
            span = slice(r * part, (r + 1) * part)
            store_halves(
                core,
                up_own,
                up_send,
                (shard ^ m, (shard & 1) ^ r),
                gu[at : at + half, span],
                gu[at + half : at + height, span],
            )
    new_down = dot(act, dw, 1, 0)
    new_dh2 = dot(du, uw, 1, 1)

    @pl.when(step == 0)
    def _():
        if last:
            down[...] = old_down[...] + new_down
            dh2[...] = old_dh2[...] + new_dh2
        else:
            down[...] = new_down
            dh2[...] = new_dh2

    @pl.when(step > 0)
    def _():
        down[...] += new_down
        dh2[...] += new_dh2


def mlp_part(sc, h2, dm, sm, wup, wdown, pieces, k, old):
    rows, width = h2.shape
    half, part = wup.shape[0] // 2, wdown.shape[0] // 2
    once = pl.Buffered(1)
    full = lambda a: pl.BlockSpec(a.shape, lambda j, sc: (0,) * a.ndim, pipeline_mode=once)
    whole = pl.BlockSpec((rows, width), lambda j, sc: (0, 0), pipeline_mode=once)
    by_up = pl.BlockSpec((4, 2, half, part), lambda j, sc: (0, (sc[0] >> 1) ^ j, 0, 0))
    by_down = pl.BlockSpec((2, 4, half, part), lambda j, sc: (j, 0, 0, 0))
    shares = SD((4, 4, half, part), BF)
    return pl.pallas_call(
        functools.partial(mlp_kernel, k=k, last=old is not None),
        grid_spec=pltpu.PrefetchScalarGridSpec(
            num_scalar_prefetch=1,
            grid=(2,),
            in_specs=[full(a) for a in (h2, dm, sm)]
            + [ANY] * 14
            + ([whole] * 2 if old is not None else []),
            out_specs=[whole] * 2
            + [by_up] * 2
            + [by_down] * 2
            + [pl.BlockSpec((2, 1, part), lambda j, sc: ((sc[0] >> 1) ^ j, 0, 0))],
            scratch_shapes=[
                pltpu.VMEM((width, 4 * part), BF),
                pltpu.VMEM((4 * part, width), BF),
                pltpu.SemaphoreType.DMA((35,)),
            ],
        ),
        out_shape=[SD((rows, width), F32)] * 2 + [shares] * 4 + [SD((4, 1, part), F32)],
        compiler_params=params(),
        cost_estimate=cost(6 * 2 * rows * width * 4 * part, 20 * MB),
        name="mlp%d" % k,
    )(sc, h2, dm, sm, wup, wdown, *pieces, *(old or ()))


def after_kernel(sc, down, dh2, mid, cot, keep, sm, o, dm, own, *rest, slots):
    pieces = rest[:6]
    out, dmid, do, q_own0, q_send0, q_own1, q_send1, gs, wbuf, sems = rest[6:]
    images, count, width = cot.shape
    every = pl.ds(0, width)
    height = own.shape[0]
    copies = run_copies(
        place_rows(wbuf, sc, (own, every), pieces, every, pl.ds(width, width), height), sems
    )
    for c in copies:
        c.start()
    e0 = dh2[...]
    xhat, rsq = normalized(mid[...])
    gs[...] = jnp.zeros_like(gs)
    gs[1:2, :] = jnp.sum(e0 * xhat, axis=0, keepdims=True)
    gs[2:3, :] = jnp.sum(e0, axis=0, keepdims=True)
    gs[3:4, :] = jnp.sum(dm[...].astype(F32), axis=0, keepdims=True)
    dmid[...] = norm_back(e0 * sm[G2 : G2 + 1, :], xhat, rsq)
    for i in range(images):
        sl = slice(i * slots, i * slots + count)
        dmid[sl, :] += cot[i].astype(F32) * keep[sl, :]
        out[i] = (keep[sl, :] * (mid[sl, :] + down[sl, :] + sm[DB : DB + 1, :])).astype(BF)
    low = dmid[...].astype(BF)
    gs[0:1, :] = jnp.sum(low.astype(F32), axis=0, keepdims=True)
    for c in copies:
        c.wait()
    do[...] = dot(low, wbuf[...], 1, 1).astype(BF)
    gw = dot(o[...], low, 0, 0).astype(BF)
    half, part = height // 2, width // 2
    for m in range(4):
        for j in range(2):
            cols = slice(j * part, (j + 1) * part)
            at = m * height
            store_halves(
                sc[1],
                (q_own0, q_own1)[j],
                (q_send0, q_send1)[j],
                (sc[0] ^ m, 0),
                gw[at : at + half, cols],
                gw[at + half : at + height, cols],
            )


def after_mlp(sc, down, dh2, mid, cot, keep, sm, o, dm, own, pieces, slots):
    rows, width = o.shape
    half, part = own.shape[0] // 2, width // 2
    full = lambda a: pl.BlockSpec(a.shape, lambda j, sc: (0,) * a.ndim)
    whole = pl.BlockSpec((rows, width), lambda j, sc: (0, 0))
    share = pl.BlockSpec((4, 1, half, part), lambda j, sc: (0, 1, 0, 0))
    return pl.pallas_call(
        functools.partial(after_kernel, slots=slots),
        grid_spec=pltpu.PrefetchScalarGridSpec(
            num_scalar_prefetch=1,
            grid=(1,),
            in_specs=[full(a) for a in (down, dh2, mid, cot, keep, sm, o, dm)] + [ANY] * 7,
            out_specs=[full(cot), whole, whole] + [share] * 4
            + [pl.BlockSpec((8, width), lambda j, sc: (0, 0))],
            scratch_shapes=[pltpu.VMEM((width, width), BF), pltpu.SemaphoreType.DMA((7,))],
        ),
        out_shape=[SD(cot.shape, BF), SD((rows, width), F32), SD((rows, width), BF)]
        + [SD((4, 2, half, part), BF)] * 4
        + [SD((8, width), F32)],
        compiler_params=params(),
        cost_estimate=cost(8 * rows * width * width, 18 * MB),
        name="after_mlp",
    )(sc, down, dh2, mid, cot, keep, sm, o, dm, own, *pieces)


def project_grad_kernel(sc, h1, dx, q0, q1, p_own, p_send, q_own, q_send, gs, *, height):
    half, part = height // 2, dx.shape[1] // 3
    low = dx[...]
    gs[...] = jnp.broadcast_to(jnp.sum(low.astype(F32), axis=0, keepdims=True), gs.shape)
    gw = dot(h1[...], low, 0, 0).astype(BF)
    for m in range(4):
        for j in range(3):
            cols = slice(j * part, (j + 1) * part)
            at = m * height
            own, send = (q_own, q_send) if j == 2 else (p_own, p_send)
            store_halves(
                sc[1],
                own,
                send,
                (sc[0] ^ m, j % 2),
                gw[at : at + half, cols],
                gw[at + half : at + height, cols],
            )


def project_grad(sc, h1, dx, q_own, q_send, height, group):
    rows, width = h1.shape
    half, part = height // 2, dx.shape[1] // 3
    full = lambda a: pl.BlockSpec(a.shape, lambda j, sc: (0,) * a.ndim)
    pshare = pl.BlockSpec((4, 2, half, part), lambda j, sc: (0, 0, 0, 0))
    qshare = pl.BlockSpec((4, 1, half, part), lambda j, sc: (0, 0, 0, 0))
    shares = SD((4, 2, half, part), BF)
    return pl.pallas_call(
        functools.partial(project_grad_kernel, height=height),
        grid_spec=pltpu.PrefetchScalarGridSpec(
            num_scalar_prefetch=1,
            grid=(1,),
            in_specs=[full(h1), full(dx)] + [ANY] * 2,
            out_specs=[pshare, pshare, qshare, qshare]
            + [pl.BlockSpec((8, 3 * part), lambda j, sc: (0, 0))],
        ),
        out_shape=[shares] * 4 + [SD((8, 3 * part), F32)],
        input_output_aliases={3: 2, 4: 3},
        compiler_params=params(),
        cost_estimate=cost(6 * rows * width * part, 7 * MB),
        name="project_grad%d" % group,
    )(sc, h1, dx, q_own, q_send)


def tokens_grad_kernel(sc, dx0, dx1, tok, sm, dmid, ga, gp0, gp1, gu0, gu1, own, *rest, slots):
    pp, pq = rest[:6], rest[6:12]
    out, gs, wbuf, acc, sems = rest[12:]
    images, count, width = tok.shape
    height, part = own.shape[0], width // 2
    pairs = []
    for n in range(2):
        for m in range(3):
            dst = pl.ds((3 * n + m) * part, part)
            src = pl.ds(m * width + n * part, part)
            sub = pl.ds(n * part, part) if m == 2 else src
            pairs += place_rows(wbuf, sc, (own, src), pq if m == 2 else pp, dst, sub, height)
    copies = run_copies(pairs, sems)
    for c in copies:
        c.start()
    gs[...] = jnp.zeros_like(gs)
    gs[OB : OB + 4, :] = ga[0:4, :]
    for n, gp in enumerate((gp0, gp1)):
        cols = slice(n * part, (n + 1) * part)
        gs[QB : QB + 1, cols] = gp[0:1, :part]
        gs[VB : VB + 1, cols] = gp[0:1, 2 * part :]
    for b in range(4):
        gs[UB + b : UB + b + 1, :part] = gu0[b]
        gs[UB + b : UB + b + 1, part:] = gu1[b]
    for c in copies:
        c.wait()
    acc[...] = dot(dx0[...], wbuf[:, : 3 * part], 1, 1) + dot(dx1[...], wbuf[:, 3 * part :], 1, 1)
    gain = jnp.zeros((1, width), F32)
    shift = jnp.zeros((1, width), F32)
    for i in range(images):
        sl = slice(i * slots, i * slots + count)
        e0 = acc[sl, :]
        xhat, rsq = normalized(tok[i].astype(F32))
        gain += jnp.sum(e0 * xhat, axis=0, keepdims=True)
        shift += jnp.sum(e0, axis=0, keepdims=True)
        out[i] = (dmid[sl, :] + norm_back(e0 * sm[G1 : G1 + 1, :], xhat, rsq)).astype(BF)
    gs[G1 : G1 + 1, :] = gain
    gs[B1 : B1 + 1, :] = shift


def tokens_grad(sc, dx0, dx1, tok, sm, dmid, ga, gp0, gp1, gu0, gu1, own, pieces, slots):
    rows, width = dmid.shape
    full = lambda a: pl.BlockSpec(a.shape, lambda j, sc: (0,) * a.ndim)
    operands = (dx0, dx1, tok, sm, dmid, ga, gp0, gp1, gu0, gu1)
    return pl.pallas_call(
        functools.partial(tokens_grad_kernel, slots=slots),
        grid_spec=pltpu.PrefetchScalarGridSpec(
            num_scalar_prefetch=1,
            grid=(1,),
            in_specs=[full(a) for a in operands] + [ANY] * 13,
            out_specs=[full(tok), pl.BlockSpec((16, width), lambda j, sc: (0, 0))],
            scratch_shapes=[
                pltpu.VMEM((width, 3 * width), BF),
                pltpu.VMEM((rows, width), F32),
                pltpu.SemaphoreType.DMA((42,)),
            ],
        ),
        out_shape=[SD(tok.shape, BF), SD((16, width), F32)],
        compiler_params=params(),
        cost_estimate=cost(6 * rows * width * width, 16 * MB),
        name="tokens_grad",
    )(sc, *operands, own, *pieces)


def lay_kernel(sc, *refs, kind, part):
    core, odd = sc[1], sc[2] % 2
    ins, (wide, tall) = refs[:8], refs[8:]
    half = ins[0].shape[1]

    def put(k, side, first, second):
        which = core if side == 0 else 1 - core
        rows = pl.ds(pl.multiple_of(which * half, 8), half)
        if kind == "mlp":
            for b in range(4):
                wide[rows, pl.ds((2 * b + k) * part, part)] = first[b].astype(F32)
            for i in range(2):
                at = pl.multiple_of(which * 2 * half + (k * 4 + i) * half, 8)
                for j in range(2):
                    tall[pl.ds(at, half), pl.ds(j * part, part)] = second[2 * i + j].astype(F32)
        else:
            for n, block in enumerate((first[0], first[1], second[0])):
                wide[rows, pl.ds((2 * n + k) * part, part)] = block.astype(F32)
            tall[rows, pl.ds(k * part, part)] = second[1].astype(F32)

    for k in range(2):
        kept, other, skept, sother = ins[4 * k : 4 * k + 4]

        @pl.when(odd == 0)
        def _(k=k, kept=kept, other=other, skept=skept, sother=sother):
            put(k, 0, kept, other)
            put(k, 1, skept, sother)

        @pl.when(odd != 0)
        def _(k=k, kept=kept, other=other, skept=skept, sother=sother):
            put(k, 0, other, kept)
            put(k, 1, sother, skept)


def lay_out(sc, finals, kind, shapes, part):
    full = lambda s: pl.BlockSpec(s, lambda j, sc: (0,) * len(s))
    flat = [a for group in finals for a in group]
    return pl.pallas_call(
        functools.partial(lay_kernel, kind=kind, part=part),
        grid_spec=pltpu.PrefetchScalarGridSpec(
            num_scalar_prefetch=1,
            grid=(1,),
            in_specs=[full(a.shape) for a in flat],
            out_specs=[full(s) for s in shapes],
        ),
        out_shape=[SD(s, F32) for s in shapes],
        compiler_params=params(),
        cost_estimate=cost(0, 8 * MB),
        name="lay_" + kind,
    )(sc, *flat)


def hops():
    def table(move):
        pairs = []
        for dp in range(8):
            for fs in range(4):
                z, core, shard = move(dp // 2, dp % 2, fs)
                pairs.append((dp * 4 + fs, (z * 2 + core) * 4 + shard))
        return pairs

    moves = {
        "sib": lambda z, c, f: (z, 1 - c, f),
        "x": lambda z, c, f: (z, c, f ^ 1),
        "y": lambda z, c, f: (z, c, f ^ 2),
        "z1": lambda z, c, f: (z ^ 1, c, f),
        "z2": lambda z, c, f: (z ^ 2, c, f),
    }
    tables = {name: table(move) for name, move in moves.items()}
    return lambda value, name: lax.ppermute(value, ("dp", "fsdp"), tables[name])


class Transfer:
    def __init__(self, stages):
        self.stages = stages
        self.flying = next(stages)
        self.result = None

    def step(self, landed):
        try:
            self.flying = self.stages.send(landed)
        except StopIteration as end:
            self.flying, self.result = (), end.value


def advance(held, *transfers):
    values = lax.optimization_barrier((held, tuple(t.flying for t in transfers)))
    for t, landed in zip(transfers, values[1]):
        t.step(landed)
    return values[0]


def gather_stages(hop, sp, sq):
    xp, yp, xq, yq = yield (hop(sp, "x"), hop(sp, "y"), hop(sq, "x"), hop(sq, "y"))
    first = (xp, yp, xq, yq)
    zp, zq, *near = yield (hop(xp, "y"), hop(yq, "x")) + tuple(hop(a, "sib") for a in first)
    szp, szq = yield (hop(zp, "sib"), hop(zq, "sib"))
    sxp, syp, sxq, syq = near
    return (xp, yp, zp, sxp, syp, szp), (xq, yq, zq, sxq, syq, szq)


def add(a, b):
    return (a.astype(F32) + b.astype(F32)).astype(BF)


def reduce_stages(hop, even, p_own, p_send, q_own, q_send):
    p_got, q_got = yield (hop(p_send, "sib"), hop(q_send, "sib"))

    def pick(own, got, first, second):
        return jnp.stack([add(own[first], got[first]), add(own[second], got[second])])

    p_out = pick(p_own, p_got, 1, 3)
    q_out = pick(q_own, q_got, 2, 3)
    p_in, q_in = yield (hop(p_out, "x"), hop(q_out, "y"))
    p_next = add(add(p_own[2], p_got[2]), p_in[1])
    q_next = add(add(q_own[1], q_got[1]), q_in[1])
    p_in2, q_in2 = yield (hop(p_next, "y"), hop(q_next, "x"))
    p_all = add(add(add(p_own[0], p_got[0]), p_in[0]), p_in2)
    q_all = add(add(add(q_own[0], q_got[0]), q_in[0]), q_in2)
    keep = jnp.where(even, p_all, q_all)
    give = jnp.where(even, q_all, p_all)
    (got,) = yield (hop(give, "z1"),)
    half = lax.optimization_barrier(add(keep, got))
    (got,) = yield (hop(half, "z2"),)
    kept = add(half, got)
    other, skept = yield (hop(kept, "z1"), hop(kept, "sib"))
    (sother,) = yield (hop(other, "sib"),)
    return kept, other, skept, sother


def sum_stages(hop, value):
    for name in ("sib", "x", "y", "z1", "z2"):
        (got,) = yield (hop(value, name),)
        value = value + got
    return value


def on_device_fast(
    tokens,
    mask,
    cotangent,
    ln1_gain,
    ln1_bias,
    w_qkv,
    qv_bias,
    w_out,
    out_bias,
    ln2_gain,
    ln2_bias,
    w_up,
    up_bias,
    w_down,
    down_bias,
):
    images, count, width = tokens.shape
    slots = -(-count // 8) * 8
    height = w_out.shape[0]
    half, part = height // 2, width // 2
    hop = hops()
    shard = lax.axis_index("fsdp")
    dp = lax.axis_index("dp")
    sc = jnp.stack([shard, dp % 2, dp // 2]).astype(jnp.int32)
    even = (dp // 2) % 2 == 0

    small = (ln1_gain, ln1_bias, qv_bias, out_bias, ln2_gain, ln2_bias, down_bias, up_bias)
    own_small = jnp.concatenate([a.reshape(-1, height) for a in small])
    own_small = jnp.pad(own_small, ((0, 4), (0, -height % 128)))
    sp, sq = pack_first(sc, w_qkv, w_out, own_small)
    first = Transfer(gather_stages(hop, sp, sq))
    sp0, sq0, sp1, sq1 = pack_mlp(sc, w_up, w_down)
    sp0, sq0, sp1, sq1 = advance((sp0, sq0, sp1, sq1), first)
    ffn0 = Transfer(gather_stages(hop, sp0, sq0))
    sc = advance(sc, first)
    sc = advance(sc, first)
    first_p, first_q = first.result

    keep = jnp.pad(mask.astype(F32), ((0, 0), (0, slots - count)))
    mask_row = keep.reshape(images, 1, slots)
    keep_col = keep.reshape(images * slots, 1)

    h1, qkv, sm = project(sc, tokens, own_small, w_qkv, first_p + first_q, slots)
    qkv, sp1, sq1 = advance((qkv, sp1, sq1), ffn0)
    ffn1 = Transfer(gather_stages(hop, sp1, sq1))
    o = attend(qkv, mask_row, slots)
    o = advance(o, ffn0)
    mid, h2, dm = middle_part(sc, tokens, o, sm, cotangent, keep_col, w_out, first_q, slots)
    h2 = advance(h2, ffn0, ffn1)
    up0, down0 = ffn0.result
    got0 = mlp_part(sc, h2, dm, sm, w_up, w_down, up0 + down0, 0, None)
    got0 = advance(tuple(got0), ffn1)
    m0 = Transfer(reduce_stages(hop, even, *got0[2:6]))
    sc = advance(sc, ffn1, m0)
    up1, down1 = ffn1.result
    got1 = mlp_part(sc, h2, dm, sm, w_up, w_down, up1 + down1, 1, (got0[0], got0[1]))
    got1 = advance(tuple(got1), m0)
    m1 = Transfer(reduce_stages(hop, even, *got1[2:6]))
    layer_out, dmid, do, qo0, qs0, qo1, qs1, ga = after_mlp(
        sc, got1[0], got1[1], mid, cotangent, keep_col, sm, o, dm, w_out, first_q, slots
    )
    do = advance(do, m0, m1)
    dx0 = attend_back(qkv, do, keep_col, slots, 0)
    dx0 = advance(dx0, m0, m1)
    *part0, gp0 = project_grad(sc, h1, dx0, qo0, qs0, height, 0)
    do, *part0 = advance((do, *part0), m0, m1)
    m2 = Transfer(reduce_stages(hop, even, *part0))
    dx1 = attend_back(qkv, do, keep_col, slots, 1)
    dx1 = advance(dx1, m0, m1, m2)
    *part1, gp1 = project_grad(sc, h1, dx1, qo1, qs1, height, 1)
    dx0, *part1 = advance((dx0, *part1), m0, m1, m2)
    m3 = Transfer(reduce_stages(hop, even, *part1))
    sc = advance(sc, m3)
    grad_tokens, gs = tokens_grad(
        sc,
        dx0,
        dx1,
        tokens,
        sm,
        dmid,
        ga,
        gp0,
        gp1,
        got0[6],
        got1[6],
        w_qkv,
        first_p + first_q,
        slots,
    )
    gs = advance(gs, m1, m2, m3)
    total = Transfer(sum_stages(hop, gs))
    ffn = None
    chains = (m0, m1, m2, m3, total)
    while any(t.flying for t in chains):
        ffn = advance(ffn, *[t for t in chains if t.flying])
        if ffn is None and m1.result is not None:
            ffn = lay_out(
                sc, (m0.result, m1.result), "mlp", ((height, 4 * width), (4 * height, width)), part
            )
    gs = total.result
    grad_w_up, grad_w_down = ffn
    grad_w_qkv, grad_w_out = lay_out(
        sc, (m2.result, m3.result), "attn", ((height, 3 * width), (height, width)), part
    )

    def mine(r, n=1):
        return lax.dynamic_slice(gs[r : r + n].reshape(-1), (shard * (n * height),), (n * height,))

    return (
        layer_out,
        grad_tokens,
        mine(G1),
        mine(B1),
        grad_w_qkv,
        mine(QB, 2),
        grad_w_out,
        mine(OB),
        mine(G2),
        mine(B2),
        grad_w_up,
        mine(UB, 4),
        grad_w_down,
        mine(DB),
    )


def norm(values, gain, shift):
    mean_value = jnp.mean(values, axis=-1, keepdims=True)
    centred = values - mean_value
    variance = jnp.mean(centred * centred, axis=-1, keepdims=True)
    return centred * lax.rsqrt(variance + EPS) * gain + shift


def gelu_exact(values):
    return jax.nn.gelu(values, approximate=False)


def score_block(query, key_part, valid):
    scores = jnp.einsum(
        "iqhe,ikhe->ihqk", query, key_part, preferred_element_type=jnp.float32
    ) * HD ** (-0.5)
    return jnp.where(valid, scores, -1e30)


def arrange(grad, groups, copies):
    shaped = grad.reshape((groups, copies, grad.shape[0] // (groups * copies)) + grad.shape[1:])
    return jnp.swapaxes(shaped, 0, 1).reshape(grad.shape)


def reduce_six(grad_one, grad_two, grad_three, grad_four, grad_five, grad_six):
    groups = lax.axis_size("fsdp")
    copies = lax.axis_size("dp")
    pieces = (
        lax.psum_scatter(
            arrange(grad_one, groups, copies), ("dp", "fsdp"), scatter_dimension=0, tiled=True
        ),
        lax.psum_scatter(
            arrange(grad_two, groups, copies), ("dp", "fsdp"), scatter_dimension=0, tiled=True
        ),
        lax.psum_scatter(
            arrange(grad_three, groups, copies), ("dp", "fsdp"), scatter_dimension=0, tiled=True
        ),
        lax.psum_scatter(
            arrange(grad_four, groups, copies), ("dp", "fsdp"), scatter_dimension=0, tiled=True
        ),
        lax.psum_scatter(
            arrange(grad_five, groups, copies), ("dp", "fsdp"), scatter_dimension=0, tiled=True
        ),
        lax.psum_scatter(
            arrange(grad_six, groups, copies), ("dp", "fsdp"), scatter_dimension=0, tiled=True
        ),
    )
    return (
        lax.all_gather(pieces[0].astype(jnp.bfloat16), "dp", axis=0, tiled=True).astype(
            jnp.float32
        ),
        lax.all_gather(pieces[1].astype(jnp.bfloat16), "dp", axis=0, tiled=True).astype(
            jnp.float32
        ),
        lax.all_gather(pieces[2].astype(jnp.bfloat16), "dp", axis=0, tiled=True).astype(
            jnp.float32
        ),
        lax.all_gather(pieces[3].astype(jnp.bfloat16), "dp", axis=0, tiled=True).astype(
            jnp.float32
        ),
        lax.all_gather(pieces[4].astype(jnp.bfloat16), "dp", axis=0, tiled=True).astype(
            jnp.float32
        ),
        lax.all_gather(pieces[5].astype(jnp.bfloat16), "dp", axis=0, tiled=True).astype(
            jnp.float32
        ),
    )


def on_device(
    tokens,
    mask,
    cotangent,
    ln1_gain,
    ln1_bias,
    w_qkv,
    qv_bias,
    w_out,
    out_bias,
    ln2_gain,
    ln2_bias,
    w_up,
    up_bias,
    w_down,
    down_bias,
):
    image_count, slot_count, width = tokens.shape
    row_count = image_count * slot_count
    heads = width // HD
    scale = HD ** (-0.5)
    attn_full = (
        lax.all_gather(ln1_gain, "fsdp", axis=0, tiled=True),
        lax.all_gather(ln1_bias, "fsdp", axis=0, tiled=True),
        lax.all_gather(w_qkv, "fsdp", axis=0, tiled=True),
        lax.all_gather(qv_bias, "fsdp", axis=0, tiled=True),
        lax.all_gather(w_out, "fsdp", axis=0, tiled=True),
        lax.all_gather(out_bias, "fsdp", axis=0, tiled=True),
    )
    mlp_full = (
        lax.all_gather(ln2_gain, "fsdp", axis=0, tiled=True),
        lax.all_gather(ln2_bias, "fsdp", axis=0, tiled=True),
        lax.all_gather(w_up, "fsdp", axis=0, tiled=True),
        lax.all_gather(up_bias, "fsdp", axis=0, tiled=True),
        lax.all_gather(w_down, "fsdp", axis=0, tiled=True),
        lax.all_gather(down_bias, "fsdp", axis=0, tiled=True),
    )
    gain_one, shift_one, qkv_weight, qkv_shift, out_weight, out_shift = attn_full
    gain_two, shift_two, up_weight, up_shift, down_weight, down_shift = mlp_full
    keep = mask.astype(jnp.float32)
    valid = (keep > 0.5)[:, None, None, :]
    keep_rows = keep.reshape(row_count, 1)
    inputs = tokens.astype(jnp.float32).reshape(row_count, width)
    normed_one, norm_one_back = jax.vjp(
        norm, inputs, gain_one.astype(jnp.float32), shift_one.astype(jnp.float32)
    )
    normed_low = normed_one.astype(jnp.bfloat16)
    qv_float = qkv_shift.astype(jnp.float32)
    full_bias = jnp.concatenate(
        [qv_float[:width], jnp.zeros((width,), jnp.float32), qv_float[width:]]
    )
    projected = (
        jnp.dot(normed_low, qkv_weight, preferred_element_type=jnp.float32) + full_bias
    ).astype(jnp.bfloat16)
    query = projected[:, :width].reshape(image_count, slot_count, heads, HD)
    key_part = projected[:, width : 2 * width].reshape(image_count, slot_count, heads, HD)
    value = projected[:, 2 * width :].reshape(image_count, slot_count, heads, HD)
    scores = score_block(query, key_part, valid)
    top = jnp.max(scores, axis=-1, keepdims=True)
    lse = top + jnp.log(jnp.sum(jnp.exp(scores - top), axis=-1, keepdims=True))
    probs_low = jnp.exp(scores - lse).astype(jnp.bfloat16)
    mixed = jnp.einsum("ihqk,ikhe->iqhe", probs_low, value, preferred_element_type=jnp.float32)
    mixed = mixed.reshape(row_count, width).astype(jnp.bfloat16)
    middle = (
        inputs
        + jnp.dot(mixed, out_weight, preferred_element_type=jnp.float32)
        + out_shift.astype(jnp.float32)
    )
    normed_two, norm_two_back = jax.vjp(
        norm, middle, gain_two.astype(jnp.float32), shift_two.astype(jnp.float32)
    )
    normed_two_low = normed_two.astype(jnp.bfloat16)
    upward = jnp.dot(
        normed_two_low, up_weight, preferred_element_type=jnp.float32
    ) + up_shift.astype(jnp.float32)
    active, gelu_back = jax.vjp(gelu_exact, upward)
    active_low = active.astype(jnp.bfloat16)
    downward = jnp.dot(
        active_low, down_weight, preferred_element_type=jnp.float32
    ) + down_shift.astype(jnp.float32)
    layer_out = (
        (keep_rows * (middle + downward))
        .astype(jnp.bfloat16)
        .reshape(image_count, slot_count, width)
    )
    mlp_back = (
        lax.all_gather(ln2_gain, "fsdp", axis=0, tiled=True),
        lax.all_gather(ln2_bias, "fsdp", axis=0, tiled=True),
        lax.all_gather(w_up, "fsdp", axis=0, tiled=True),
        lax.all_gather(up_bias, "fsdp", axis=0, tiled=True),
        lax.all_gather(w_down, "fsdp", axis=0, tiled=True),
        lax.all_gather(down_bias, "fsdp", axis=0, tiled=True),
    )
    up_back = mlp_back[2]
    down_back = mlp_back[4]
    grad_rows = cotangent.astype(jnp.float32).reshape(row_count, width) * keep_rows
    grad_down_low = grad_rows.astype(jnp.bfloat16)
    grad_w_down = jnp.einsum(
        "rf,rd->fd", active_low, grad_down_low, preferred_element_type=jnp.float32
    )
    grad_down_bias = jnp.sum(grad_down_low, axis=0, dtype=jnp.float32)
    grad_active = jnp.einsum(
        "rd,fd->rf", grad_down_low, down_back, preferred_element_type=jnp.float32
    )
    grad_up_low = gelu_back(grad_active)[0].astype(jnp.bfloat16)
    grad_w_up = jnp.einsum(
        "rd,rf->df", normed_two_low, grad_up_low, preferred_element_type=jnp.float32
    )
    grad_up_bias = jnp.sum(grad_up_low, axis=0, dtype=jnp.float32)
    grad_normed_two = jnp.einsum(
        "rf,df->rd", grad_up_low, up_back, preferred_element_type=jnp.float32
    )
    grad_mid_norm, grad_ln2_gain, grad_ln2_bias = norm_two_back(grad_normed_two)
    grad_middle = grad_rows + grad_mid_norm
    mlp_grads = reduce_six(
        grad_ln2_gain, grad_ln2_bias, grad_w_up, grad_up_bias, grad_w_down, grad_down_bias
    )
    attn_back = (
        lax.all_gather(ln1_gain, "fsdp", axis=0, tiled=True),
        lax.all_gather(ln1_bias, "fsdp", axis=0, tiled=True),
        lax.all_gather(w_qkv, "fsdp", axis=0, tiled=True),
        lax.all_gather(qv_bias, "fsdp", axis=0, tiled=True),
        lax.all_gather(w_out, "fsdp", axis=0, tiled=True),
        lax.all_gather(out_bias, "fsdp", axis=0, tiled=True),
    )
    qkv_back = attn_back[2]
    out_back = attn_back[4]
    grad_attn_low = grad_middle.astype(jnp.bfloat16)
    grad_w_out = jnp.einsum("rd,re->de", mixed, grad_attn_low, preferred_element_type=jnp.float32)
    grad_out_bias = jnp.sum(grad_attn_low, axis=0, dtype=jnp.float32)
    grad_mixed = jnp.einsum(
        "re,de->rd", grad_attn_low, out_back, preferred_element_type=jnp.float32
    )
    grad_mixed = grad_mixed.astype(jnp.bfloat16).reshape(image_count, slot_count, heads, HD)
    probs = jnp.exp(score_block(query, key_part, valid) - lse)
    probs_again = probs.astype(jnp.bfloat16)
    grad_value = jnp.einsum(
        "ihqk,iqhe->ikhe", probs_again, grad_mixed, preferred_element_type=jnp.float32
    )
    grad_probs = jnp.einsum(
        "iqhe,ikhe->ihqk", grad_mixed, value, preferred_element_type=jnp.float32
    )
    inner = jnp.sum(grad_probs * probs, axis=-1, keepdims=True)
    grad_scores = (probs * (grad_probs - inner)).astype(jnp.bfloat16)
    grad_query = (
        jnp.einsum("ihqk,ikhe->iqhe", grad_scores, key_part, preferred_element_type=jnp.float32)
        * scale
    )
    grad_key = (
        jnp.einsum("ihqk,iqhe->ikhe", grad_scores, query, preferred_element_type=jnp.float32)
        * scale
    )
    grad_projected = jnp.concatenate(
        [
            grad_query.reshape(row_count, width),
            grad_key.reshape(row_count, width),
            grad_value.reshape(row_count, width),
        ],
        axis=1,
    ).astype(jnp.bfloat16)
    grad_w_qkv = jnp.einsum(
        "rd,re->de", normed_low, grad_projected, preferred_element_type=jnp.float32
    )
    grad_qv_bias = jnp.concatenate(
        [
            jnp.sum(grad_projected[:, :width], axis=0, dtype=jnp.float32),
            jnp.sum(grad_projected[:, 2 * width :], axis=0, dtype=jnp.float32),
        ]
    )
    grad_normed_one = jnp.einsum(
        "re,de->rd", grad_projected, qkv_back, preferred_element_type=jnp.float32
    )
    grad_in_norm, grad_ln1_gain, grad_ln1_bias = norm_one_back(grad_normed_one)
    grad_tokens = (
        (grad_middle + grad_in_norm).astype(jnp.bfloat16).reshape(image_count, slot_count, width)
    )
    attn_grads = reduce_six(
        grad_ln1_gain, grad_ln1_bias, grad_w_qkv, grad_qv_bias, grad_w_out, grad_out_bias
    )
    return (
        layer_out,
        grad_tokens,
        attn_grads[0],
        attn_grads[1],
        attn_grads[2],
        attn_grads[3],
        attn_grads[4],
        attn_grads[5],
        mlp_grads[0],
        mlp_grads[1],
        mlp_grads[2],
        mlp_grads[3],
        mlp_grads[4],
        mlp_grads[5],
    )


def solution(mesh):
    in_specs = (
        P(("dp", "fsdp"), None, None),
        P(("dp", "fsdp"), None),
        P(("dp", "fsdp"), None, None),
        P("fsdp"),
        P("fsdp"),
        P("fsdp", None),
        P("fsdp"),
        P("fsdp", None),
        P("fsdp"),
        P("fsdp"),
        P("fsdp"),
        P("fsdp", None),
        P("fsdp"),
        P("fsdp", None),
        P("fsdp"),
    )
    out_specs = (
        P(("dp", "fsdp"), None, None),
        P(("dp", "fsdp"), None, None),
        P("fsdp"),
        P("fsdp"),
        P("fsdp", None),
        P("fsdp"),
        P("fsdp", None),
        P("fsdp"),
        P("fsdp"),
        P("fsdp"),
        P("fsdp", None),
        P("fsdp"),
        P("fsdp", None),
        P("fsdp"),
    )
    fast = dict(mesh.shape) == {"dp": 8, "fsdp": 4}
    return jax.shard_map(
        on_device_fast if fast else on_device, mesh=mesh, in_specs=in_specs, out_specs=out_specs, check_vma=False
    )
```

```python
import functools

import jax
import jax.numpy as jnp
import numpy as np
from jax import lax
from jax.experimental import pallas as pl
from jax.experimental.pallas import tpu as pltpu
from jax.sharding import PartitionSpec as P

HD = 64
EPS = 1e-06
F32 = jnp.float32
BF = jnp.bfloat16
MB = 2**20
SCORE_SCALE = np.float32(np.log2(np.e) * HD ** (-0.5))
MASKED = np.float32(-1e30)
SD = jax.ShapeDtypeStruct
ANY = pl.BlockSpec(memory_space=pl.ANY)
VM = pl.BlockSpec(memory_space=pltpu.VMEM)


def dot(a, b, ca, cb):
    return lax.dot_general(a, b, (((ca,), (cb,)), ((), ())), preferred_element_type=F32)


def params(mb=58):
    return pltpu.CompilerParams(vmem_limit_bytes=mb * MB)


def cost(micros):
    return pl.CostEstimate(flops=int(micros * 1.15e9), bytes_accessed=0, transcendentals=0)


def normalized(values):
    mean = jnp.mean(values, axis=-1, keepdims=True)
    centred = values - mean
    rsq = lax.rsqrt(jnp.mean(centred * centred, axis=-1, keepdims=True) + EPS)
    return centred * rsq, rsq


def norm_back(e, xhat, rsq):
    return rsq * (
        e
        - jnp.mean(e, axis=-1, keepdims=True)
        - xhat * jnp.mean(e * xhat, axis=-1, keepdims=True)
    )


def run_copies(pairs, sems, base=0):
    copies = [
        pltpu.make_async_copy(src, dst, sems.at[base + n]) for n, (src, dst) in enumerate(pairs)
    ]
    return copies


G1, B1, QB, VB, OB, G2, B2, DB, UB = range(9)


def all_copies(pairs, sems):
    copies = run_copies(pairs, sems)
    for c in copies:
        c.start()
    for c in copies:
        c.wait()


def pack_attn_kernel(sc, wqkv, wout, packed, sems):
    width = wout.shape[1]
    half = wout.shape[0] // 2
    rows = pl.ds(pl.multiple_of(sc[1] * half, 16), half)
    top, bottom = pl.ds(0, half), pl.ds(half, half)
    all_copies(
        [
            (wqkv.at[rows, pl.ds(0, 2 * width)], packed.at[top, :]),
            (wqkv.at[rows, pl.ds(2 * width, width)], packed.at[bottom, pl.ds(0, width)]),
            (wout.at[rows, :], packed.at[bottom, pl.ds(width, width)]),
        ],
        sems,
    )


def pack_ffn_kernel(sc, wup, wdown, ffn0, ffn1, sems):
    width = wdown.shape[1]
    half, part = wup.shape[0] // 2, wdown.shape[0] // 2
    rows = pl.ds(pl.multiple_of(sc[1] * half, 16), half)
    pairs = []
    for k, ffn in enumerate((ffn0, ffn1)):
        for g in range(2):
            for h in range(2):
                block = 2 * ((sc[0] >> 1) ^ g) + h
                at = pl.multiple_of(block * width + k * part, 128)
                pairs.append(
                    (
                        wup.at[rows, pl.ds(at, part)],
                        ffn.at[pl.ds(g * half, half), pl.ds(h * part, part)],
                    )
                )
        at = pl.multiple_of(k * part + sc[1] * (part // 2), 16)
        pairs.append((wdown.at[pl.ds(at, part // 2), :], ffn.at[pl.ds(2 * half, part // 2), :]))
    all_copies(pairs, sems)


def pack(sc, kernel, copies, shapes, *weights):
    return pl.pallas_call(
        kernel,
        grid_spec=pltpu.PrefetchScalarGridSpec(
            num_scalar_prefetch=1,
            in_specs=[ANY] * len(weights),
            out_specs=[ANY] * len(shapes),
            scratch_shapes=[pltpu.SemaphoreType.DMA((copies,))],
        ),
        out_shape=[SD(shape, BF) for shape in shapes],
        compiler_params=params(2),
        name="pack",
    )(sc, *weights)


def place_rows(dst, sc, own, pieces, cols, src_cols, height, base=0):
    half = height // 2
    shard, core = sc[0], sc[1]
    pairs = []
    if own is not None:
        src, take = own
        pairs.append((src.at[:, take], dst.at[pl.ds(pl.multiple_of(shard * height, 16), height), cols]))
    for side in range(2):
        which = core if side == 0 else 1 - core
        for r in range(1, 4):
            at = pl.multiple_of((shard ^ r) * height + which * half, 16)
            pairs.append(
                (
                    pieces[side * 3 + r - 1].at[pl.ds(base * half, half), src_cols],
                    dst.at[pl.ds(at, half), cols],
                )
            )
    return pairs


def fill_small(sc, pieces, sm, height):
    shard = sc[0]
    vals = [pieces[r][...].astype(F32) for r in range(4)]

    def of(j):
        got = vals[3]
        for r in range(3):
            got = jnp.where(shard == (j ^ r), vals[r], got)
        return got[:, :height]

    by = [of(j) for j in range(4)]
    sm[...] = jnp.zeros_like(sm)
    for j in range(4):
        cols = slice(j * height, (j + 1) * height)
        sm[G1 : B1 + 1, cols] = by[j][0:2]
        sm[OB : DB + 1, cols] = by[j][4:8]
        for n in range(2):
            at = (2 * j + n) % 4 * height
            row = QB if j < 2 else VB
            sm[row : row + 1, at : at + height] = by[j][2 + n : 3 + n]
        for n in range(4):
            sm[UB + j : UB + j + 1, n * height : (n + 1) * height] = by[j][8 + n : 9 + n]


def project_kernel(sc, tok, own, *rest, slots):
    pieces, small = rest[:6], rest[6:10]
    h1, qkv, sm, wbuf, sems = rest[10:]
    images, count, width = tok.shape
    height = own.shape[0]
    step = pl.program_id(0)
    two = pl.ds(0, 2 * width)
    third = pl.ds(2 * width, width)
    first = run_copies(place_rows(wbuf, sc, (own, two), pieces, two, two, height), sems)
    last = run_copies(
        place_rows(wbuf, sc, (own, third), pieces, third, pl.ds(0, width), height, 1),
        sems,
        len(first),
    )

    @pl.when(step == 0)
    def _():
        for c in first + last:
            c.start()
        fill_small(sc, small, sm, height)
        for i in range(images):
            xhat, _ = normalized(tok[i].astype(F32))
            low = (xhat * sm[G1 : G1 + 1, :] + sm[B1 : B1 + 1, :]).astype(BF)
            tail = count // 8 * 8
            h1[i * slots + tail : (i + 1) * slots, :] = jnp.zeros((slots - tail, width), BF)
            h1[i * slots : i * slots + count, :] = low
        for c in first:
            c.wait()

    @pl.when(step == 2)
    def _():
        for c in last:
            c.wait()

    row = jnp.where(step == 0, sm[QB : QB + 1, :], sm[VB : VB + 1, :])
    row = jnp.where(step == 1, jnp.zeros_like(row), row)
    weight = wbuf[:, pl.ds(pl.multiple_of(step * width, 128), width)]
    qkv[...] = (dot(h1[...], weight, 1, 0) + row).astype(BF)


def project(sc, tok, own, pieces, small, slots):
    images, _, width = tok.shape
    rows = images * slots
    full = lambda *s: pl.BlockSpec(s, lambda j, sc: (0,) * len(s))
    return pl.pallas_call(
        functools.partial(project_kernel, slots=slots),
        grid_spec=pltpu.PrefetchScalarGridSpec(
            num_scalar_prefetch=1,
            grid=(3,),
            in_specs=[VM] + [ANY] * 7 + [VM] * 4,
            out_specs=[
                VM,
                pl.BlockSpec((rows, width), lambda j, sc: (0, j)),
                VM,
            ],
            scratch_shapes=[
                pltpu.VMEM((width, 3 * width), BF),
                pltpu.SemaphoreType.DMA((14,)),
            ],
        ),
        out_shape=[SD((rows, width), BF), SD((rows, 3 * width), BF), SD((16, width), F32)],
        compiler_params=params(54),
        cost_estimate=cost(10),
        name="project",
    )(sc, tok, own, *pieces, *small)


def head_lanes():
    return lax.broadcasted_iota(jnp.int32, (1, 2 * HD), 1) < HD


def attend_kernel(q, k, v, mask, o, *, pairs):
    low_half = head_lanes()
    keep = mask[0] > 0
    zero = jnp.zeros((), BF)
    for p in range(pairs):
        sl = slice(p * 2 * HD, (p + 1) * 2 * HD)
        qp, kp, vp = q[:, sl], k[:, sl], v[:, sl]
        outs = []
        for a in range(2):
            mine = low_half if a == 0 else jnp.logical_not(low_half)
            s = dot(jnp.where(mine, qp, zero), kp, 1, 1)
            s = jnp.where(keep, s * SCORE_SCALE, MASKED)
            e = jnp.exp2(s - jnp.max(s, axis=-1, keepdims=True))
            prob = (e * (1.0 / jnp.sum(e, axis=-1, keepdims=True))).astype(BF)
            outs.append(dot(prob, jnp.where(mine, vp, zero), 1, 0))
        o[:, sl] = (outs[0] + outs[1]).astype(BF)


def attend(qkv, mask_row, slots):
    rows, three = qkv.shape
    width, images = three // 3, rows // slots
    block = lambda n: pl.BlockSpec((slots, width), lambda i: (i, n))
    return pl.pallas_call(
        functools.partial(attend_kernel, pairs=width // (2 * HD)),
        grid=(images,),
        in_specs=[block(0), block(1), block(2), pl.BlockSpec((1, 1, slots), lambda i: (i, 0, 0))],
        out_specs=block(0),
        out_shape=SD((rows, width), BF),
        compiler_params=params(12),
        cost_estimate=cost(11),
        name="attend",
    )(qkv, qkv, qkv, mask_row)


def attend_back_kernel(q, k, v, do, mask, dx, *, pairs):
    low_half = head_lanes()
    keep = mask[...] > 0
    zero = jnp.zeros((), BF)
    scale = np.float32(HD ** (-0.5))
    wide = pairs * 2 * HD
    for p in range(pairs):
        sl = slice(p * 2 * HD, (p + 1) * 2 * HD)
        qp, kp, vp, dop = q[:, sl], k[:, sl], v[:, sl], do[:, sl]
        gq, gk, gv = [], [], []
        for a in range(2):
            mine = low_half if a == 0 else jnp.logical_not(low_half)
            qm, km, dm = (jnp.where(mine, t, zero) for t in (qp, kp, dop))
            s = dot(km, qp, 1, 1)
            s = jnp.where(keep, s * SCORE_SCALE, MASKED)
            e = jnp.exp2(s - jnp.max(s, axis=0, keepdims=True))
            prob = e * (1.0 / jnp.sum(e, axis=0, keepdims=True))
            gv.append(dot(prob.astype(BF), dm, 1, 0))
            weighed = prob * dot(vp, dm, 1, 1)
            inner = jnp.sum(weighed, axis=0, keepdims=True)
            ds = (weighed - prob * inner).astype(BF)
            gk.append(dot(ds, qm, 1, 0))
            gq.append(dot(ds, km, 0, 0))
        at = p * 2 * HD
        dx[:, at : at + 2 * HD] = ((gq[0] + gq[1]) * scale).astype(BF)
        dx[:, wide + at : wide + at + 2 * HD] = ((gk[0] + gk[1]) * scale).astype(BF)
        dx[:, 2 * wide + at : 2 * wide + at + 2 * HD] = (gv[0] + gv[1]).astype(BF)


def attend_back(qkv, do, mask_col, slots):
    rows, three = qkv.shape
    width, images = three // 3, rows // slots
    block = lambda n: pl.BlockSpec((slots, width), lambda i: (i, n))
    return pl.pallas_call(
        functools.partial(attend_back_kernel, pairs=width // (2 * HD)),
        grid=(images,),
        in_specs=[block(0), block(1), block(2), block(0), pl.BlockSpec((slots, 1), lambda i: (i, 0))],
        out_specs=pl.BlockSpec((slots, 3 * width), lambda i: (i, 0)),
        out_shape=SD((rows, 3 * width), BF),
        compiler_params=params(16),
        cost_estimate=cost(20),
        name="attend_back",
    )(qkv, qkv, qkv, do, mask_col)


def middle_kernel(sc, tok, o, sm, cot, keep, own, *rest, slots):
    pieces = rest[:6]
    mid, h2, dm, wbuf, sems = rest[6:]
    images, count, width = tok.shape
    every = pl.ds(0, width)
    copies = run_copies(
        place_rows(wbuf, sc, (own, every), pieces, every, pl.ds(width, width), own.shape[0], 1),
        sems,
    )
    for c in copies:
        c.start()
    tail = count // 8 * 8
    for i in range(images):
        sl = slice(i * slots, i * slots + count)
        dm[i * slots + tail : (i + 1) * slots, :] = jnp.zeros((slots - tail, width), BF)
        dm[sl, :] = (cot[i].astype(F32) * keep[sl, :]).astype(BF)
    for c in copies:
        c.wait()
    mid[...] = dot(o[...], wbuf[...], 1, 0) + sm[OB : OB + 1, :]
    for i in range(images):
        sl = slice(i * slots, i * slots + count)
        mid[sl, :] += tok[i].astype(F32)
    xhat, _ = normalized(mid[...])
    h2[...] = (xhat * sm[G2 : G2 + 1, :] + sm[B2 : B2 + 1, :]).astype(BF)


def middle_part(sc, tok, o, sm, cot, keep, own, pieces, slots):
    rows, width = o.shape
    full = lambda a: pl.BlockSpec(a.shape, lambda j, sc: (0,) * a.ndim)
    whole = pl.BlockSpec((rows, width), lambda j, sc: (0, 0))
    return pl.pallas_call(
        functools.partial(middle_kernel, slots=slots),
        grid_spec=pltpu.PrefetchScalarGridSpec(
            num_scalar_prefetch=1,
            grid=(1,),
            in_specs=[VM] * 5 + [ANY] * 7,
            out_specs=[VM] * 3,
            scratch_shapes=[pltpu.VMEM((width, width), BF), pltpu.SemaphoreType.DMA((7,))],
        ),
        out_shape=[SD((rows, width), F32), SD((rows, width), BF), SD((rows, width), BF)],
        compiler_params=params(16),
        cost_estimate=cost(9),
        name="middle",
    )(sc, tok, o, sm, cot, keep, own, *pieces)


def store_halves(core, own_ref, send_ref, index, first, second):
    @pl.when(core == 0)
    def _():
        own_ref[index] = first
        send_ref[index] = second

    @pl.when(core != 0)
    def _():
        own_ref[index] = second
        send_ref[index] = first


def mlp_kernel(sc, h2, dm, sm, wup, wdown, *rest, k):
    pieces, rest = rest[:6], rest[6:]
    if k:
        old_down, old_dh2 = rest[:2]
        rest = rest[2:]
    down, dh2, up_own, up_send, dn_own, dn_send, gub, ubuf, dbuf, sems = rest
    shard, core = sc[0], sc[1]
    step = pl.program_id(0)
    width = h2.shape[1]
    height = wup.shape[0]
    half, part = height // 2, wdown.shape[0] // 2
    take = slice(k * part, (k + 1) * part)
    blocks = []
    for j in range(2):
        mine = pl.ds(pl.multiple_of(shard * height, 16), height)
        pairs = []
        for h in range(2):
            at = pl.multiple_of((2 * ((shard >> 1) ^ j) + h) * width + k * part, 128)
            pairs.append(
                (wup.at[:, pl.ds(at, part)], ubuf.at[j, mine, pl.ds(h * part, part)])
            )
        if j == 0:
            at = pl.multiple_of((shard & 1) * part, 16)
            pairs.append((wdown.at[pl.ds(k * part, part), :], dbuf.at[0, pl.ds(at, part), :]))
        for side in range(2):
            which = core if side == 0 else 1 - core
            for m in range(1, 4):
                piece = pieces[side * 3 + m - 1]
                at = pl.multiple_of((shard ^ m) * height + which * half, 16)
                g = j ^ (m >> 1)
                pairs.append((piece.at[pl.ds(g * half, half), :], ubuf.at[j, pl.ds(at, half), :]))
                if m >> 1 == j:
                    at = ((shard ^ m) & 1) * part + which * (part // 2)
                    at = pl.multiple_of(at, 16)
                    pairs.append(
                        (
                            piece.at[pl.ds(2 * half, part // 2), :],
                            dbuf.at[j, pl.ds(at, part // 2), :],
                        )
                    )
        blocks.append(run_copies(pairs, sems, 12 * j))

    @pl.when(step == 0)
    def _():
        for c in blocks[0] + blocks[1]:
            c.start()
        for c in blocks[0]:
            c.wait()

    @pl.when(step == 1)
    def _():
        for c in blocks[1]:
            c.wait()

    uw, dw = ubuf[step], dbuf[step]
    x, g = h2[...], dm[...]
    pair = 2 * ((shard >> 1) ^ step)
    bias = jnp.concatenate([sm[pl.ds(UB + pair + h, 1), take] for h in range(2)], axis=1)
    u = dot(x, uw, 1, 0) + bias
    dact = dot(g, dw, 1, 1)
    cdf = 0.5 * (1.0 + lax.erf(u * np.float32(np.sqrt(0.5))))
    act = (u * cdf).astype(BF)
    slope = cdf + u * (jnp.exp(-0.5 * u * u) * np.float32(1.0 / np.sqrt(2.0 * np.pi)))
    du = (dact * slope).astype(BF)
    bsum = jnp.sum(du.astype(F32), axis=0, keepdims=True)
    gd = dot(act, g, 0, 0).astype(BF)
    for h in range(2):
        gub[h] = bsum[:, h * part : (h + 1) * part]
        for i in range(2):
            for n in range(2):
                span = slice(n * part, (n + 1) * part)
                at = h * part + i * half
                store_halves(
                    core,
                    dn_own,
                    dn_send,
                    (h ^ (shard & 1), 2 * i + n),
                    gd[at : at + half, span],
                    gd[at + part // 2 : at + part // 2 + half, span],
                )
    gu = dot(x, du, 0, 0).astype(BF)
    for m in range(4):
        at = m * height
        for h in range(2):
            span = slice(h * part, (h + 1) * part)
            store_halves(
                core,
                up_own,
                up_send,
                (shard ^ m, h),
                gu[at : at + half, span],
                gu[at + half : at + height, span],
            )
    new_down = dot(act, dw, 1, 0)
    new_dh2 = dot(du, uw, 1, 1)

    @pl.when(step == 0)
    def _():
        if k:
            down[...] = old_down[...] + new_down
            dh2[...] = old_dh2[...] + new_dh2
        else:
            down[...] = new_down
            dh2[...] = new_dh2

    @pl.when(step > 0)
    def _():
        down[...] += new_down
        dh2[...] += new_dh2


def mlp_part(sc, h2, dm, sm, wup, wdown, pieces, k, old):
    rows, width = h2.shape
    half, part = wup.shape[0] // 2, wdown.shape[0] // 2
    once = pl.Buffered(1)
    full = lambda a: pl.BlockSpec(a.shape, lambda j, sc: (0,) * a.ndim, pipeline_mode=once)
    whole = pl.BlockSpec((rows, width), lambda j, sc: (0, 0), pipeline_mode=once)
    by_up = pl.BlockSpec((4, 2, half, part), lambda j, sc: (0, (sc[0] >> 1) ^ j, 0, 0))
    by_down = pl.BlockSpec((2, 4, half, part), lambda j, sc: (j, 0, 0, 0))
    shares = SD((4, 4, half, part), BF)
    return pl.pallas_call(
        functools.partial(mlp_kernel, k=k),
        grid_spec=pltpu.PrefetchScalarGridSpec(
            num_scalar_prefetch=1,
            grid=(2,),
            in_specs=[VM] * 3 + [ANY] * 8 + [VM] * len(old),
            out_specs=[VM] * 2
            + [by_up] * 2
            + [by_down] * 2
            + [pl.BlockSpec((2, 1, part), lambda j, sc: ((sc[0] >> 1) ^ j, 0, 0))],
            scratch_shapes=[
                pltpu.VMEM((2, width, width), BF),
                pltpu.VMEM((2, width, width), BF),
                pltpu.SemaphoreType.DMA((24,)),
            ],
        ),
        out_shape=[SD((rows, width), F32)] * 2 + [shares] * 4 + [SD((4, 1, part), F32)],
        compiler_params=params(36),
        cost_estimate=cost(26),
        name="mlp%d" % k,
    )(sc, h2, dm, sm, wup, wdown, *pieces, *old)


def after_kernel(sc, down, dh2, mid, cot, keep, sm, o, dm, own, *rest, slots):
    pieces = rest[:6]
    out, dmid, do, g_own, g_send, gs, wbuf, sems = rest[6:]
    images, count, width = cot.shape
    every = pl.ds(0, width)
    height = own.shape[0]
    copies = run_copies(
        place_rows(wbuf, sc, (own, every), pieces, every, pl.ds(width, width), height, 1), sems
    )
    for c in copies:
        c.start()
    e0 = dh2[...]
    xhat, rsq = normalized(mid[...])
    gs[...] = jnp.zeros_like(gs)
    gs[1:2, :] = jnp.sum(e0 * xhat, axis=0, keepdims=True)
    gs[2:3, :] = jnp.sum(e0, axis=0, keepdims=True)
    gs[3:4, :] = jnp.sum(dm[...].astype(F32), axis=0, keepdims=True)
    dmid[...] = norm_back(e0 * sm[G2 : G2 + 1, :], xhat, rsq)
    for i in range(images):
        sl = slice(i * slots, i * slots + count)
        dmid[sl, :] += cot[i].astype(F32) * keep[sl, :]
        out[i] = (keep[sl, :] * (mid[sl, :] + down[sl, :] + sm[DB : DB + 1, :])).astype(BF)
    low = dmid[...].astype(BF)
    gs[0:1, :] = jnp.sum(low.astype(F32), axis=0, keepdims=True)
    for c in copies:
        c.wait()
    do[...] = dot(low, wbuf[...], 1, 1).astype(BF)
    gw = dot(o[...], low, 0, 0).astype(BF)
    half, part = height // 2, width // 2
    for m in range(4):
        for j in range(2):
            cols = slice(j * part, (j + 1) * part)
            at = m * height
            store_halves(
                sc[1],
                g_own,
                g_send,
                (sc[0] ^ m, j),
                gw[at : at + half, cols],
                gw[at + half : at + height, cols],
            )


def after_mlp(sc, down, dh2, mid, cot, keep, sm, o, dm, own, pieces, slots):
    rows, width = o.shape
    half, part = own.shape[0] // 2, width // 2
    full = lambda a: pl.BlockSpec(a.shape, lambda j, sc: (0,) * a.ndim)
    whole = pl.BlockSpec((rows, width), lambda j, sc: (0, 0))
    share = pl.BlockSpec((4, 2, half, part), lambda j, sc: (0, 3, 0, 0))
    return pl.pallas_call(
        functools.partial(after_kernel, slots=slots),
        grid_spec=pltpu.PrefetchScalarGridSpec(
            num_scalar_prefetch=1,
            grid=(1,),
            in_specs=[VM] * 8 + [ANY] * 7,
            out_specs=[VM] * 3 + [share] * 2 + [VM],
            scratch_shapes=[pltpu.VMEM((width, width), BF), pltpu.SemaphoreType.DMA((7,))],
        ),
        out_shape=[SD(cot.shape, BF), SD((rows, width), F32), SD((rows, width), BF)]
        + [SD((4, 8, half, part), BF)] * 2
        + [SD((8, width), F32)],
        compiler_params=params(24),
        cost_estimate=cost(15),
        name="after_mlp",
    )(sc, down, dh2, mid, cot, keep, sm, o, dm, own, *pieces)


def project_grad_kernel(sc, h1, dx, old_own, old_send, g_own, g_send, gs, *, height):
    half, part = height // 2, dx.shape[1] // 2
    low = dx[...]
    gs[0] = jnp.broadcast_to(jnp.sum(low.astype(F32), axis=0, keepdims=True), gs.shape[1:])
    gw = dot(h1[...], low, 0, 0).astype(BF)
    for m in range(4):
        for j in range(2):
            cols = slice(j * part, (j + 1) * part)
            at = m * height
            store_halves(
                sc[1],
                g_own,
                g_send,
                (sc[0] ^ m, j),
                gw[at : at + half, cols],
                gw[at + half : at + height, cols],
            )


def project_grad(sc, h1, dx, g_own, g_send, height):
    rows, width = h1.shape
    half, part = height // 2, width // 2
    share = pl.BlockSpec((4, 2, half, part), lambda j, sc: (0, j, 0, 0))
    return pl.pallas_call(
        functools.partial(project_grad_kernel, height=height),
        grid_spec=pltpu.PrefetchScalarGridSpec(
            num_scalar_prefetch=1,
            grid=(3,),
            in_specs=[
                VM,
                pl.BlockSpec((rows, width), lambda j, sc: (0, j)),
                ANY,
                ANY,
            ],
            out_specs=[share, share, pl.BlockSpec((1, 8, width), lambda j, sc: (j, 0, 0))],
        ),
        out_shape=[SD((4, 8, half, part), BF)] * 2 + [SD((3, 8, width), F32)],
        input_output_aliases={3: 0, 4: 1},
        compiler_params=params(20),
        cost_estimate=cost(10),
        name="project_grad",
    )(sc, h1, dx, g_own, g_send)


def tokens_grad_kernel(sc, dx, tok, sm, dmid, ga, gp, gu0, gu1, own, *rest, slots):
    pieces = rest[:6]
    out, gs, wbuf, acc, sems = rest[6:]
    images, count, width = tok.shape
    height = own.shape[0]
    two, third = pl.ds(0, 2 * width), pl.ds(2 * width, width)
    pairs = place_rows(wbuf, sc, (own, two), pieces, two, two, height)
    pairs += place_rows(wbuf, sc, (own, third), pieces, third, pl.ds(0, width), height, 1)
    copies = run_copies(pairs, sems)
    for c in copies:
        c.start()
    gs[...] = jnp.zeros_like(gs)
    gs[OB : OB + 4, :] = ga[0:4, :]
    gs[QB : QB + 1, :] = gp[0, 0:1, :]
    gs[VB : VB + 1, :] = gp[2, 0:1, :]
    for b in range(4):
        gs[UB + b : UB + b + 1, : width // 2] = gu0[b]
        gs[UB + b : UB + b + 1, width // 2 :] = gu1[b]
    for c in copies:
        c.wait()
    acc[...] = dot(dx[...], wbuf[...], 1, 1)
    gain = jnp.zeros((1, width), F32)
    shift = jnp.zeros((1, width), F32)
    for i in range(images):
        sl = slice(i * slots, i * slots + count)
        e0 = acc[sl, :]
        xhat, rsq = normalized(tok[i].astype(F32))
        gain += jnp.sum(e0 * xhat, axis=0, keepdims=True)
        shift += jnp.sum(e0, axis=0, keepdims=True)
        out[i] = (dmid[sl, :] + norm_back(e0 * sm[G1 : G1 + 1, :], xhat, rsq)).astype(BF)
    gs[G1 : G1 + 1, :] = gain
    gs[B1 : B1 + 1, :] = shift


def tokens_grad(sc, dx, tok, sm, dmid, ga, gp, gu0, gu1, own, pieces, slots):
    rows, width = dmid.shape
    full = lambda a: pl.BlockSpec(a.shape, lambda j, sc: (0,) * a.ndim)
    operands = (dx, tok, sm, dmid, ga, gp, gu0, gu1)
    return pl.pallas_call(
        functools.partial(tokens_grad_kernel, slots=slots),
        grid_spec=pltpu.PrefetchScalarGridSpec(
            num_scalar_prefetch=1,
            grid=(1,),
            in_specs=[VM] * len(operands) + [ANY] * 7,
            out_specs=[VM] * 2,
            scratch_shapes=[
                pltpu.VMEM((width, 3 * width), BF),
                pltpu.VMEM((rows, width), F32),
                pltpu.SemaphoreType.DMA((14,)),
            ],
        ),
        out_shape=[SD(tok.shape, BF), SD((16, width), F32)],
        compiler_params=params(24),
        cost_estimate=cost(13),
        name="tokens_grad",
    )(sc, *operands, own, *pieces)


def lay_kernel(sc, *refs, kind):
    core, odd = sc[1], sc[2] % 2
    ins, (wide, tall) = refs[:-2], refs[-2:]
    half, part = ins[0].shape[1:]

    def put(k, side, first, second):
        which = core if side == 0 else 1 - core
        rows = pl.ds(pl.multiple_of(which * half, 8), half)
        if kind == "mlp":
            for b in range(4):
                wide[rows, pl.ds((2 * b + k) * part, part)] = first[b].astype(F32)
            for i in range(2):
                at = pl.multiple_of(which * 2 * half + (k * 4 + i) * half, 8)
                for j in range(2):
                    tall[pl.ds(at, half), pl.ds(j * part, part)] = second[2 * i + j].astype(F32)
        else:
            for n in range(4):
                wide[rows, pl.ds(n * part, part)] = first[n].astype(F32)
            for n in range(2):
                wide[rows, pl.ds((4 + n) * part, part)] = second[n].astype(F32)
                tall[rows, pl.ds(n * part, part)] = second[2 + n].astype(F32)

    for k in range(len(ins) // 4):
        kept, other, skept, sother = ins[4 * k : 4 * k + 4]

        @pl.when(odd == 0)
        def _(k=k, kept=kept, other=other, skept=skept, sother=sother):
            put(k, 0, kept, other)
            put(k, 1, skept, sother)

        @pl.when(odd != 0)
        def _(k=k, kept=kept, other=other, skept=skept, sother=sother):
            put(k, 0, other, kept)
            put(k, 1, sother, skept)


def lay_out(sc, finals, kind, shapes):
    full = lambda s: pl.BlockSpec(s, lambda j, sc: (0,) * len(s))
    flat = [a for group in finals for a in group]
    return pl.pallas_call(
        functools.partial(lay_kernel, kind=kind),
        grid_spec=pltpu.PrefetchScalarGridSpec(
            num_scalar_prefetch=1,
            grid=(1,),
            in_specs=[VM] * len(flat),
            out_specs=[VM] * 2,
        ),
        out_shape=[SD(s, F32) for s in shapes],
        compiler_params=params(8),
        cost_estimate=cost(4),
        name="lay_" + kind,
    )(sc, *flat)


def hops():
    def table(move):
        pairs = []
        for dp in range(8):
            for fs in range(4):
                z, core, shard = move(dp // 2, dp % 2, fs)
                pairs.append((dp * 4 + fs, (z * 2 + core) * 4 + shard))
        return pairs

    moves = {
        "sib": lambda z, c, f: (z, 1 - c, f),
        "x": lambda z, c, f: (z, c, f ^ 1),
        "y": lambda z, c, f: (z, c, f ^ 2),
        "xy": lambda z, c, f: (z, c, f ^ 3),
        "z1": lambda z, c, f: (z ^ 1, c, f),
        "z2": lambda z, c, f: (z ^ 2, c, f),
        "z3": lambda z, c, f: (z ^ 3, c, f),
    }
    tables = {name: table(move) for name, move in moves.items()}
    return lambda value, name: lax.ppermute(value, ("dp", "fsdp"), tables[name])


class Transfer:
    def __init__(self, stages):
        self.stages = stages
        self.flying = next(stages)
        self.result = None

    def step(self, landed):
        try:
            self.flying = self.stages.send(landed)
        except StopIteration as end:
            self.flying, self.result = (), end.value


def advance(held, *transfers):
    values = lax.optimization_barrier((held, tuple(t.flying for t in transfers)))
    for t, landed in zip(transfers, values[1]):
        t.step(landed)
    return values[0]


PLANE = ("x", "y", "xy")
LINE = ("z1", "z2", "z3")


def gather_stages(hop, own):
    far = yield tuple(hop(own, name) for name in PLANE)
    near = yield tuple(hop(a, "sib") for a in far)
    return tuple(far) + tuple(near)


def small_stages(hop, own):
    return (own,) + tuple((yield tuple(hop(own, name) for name in PLANE)))


def add(a, b):
    return (a.astype(F32) + b.astype(F32)).astype(BF)


def line_stages(hop, even, total):
    parts = total.shape[0] // 2
    keep = jnp.where(even, total[:parts], total[parts:])
    give = jnp.where(even, total[parts:], total[:parts]).astype(BF)
    (got,) = yield (hop(give, "z1"),)
    half = lax.optimization_barrier((keep + got.astype(F32)).astype(BF))
    (got,) = yield (hop(half, "z2"),)
    kept = add(half, got)
    other, skept = yield (hop(kept, "z1"), hop(kept, "sib"))
    (sother,) = yield (hop(other, "sib"),)
    return kept, other, skept, sother


def plane_stages(hop, even, chip):
    got = yield tuple(hop(chip(r).astype(BF), name) for r, name in enumerate(PLANE, 1))
    total = chip(0)
    for a in got:
        total = total + a.astype(F32)
    return (yield from line_stages(hop, even, total))


def ffn_stages(hop, even, up_own, up_send, dn_own, dn_send):
    up_got, dn_got = yield (hop(up_send, "sib"), hop(dn_send, "sib"))

    def chip(r):
        return jnp.concatenate(
            [
                up_own[r].astype(F32) + up_got[r].astype(F32),
                dn_own[r].astype(F32) + dn_got[r].astype(F32),
            ]
        )

    return (yield from plane_stages(hop, even, chip))


def attn_stages(hop, even, own, send):
    (got,) = yield (hop(send, "sib"),)
    chip = lambda r: own[r].astype(F32) + got[r].astype(F32)
    return (yield from plane_stages(hop, even, chip))


def sum_stages(hop, value):
    (got,) = yield (hop(value, "sib"),)
    value = value + got
    for names in (PLANE, LINE):
        one, two, three = yield tuple(hop(value, name) for name in names)
        value = (value + one) + (two + three)
    return value


def on_device_fast(
    tokens,
    mask,
    cotangent,
    ln1_gain,
    ln1_bias,
    w_qkv,
    qv_bias,
    w_out,
    out_bias,
    ln2_gain,
    ln2_bias,
    w_up,
    up_bias,
    w_down,
    down_bias,
):
    images, count, width = tokens.shape
    slots = -(-count // 8) * 8
    height = w_out.shape[0]
    half, part = height // 2, width // 2
    hop = hops()
    shard = lax.axis_index("fsdp")
    dp = lax.axis_index("dp")
    sc = jnp.stack([shard, dp % 2, dp // 2]).astype(jnp.int32)
    even = (dp // 2) % 2 == 0

    (own_attn,) = pack(sc, pack_attn_kernel, 3, [(height, 2 * width)], w_qkv, w_out)
    first = Transfer(gather_stages(hop, own_attn))
    small = (ln1_gain, ln1_bias, qv_bias, out_bias, ln2_gain, ln2_bias, down_bias, up_bias)
    small = jnp.concatenate([a.reshape(-1, height) for a in small])
    small = Transfer(small_stages(hop, jnp.pad(small, ((0, 4), (0, -height % 128)))))
    own_ffn = pack(sc, pack_ffn_kernel, 10, [(2 * height, width)] * 2, w_up, w_down)
    own_ffn = advance(own_ffn, first, small)
    ffn0 = Transfer(gather_stages(hop, own_ffn[0]))
    sc = advance(sc, first)
    pieces = first.result

    keep = jnp.pad(mask.astype(F32), ((0, 0), (0, slots - count)))
    mask_row = keep.reshape(images, 1, slots)
    keep_col = keep.reshape(images * slots, 1)

    h1, qkv, sm = project(sc, tokens, w_qkv, pieces, small.result, slots)
    o = attend(qkv, mask_row, slots)
    o, own_ffn1 = lax.optimization_barrier((o, own_ffn[1]))
    ffn1 = Transfer(gather_stages(hop, own_ffn1))
    o = advance(o, ffn0)
    mid, h2, dm = middle_part(sc, tokens, o, sm, cotangent, keep_col, w_out, pieces, slots)
    h2 = advance(h2, ffn0)
    down, dh2, *shares, gu0 = mlp_part(sc, h2, dm, sm, w_up, w_down, ffn0.result, 0, ())
    down, dh2, *shares = advance((down, dh2, *shares), ffn1)
    m0 = Transfer(ffn_stages(hop, even, *shares))
    sc = advance(sc, ffn1, m0)
    down, dh2, *shares, gu1 = mlp_part(
        sc, h2, dm, sm, w_up, w_down, ffn1.result, 1, (down, dh2)
    )
    down, dh2, *shares = advance((down, dh2, *shares), m0)
    m1 = Transfer(ffn_stages(hop, even, *shares))
    layer_out, dmid, do, g_own, g_send, ga = after_mlp(
        sc, down, dh2, mid, cotangent, keep_col, sm, o, dm, w_out, pieces, slots
    )
    do = advance(do, m0, m1)
    dx = attend_back(qkv, do, keep_col, slots)
    dx = advance(dx, m0)
    g_own, g_send, gp = project_grad(sc, h1, dx, g_own, g_send, height)
    g_own, g_send, dx = advance((g_own, g_send, dx), m0, m1)
    attn = Transfer(attn_stages(hop, even, g_own, g_send))
    sc = advance(sc, attn)
    sc = advance(sc, m1)
    grad_tokens, gs = tokens_grad(
        sc, dx, tokens, sm, dmid, ga, gp, gu0, gu1, w_qkv, pieces, slots
    )
    gs = advance(gs, m0)
    total = Transfer(sum_stages(hop, gs))
    advance((), m1)
    advance((), attn, total)
    advance((), m1)
    advance((), attn, total)
    advance((), m1)
    ffn = lay_out(
        sc, (m0.result, m1.result), "mlp", ((height, 4 * width), (4 * height, width))
    )
    ffn = advance(ffn, attn, total)
    gs = total.result

    def mine(r, n=1):
        return lax.dynamic_slice(gs[r : r + n].reshape(-1), (shard * (n * height),), (n * height,))

    rows = tuple(mine(r) for r in (G1, B1, OB, G2, B2, DB)) + (mine(QB, 2), mine(UB, 4))
    while attn.flying:
        ffn, rows = advance((ffn, rows), attn)
    g1, b1, ob, g2, b2, db, qvb, ub = rows
    grad_w_up, grad_w_down = ffn
    grad_w_qkv, grad_w_out = lay_out(
        sc, (attn.result,), "attn", ((height, 3 * width), (height, width))
    )
    return (
        layer_out,
        grad_tokens,
        g1,
        b1,
        grad_w_qkv,
        qvb,
        grad_w_out,
        ob,
        g2,
        b2,
        grad_w_up,
        ub,
        grad_w_down,
        db,
    )


def norm(values, gain, shift):
    mean_value = jnp.mean(values, axis=-1, keepdims=True)
    centred = values - mean_value
    variance = jnp.mean(centred * centred, axis=-1, keepdims=True)
    return centred * lax.rsqrt(variance + EPS) * gain + shift


def gelu_exact(values):
    return jax.nn.gelu(values, approximate=False)


def score_block(query, key_part, valid):
    scores = jnp.einsum(
        "iqhe,ikhe->ihqk", query, key_part, preferred_element_type=jnp.float32
    ) * HD ** (-0.5)
    return jnp.where(valid, scores, -1e30)


def arrange(grad, groups, copies):
    shaped = grad.reshape((groups, copies, grad.shape[0] // (groups * copies)) + grad.shape[1:])
    return jnp.swapaxes(shaped, 0, 1).reshape(grad.shape)


def reduce_six(grad_one, grad_two, grad_three, grad_four, grad_five, grad_six):
    groups = lax.axis_size("fsdp")
    copies = lax.axis_size("dp")
    pieces = (
        lax.psum_scatter(
            arrange(grad_one, groups, copies), ("dp", "fsdp"), scatter_dimension=0, tiled=True
        ),
        lax.psum_scatter(
            arrange(grad_two, groups, copies), ("dp", "fsdp"), scatter_dimension=0, tiled=True
        ),
        lax.psum_scatter(
            arrange(grad_three, groups, copies), ("dp", "fsdp"), scatter_dimension=0, tiled=True
        ),
        lax.psum_scatter(
            arrange(grad_four, groups, copies), ("dp", "fsdp"), scatter_dimension=0, tiled=True
        ),
        lax.psum_scatter(
            arrange(grad_five, groups, copies), ("dp", "fsdp"), scatter_dimension=0, tiled=True
        ),
        lax.psum_scatter(
            arrange(grad_six, groups, copies), ("dp", "fsdp"), scatter_dimension=0, tiled=True
        ),
    )
    return (
        lax.all_gather(pieces[0].astype(jnp.bfloat16), "dp", axis=0, tiled=True).astype(
            jnp.float32
        ),
        lax.all_gather(pieces[1].astype(jnp.bfloat16), "dp", axis=0, tiled=True).astype(
            jnp.float32
        ),
        lax.all_gather(pieces[2].astype(jnp.bfloat16), "dp", axis=0, tiled=True).astype(
            jnp.float32
        ),
        lax.all_gather(pieces[3].astype(jnp.bfloat16), "dp", axis=0, tiled=True).astype(
            jnp.float32
        ),
        lax.all_gather(pieces[4].astype(jnp.bfloat16), "dp", axis=0, tiled=True).astype(
            jnp.float32
        ),
        lax.all_gather(pieces[5].astype(jnp.bfloat16), "dp", axis=0, tiled=True).astype(
            jnp.float32
        ),
    )


def on_device(
    tokens,
    mask,
    cotangent,
    ln1_gain,
    ln1_bias,
    w_qkv,
    qv_bias,
    w_out,
    out_bias,
    ln2_gain,
    ln2_bias,
    w_up,
    up_bias,
    w_down,
    down_bias,
):
    image_count, slot_count, width = tokens.shape
    row_count = image_count * slot_count
    heads = width // HD
    scale = HD ** (-0.5)
    attn_full = (
        lax.all_gather(ln1_gain, "fsdp", axis=0, tiled=True),
        lax.all_gather(ln1_bias, "fsdp", axis=0, tiled=True),
        lax.all_gather(w_qkv, "fsdp", axis=0, tiled=True),
        lax.all_gather(qv_bias, "fsdp", axis=0, tiled=True),
        lax.all_gather(w_out, "fsdp", axis=0, tiled=True),
        lax.all_gather(out_bias, "fsdp", axis=0, tiled=True),
    )
    mlp_full = (
        lax.all_gather(ln2_gain, "fsdp", axis=0, tiled=True),
        lax.all_gather(ln2_bias, "fsdp", axis=0, tiled=True),
        lax.all_gather(w_up, "fsdp", axis=0, tiled=True),
        lax.all_gather(up_bias, "fsdp", axis=0, tiled=True),
        lax.all_gather(w_down, "fsdp", axis=0, tiled=True),
        lax.all_gather(down_bias, "fsdp", axis=0, tiled=True),
    )
    gain_one, shift_one, qkv_weight, qkv_shift, out_weight, out_shift = attn_full
    gain_two, shift_two, up_weight, up_shift, down_weight, down_shift = mlp_full
    keep = mask.astype(jnp.float32)
    valid = (keep > 0.5)[:, None, None, :]
    keep_rows = keep.reshape(row_count, 1)
    inputs = tokens.astype(jnp.float32).reshape(row_count, width)
    normed_one, norm_one_back = jax.vjp(
        norm, inputs, gain_one.astype(jnp.float32), shift_one.astype(jnp.float32)
    )
    normed_low = normed_one.astype(jnp.bfloat16)
    qv_float = qkv_shift.astype(jnp.float32)
    full_bias = jnp.concatenate(
        [qv_float[:width], jnp.zeros((width,), jnp.float32), qv_float[width:]]
    )
    projected = (
        jnp.dot(normed_low, qkv_weight, preferred_element_type=jnp.float32) + full_bias
    ).astype(jnp.bfloat16)
    query = projected[:, :width].reshape(image_count, slot_count, heads, HD)
    key_part = projected[:, width : 2 * width].reshape(image_count, slot_count, heads, HD)
    value = projected[:, 2 * width :].reshape(image_count, slot_count, heads, HD)
    scores = score_block(query, key_part, valid)
    top = jnp.max(scores, axis=-1, keepdims=True)
    lse = top + jnp.log(jnp.sum(jnp.exp(scores - top), axis=-1, keepdims=True))
    probs_low = jnp.exp(scores - lse).astype(jnp.bfloat16)
    mixed = jnp.einsum("ihqk,ikhe->iqhe", probs_low, value, preferred_element_type=jnp.float32)
    mixed = mixed.reshape(row_count, width).astype(jnp.bfloat16)
    middle = (
        inputs
        + jnp.dot(mixed, out_weight, preferred_element_type=jnp.float32)
        + out_shift.astype(jnp.float32)
    )
    normed_two, norm_two_back = jax.vjp(
        norm, middle, gain_two.astype(jnp.float32), shift_two.astype(jnp.float32)
    )
    normed_two_low = normed_two.astype(jnp.bfloat16)
    upward = jnp.dot(
        normed_two_low, up_weight, preferred_element_type=jnp.float32
    ) + up_shift.astype(jnp.float32)
    active, gelu_back = jax.vjp(gelu_exact, upward)
    active_low = active.astype(jnp.bfloat16)
    downward = jnp.dot(
        active_low, down_weight, preferred_element_type=jnp.float32
    ) + down_shift.astype(jnp.float32)
    layer_out = (
        (keep_rows * (middle + downward))
        .astype(jnp.bfloat16)
        .reshape(image_count, slot_count, width)
    )
    mlp_back = (
        lax.all_gather(ln2_gain, "fsdp", axis=0, tiled=True),
        lax.all_gather(ln2_bias, "fsdp", axis=0, tiled=True),
        lax.all_gather(w_up, "fsdp", axis=0, tiled=True),
        lax.all_gather(up_bias, "fsdp", axis=0, tiled=True),
        lax.all_gather(w_down, "fsdp", axis=0, tiled=True),
        lax.all_gather(down_bias, "fsdp", axis=0, tiled=True),
    )
    up_back = mlp_back[2]
    down_back = mlp_back[4]
    grad_rows = cotangent.astype(jnp.float32).reshape(row_count, width) * keep_rows
    grad_down_low = grad_rows.astype(jnp.bfloat16)
    grad_w_down = jnp.einsum(
        "rf,rd->fd", active_low, grad_down_low, preferred_element_type=jnp.float32
    )
    grad_down_bias = jnp.sum(grad_down_low, axis=0, dtype=jnp.float32)
    grad_active = jnp.einsum(
        "rd,fd->rf", grad_down_low, down_back, preferred_element_type=jnp.float32
    )
    grad_up_low = gelu_back(grad_active)[0].astype(jnp.bfloat16)
    grad_w_up = jnp.einsum(
        "rd,rf->df", normed_two_low, grad_up_low, preferred_element_type=jnp.float32
    )
    grad_up_bias = jnp.sum(grad_up_low, axis=0, dtype=jnp.float32)
    grad_normed_two = jnp.einsum(
        "rf,df->rd", grad_up_low, up_back, preferred_element_type=jnp.float32
    )
    grad_mid_norm, grad_ln2_gain, grad_ln2_bias = norm_two_back(grad_normed_two)
    grad_middle = grad_rows + grad_mid_norm
    mlp_grads = reduce_six(
        grad_ln2_gain, grad_ln2_bias, grad_w_up, grad_up_bias, grad_w_down, grad_down_bias
    )
    attn_back = (
        lax.all_gather(ln1_gain, "fsdp", axis=0, tiled=True),
        lax.all_gather(ln1_bias, "fsdp", axis=0, tiled=True),
        lax.all_gather(w_qkv, "fsdp", axis=0, tiled=True),
        lax.all_gather(qv_bias, "fsdp", axis=0, tiled=True),
        lax.all_gather(w_out, "fsdp", axis=0, tiled=True),
        lax.all_gather(out_bias, "fsdp", axis=0, tiled=True),
    )
    qkv_back = attn_back[2]
    out_back = attn_back[4]
    grad_attn_low = grad_middle.astype(jnp.bfloat16)
    grad_w_out = jnp.einsum("rd,re->de", mixed, grad_attn_low, preferred_element_type=jnp.float32)
    grad_out_bias = jnp.sum(grad_attn_low, axis=0, dtype=jnp.float32)
    grad_mixed = jnp.einsum(
        "re,de->rd", grad_attn_low, out_back, preferred_element_type=jnp.float32
    )
    grad_mixed = grad_mixed.astype(jnp.bfloat16).reshape(image_count, slot_count, heads, HD)
    probs = jnp.exp(score_block(query, key_part, valid) - lse)
    probs_again = probs.astype(jnp.bfloat16)
    grad_value = jnp.einsum(
        "ihqk,iqhe->ikhe", probs_again, grad_mixed, preferred_element_type=jnp.float32
    )
    grad_probs = jnp.einsum(
        "iqhe,ikhe->ihqk", grad_mixed, value, preferred_element_type=jnp.float32
    )
    inner = jnp.sum(grad_probs * probs, axis=-1, keepdims=True)
    grad_scores = (probs * (grad_probs - inner)).astype(jnp.bfloat16)
    grad_query = (
        jnp.einsum("ihqk,ikhe->iqhe", grad_scores, key_part, preferred_element_type=jnp.float32)
        * scale
    )
    grad_key = (
        jnp.einsum("ihqk,iqhe->ikhe", grad_scores, query, preferred_element_type=jnp.float32)
        * scale
    )
    grad_projected = jnp.concatenate(
        [
            grad_query.reshape(row_count, width),
            grad_key.reshape(row_count, width),
            grad_value.reshape(row_count, width),
        ],
        axis=1,
    ).astype(jnp.bfloat16)
    grad_w_qkv = jnp.einsum(
        "rd,re->de", normed_low, grad_projected, preferred_element_type=jnp.float32
    )
    grad_qv_bias = jnp.concatenate(
        [
            jnp.sum(grad_projected[:, :width], axis=0, dtype=jnp.float32),
            jnp.sum(grad_projected[:, 2 * width :], axis=0, dtype=jnp.float32),
        ]
    )
    grad_normed_one = jnp.einsum(
        "re,de->rd", grad_projected, qkv_back, preferred_element_type=jnp.float32
    )
    grad_in_norm, grad_ln1_gain, grad_ln1_bias = norm_one_back(grad_normed_one)
    grad_tokens = (
        (grad_middle + grad_in_norm).astype(jnp.bfloat16).reshape(image_count, slot_count, width)
    )
    attn_grads = reduce_six(
        grad_ln1_gain, grad_ln1_bias, grad_w_qkv, grad_qv_bias, grad_w_out, grad_out_bias
    )
    return (
        layer_out,
        grad_tokens,
        attn_grads[0],
        attn_grads[1],
        attn_grads[2],
        attn_grads[3],
        attn_grads[4],
        attn_grads[5],
        mlp_grads[0],
        mlp_grads[1],
        mlp_grads[2],
        mlp_grads[3],
        mlp_grads[4],
        mlp_grads[5],
    )


def solution(mesh):
    in_specs = (
        P(("dp", "fsdp"), None, None),
        P(("dp", "fsdp"), None),
        P(("dp", "fsdp"), None, None),
        P("fsdp"),
        P("fsdp"),
        P("fsdp", None),
        P("fsdp"),
        P("fsdp", None),
        P("fsdp"),
        P("fsdp"),
        P("fsdp"),
        P("fsdp", None),
        P("fsdp"),
        P("fsdp", None),
        P("fsdp"),
    )
    out_specs = (
        P(("dp", "fsdp"), None, None),
        P(("dp", "fsdp"), None, None),
        P("fsdp"),
        P("fsdp"),
        P("fsdp", None),
        P("fsdp"),
        P("fsdp", None),
        P("fsdp"),
        P("fsdp"),
        P("fsdp"),
        P("fsdp", None),
        P("fsdp"),
        P("fsdp", None),
        P("fsdp"),
    )
    fast = dict(mesh.shape) == {"dp": 8, "fsdp": 4}
    return jax.shard_map(
        on_device_fast if fast else on_device, mesh=mesh, in_specs=in_specs, out_specs=out_specs, check_vma=False
    )
```

```python
import functools

import jax
import jax.numpy as jnp
import numpy as np
from jax import lax
from jax.experimental import pallas as pl
from jax.experimental.pallas import tpu as pltpu
from jax.sharding import PartitionSpec as P

HD = 64
EPS = 1e-06
F32 = jnp.float32
BF = jnp.bfloat16
MB = 2**20
SCORE_SCALE = np.float32(np.log2(np.e) * HD ** (-0.5))
MASKED = np.float32(-1e30)
SD = jax.ShapeDtypeStruct
ANY = pl.BlockSpec(memory_space=pl.ANY)
VM = pl.BlockSpec(memory_space=pltpu.VMEM)


def dot(a, b, ca, cb):
    return lax.dot_general(a, b, (((ca,), (cb,)), ((), ())), preferred_element_type=F32)


def params(mb=58):
    return pltpu.CompilerParams(vmem_limit_bytes=mb * MB)


def cost(micros):
    return pl.CostEstimate(flops=int(micros * 1.15e9), bytes_accessed=0, transcendentals=0)


def normalized(values):
    mean = jnp.mean(values, axis=-1, keepdims=True)
    centred = values - mean
    rsq = lax.rsqrt(jnp.mean(centred * centred, axis=-1, keepdims=True) + EPS)
    return centred * rsq, rsq


def norm_back(e, xhat, rsq):
    return rsq * (
        e
        - jnp.mean(e, axis=-1, keepdims=True)
        - xhat * jnp.mean(e * xhat, axis=-1, keepdims=True)
    )


def run_copies(pairs, sems, base=0):
    copies = [
        pltpu.make_async_copy(src, dst, sems.at[base + n]) for n, (src, dst) in enumerate(pairs)
    ]
    return copies


PACK_MB = 54

G1, B1, QB, VB, OB, G2, B2, DB, UB = range(9)


def all_copies(pairs, sems):
    copies = run_copies(pairs, sems)
    for c in copies:
        c.start()
    for c in copies:
        c.wait()


def pack_attn_kernel(sc, wqkv, wout, *rest):
    small, (top, bottom, table, sems) = rest[:8], rest[8:]
    height, width = wout.shape
    half = height // 2
    rows = pl.ds(pl.multiple_of(sc[1] * half, 16), half)
    copies = run_copies(
        [
            (wqkv.at[rows, pl.ds(0, 2 * width)], top.at[pl.ds(0, half), :]),
            (wqkv.at[rows, pl.ds(2 * width, width)], bottom.at[:, pl.ds(0, width)]),
            (wout.at[rows, :], bottom.at[:, pl.ds(width, width)]),
        ],
        sems,
    )
    for c in copies:
        c.start()
    table[...] = jnp.zeros_like(table)
    row = 0
    for ref in small:
        values = ref[...].astype(F32)
        for n in range(ref.shape[0] // height):
            table[row : row + 1, :height] = values[n * height : (n + 1) * height].reshape(1, height)
            row += 1
    top[half:, : table.shape[1]] = table[...].astype(BF)
    for c in copies:
        c.wait()


def pack_attn(sc, wqkv, wout, small):
    height, width = wout.shape
    lanes = -(-height // 128) * 128
    return pl.pallas_call(
        pack_attn_kernel,
        grid_spec=pltpu.PrefetchScalarGridSpec(
            num_scalar_prefetch=1,
            in_specs=[ANY] * 2 + [VM] * 8,
            out_specs=[VM] * 2,
            scratch_shapes=[pltpu.VMEM((16, lanes), F32), pltpu.SemaphoreType.DMA((3,))],
        ),
        out_shape=[SD((height // 2 + 16, 2 * width), BF), SD((height // 2, 2 * width), BF)],
        compiler_params=params(PACK_MB),
        name="pack_attn",
    )(sc, wqkv, wout, *small)


def pack_ffn_kernel(sc, wup, wdown, ffn0, ffn1, sems):
    width = wdown.shape[1]
    half, part = wup.shape[0] // 2, wdown.shape[0] // 2
    rows = pl.ds(pl.multiple_of(sc[1] * half, 16), half)
    pairs = []
    for k, ffn in enumerate((ffn0, ffn1)):
        for g in range(2):
            for h in range(2):
                block = 2 * ((sc[0] >> 1) ^ g) + h
                at = pl.multiple_of(block * width + k * part, 128)
                pairs.append(
                    (
                        wup.at[rows, pl.ds(at, part)],
                        ffn.at[pl.ds(g * half, half), pl.ds(h * part, part)],
                    )
                )
        at = pl.multiple_of(k * part + sc[1] * (part // 2), 16)
        pairs.append((wdown.at[pl.ds(at, part // 2), :], ffn.at[pl.ds(2 * half, part // 2), :]))
    all_copies(pairs, sems)


def pack(sc, kernel, copies, shapes, *weights):
    return pl.pallas_call(
        kernel,
        grid_spec=pltpu.PrefetchScalarGridSpec(
            num_scalar_prefetch=1,
            in_specs=[ANY] * len(weights),
            out_specs=[ANY] * len(shapes),
            scratch_shapes=[pltpu.SemaphoreType.DMA((copies,))],
        ),
        out_shape=[SD(shape, BF) for shape in shapes],
        compiler_params=params(2),
        name="pack",
    )(sc, *weights)


def place_rows(dst, sc, own, pieces, cols, src_cols, height, base=0):
    half = height // 2
    shard, core = sc[0], sc[1]
    pairs = []
    if own is not None:
        src, take = own
        pairs.append((src.at[:, take], dst.at[pl.ds(pl.multiple_of(shard * height, 16), height), cols]))
    for side in range(2):
        which = core if side == 0 else 1 - core
        for r in range(1, 4):
            at = pl.multiple_of((shard ^ r) * height + which * half, 16)
            pairs.append(
                (
                    pieces[side * 3 + r - 1].at[pl.ds(base * half, half), src_cols],
                    dst.at[pl.ds(at, half), cols],
                )
            )
    return pairs


def fill_small(sc, pieces, sm, height):
    shard = sc[0]
    vals = [pieces[r].astype(F32) for r in range(4)]

    def of(j):
        got = vals[3]
        for r in range(3):
            got = jnp.where(shard == (j ^ r), vals[r], got)
        return got[:, :height]

    by = [of(j) for j in range(4)]
    sm[...] = jnp.zeros_like(sm)
    for j in range(4):
        cols = slice(j * height, (j + 1) * height)
        sm[G1 : B1 + 1, cols] = by[j][0:2]
        sm[OB : DB + 1, cols] = by[j][4:8]
        for n in range(2):
            at = (2 * j + n) % 4 * height
            row = QB if j < 2 else VB
            sm[row : row + 1, at : at + height] = by[j][2 + n : 3 + n]
        for n in range(4):
            sm[UB + j : UB + j + 1, n * height : (n + 1) * height] = by[j][8 + n : 9 + n]


def project_kernel(sc, tok, own, packed, *rest, slots):
    pp, pq = rest[:6], rest[6:12]
    h1, qkv, sm, wbuf, small, sems = rest[12:]
    images, count, width = tok.shape
    height = own.shape[0]
    step = pl.program_id(0)
    two = pl.ds(0, 2 * width)
    third = pl.ds(2 * width, width)
    first = run_copies(place_rows(wbuf, sc, (own, two), pp, two, two, height), sems)
    last = run_copies(
        place_rows(wbuf, sc, (own, third), pq, third, pl.ds(0, width), height),
        sems,
        len(first),
    )

    corner = (pl.ds(height // 2, 16), pl.ds(0, small.shape[2]))
    table = run_copies(
        [
            (ref.at[corner[0], corner[1]], small.at[r])
            for r, ref in enumerate((packed,) + pp[:3])
        ],
        sems,
        len(first) + len(last),
    )

    @pl.when(step == 0)
    def _():
        for c in table + first + last:
            c.start()
        for c in table:
            c.wait()
        fill_small(sc, small, sm, height)
        for i in range(images):
            xhat, _ = normalized(tok[i].astype(F32))
            low = (xhat * sm[G1 : G1 + 1, :] + sm[B1 : B1 + 1, :]).astype(BF)
            tail = count // 8 * 8
            h1[i * slots + tail : (i + 1) * slots, :] = jnp.zeros((slots - tail, width), BF)
            h1[i * slots : i * slots + count, :] = low
        for c in first:
            c.wait()

    @pl.when(step == 2)
    def _():
        for c in last:
            c.wait()

    row = jnp.where(step == 0, sm[QB : QB + 1, :], sm[VB : VB + 1, :])
    row = jnp.where(step == 1, jnp.zeros_like(row), row)
    weight = wbuf[:, pl.ds(pl.multiple_of(step * width, 128), width)]
    qkv[...] = (dot(h1[...], weight, 1, 0) + row).astype(BF)


def project(sc, tok, own, packed, pieces, slots):
    images, _, width = tok.shape
    rows = images * slots
    full = lambda *s: pl.BlockSpec(s, lambda j, sc: (0,) * len(s))
    return pl.pallas_call(
        functools.partial(project_kernel, slots=slots),
        grid_spec=pltpu.PrefetchScalarGridSpec(
            num_scalar_prefetch=1,
            grid=(3,),
            in_specs=[VM] + [ANY] * 14,
            out_specs=[
                VM,
                pl.BlockSpec((rows, width), lambda j, sc: (0, j)),
                VM,
            ],
            scratch_shapes=[
                pltpu.VMEM((width, 3 * width), BF),
                pltpu.VMEM((4, 16, -(-own.shape[0] // 128) * 128), BF),
                pltpu.SemaphoreType.DMA((18,)),
            ],
        ),
        out_shape=[SD((rows, width), BF), SD((rows, 3 * width), BF), SD((16, width), F32)],
        compiler_params=params(54),
        cost_estimate=cost(10),
        name="project",
    )(sc, tok, own, packed, *pieces)


def head_lanes():
    return lax.broadcasted_iota(jnp.int32, (1, 2 * HD), 1) < HD


def attend_kernel(q, k, v, mask, o, *, pairs):
    low_half = head_lanes()
    keep = mask[0] > 0
    zero = jnp.zeros((), BF)
    for p in range(pairs):
        sl = slice(p * 2 * HD, (p + 1) * 2 * HD)
        qp, kp, vp = q[:, sl], k[:, sl], v[:, sl]
        outs = []
        for a in range(2):
            mine = low_half if a == 0 else jnp.logical_not(low_half)
            s = dot(jnp.where(mine, qp, zero), kp, 1, 1)
            s = jnp.where(keep, s * SCORE_SCALE, MASKED)
            e = jnp.exp2(s - jnp.max(s, axis=-1, keepdims=True))
            prob = (e * (1.0 / jnp.sum(e, axis=-1, keepdims=True))).astype(BF)
            outs.append(dot(prob, jnp.where(mine, vp, zero), 1, 0))
        o[:, sl] = (outs[0] + outs[1]).astype(BF)


def attend(qkv, mask_row, slots):
    rows, three = qkv.shape
    width, images = three // 3, rows // slots
    block = lambda n: pl.BlockSpec((slots, width), lambda i: (i, n))
    return pl.pallas_call(
        functools.partial(attend_kernel, pairs=width // (2 * HD)),
        grid=(images,),
        in_specs=[block(0), block(1), block(2), pl.BlockSpec((1, 1, slots), lambda i: (i, 0, 0))],
        out_specs=block(0),
        out_shape=SD((rows, width), BF),
        compiler_params=params(12),
        cost_estimate=cost(11),
        name="attend",
    )(qkv, qkv, qkv, mask_row)


def attend_back_kernel(q, k, v, do, mask, dx, *, pairs):
    low_half = head_lanes()
    keep = mask[...] > 0
    zero = jnp.zeros((), BF)
    scale = np.float32(HD ** (-0.5))
    wide = pairs * 2 * HD
    for p in range(pairs):
        sl = slice(p * 2 * HD, (p + 1) * 2 * HD)
        qp, kp, vp, dop = q[:, sl], k[:, sl], v[:, sl], do[:, sl]
        gq, gk, gv = [], [], []
        for a in range(2):
            mine = low_half if a == 0 else jnp.logical_not(low_half)
            qm, km, dm = (jnp.where(mine, t, zero) for t in (qp, kp, dop))
            s = dot(km, qp, 1, 1)
            s = jnp.where(keep, s * SCORE_SCALE, MASKED)
            e = jnp.exp2(s - jnp.max(s, axis=0, keepdims=True))
            prob = e * (1.0 / jnp.sum(e, axis=0, keepdims=True))
            gv.append(dot(prob.astype(BF), dm, 1, 0))
            weighed = prob * dot(vp, dm, 1, 1)
            inner = jnp.sum(weighed, axis=0, keepdims=True)
            ds = (weighed - prob * inner).astype(BF)
            gk.append(dot(ds, qm, 1, 0))
            gq.append(dot(ds, km, 0, 0))
        at = p * 2 * HD
        dx[:, at : at + 2 * HD] = ((gq[0] + gq[1]) * scale).astype(BF)
        dx[:, wide + at : wide + at + 2 * HD] = ((gk[0] + gk[1]) * scale).astype(BF)
        dx[:, 2 * wide + at : 2 * wide + at + 2 * HD] = (gv[0] + gv[1]).astype(BF)


def attend_back(qkv, do, mask_col, slots):
    rows, three = qkv.shape
    width, images = three // 3, rows // slots
    block = lambda n: pl.BlockSpec((slots, width), lambda i: (i, n))
    return pl.pallas_call(
        functools.partial(attend_back_kernel, pairs=width // (2 * HD)),
        grid=(images,),
        in_specs=[block(0), block(1), block(2), block(0), pl.BlockSpec((slots, 1), lambda i: (i, 0))],
        out_specs=pl.BlockSpec((slots, 3 * width), lambda i: (i, 0)),
        out_shape=SD((rows, 3 * width), BF),
        compiler_params=params(16),
        cost_estimate=cost(20),
        name="attend_back",
    )(qkv, qkv, qkv, do, mask_col)


def middle_kernel(sc, tok, o, sm, cot, keep, own, *rest, slots):
    pieces = rest[:6]
    mid, h2, dm, wbuf, sems = rest[6:]
    images, count, width = tok.shape
    every = pl.ds(0, width)
    copies = run_copies(
        place_rows(wbuf, sc, (own, every), pieces, every, pl.ds(width, width), own.shape[0]),
        sems,
    )
    for c in copies:
        c.start()
    tail = count // 8 * 8
    for i in range(images):
        sl = slice(i * slots, i * slots + count)
        dm[i * slots + tail : (i + 1) * slots, :] = jnp.zeros((slots - tail, width), BF)
        dm[sl, :] = (cot[i].astype(F32) * keep[sl, :]).astype(BF)
    for c in copies:
        c.wait()
    mid[...] = dot(o[...], wbuf[...], 1, 0) + sm[OB : OB + 1, :]
    for i in range(images):
        sl = slice(i * slots, i * slots + count)
        mid[sl, :] += tok[i].astype(F32)
    xhat, _ = normalized(mid[...])
    h2[...] = (xhat * sm[G2 : G2 + 1, :] + sm[B2 : B2 + 1, :]).astype(BF)


def middle_part(sc, tok, o, sm, cot, keep, own, pieces, slots):
    rows, width = o.shape
    full = lambda a: pl.BlockSpec(a.shape, lambda j, sc: (0,) * a.ndim)
    whole = pl.BlockSpec((rows, width), lambda j, sc: (0, 0))
    return pl.pallas_call(
        functools.partial(middle_kernel, slots=slots),
        grid_spec=pltpu.PrefetchScalarGridSpec(
            num_scalar_prefetch=1,
            grid=(1,),
            in_specs=[VM] * 5 + [ANY] * 7,
            out_specs=[VM] * 3,
            scratch_shapes=[pltpu.VMEM((width, width), BF), pltpu.SemaphoreType.DMA((7,))],
        ),
        out_shape=[SD((rows, width), F32), SD((rows, width), BF), SD((rows, width), BF)],
        compiler_params=params(16),
        cost_estimate=cost(9),
        name="middle",
    )(sc, tok, o, sm, cot, keep, own, *pieces)


def store_halves(core, own_ref, send_ref, index, first, second):
    @pl.when(core == 0)
    def _():
        own_ref[index] = first
        send_ref[index] = second

    @pl.when(core != 0)
    def _():
        own_ref[index] = second
        send_ref[index] = first


def mlp_kernel(sc, h2, dm, sm, wup, wdown, *rest, k):
    pieces, rest = rest[:6], rest[6:]
    if k:
        old_down, old_dh2 = rest[:2]
        rest = rest[2:]
    down, dh2, up_own, up_send, dn_own, dn_send, gub, ubuf, dbuf, sems = rest
    shard, core = sc[0], sc[1]
    step = pl.program_id(0)
    width = h2.shape[1]
    height = wup.shape[0]
    half, part = height // 2, wdown.shape[0] // 2
    take = slice(k * part, (k + 1) * part)
    blocks = []
    for j in range(2):
        mine = pl.ds(pl.multiple_of(shard * height, 16), height)
        pairs = []
        for h in range(2):
            at = pl.multiple_of((2 * ((shard >> 1) ^ j) + h) * width + k * part, 128)
            pairs.append(
                (wup.at[:, pl.ds(at, part)], ubuf.at[j, mine, pl.ds(h * part, part)])
            )
        if j == 0:
            at = pl.multiple_of((shard & 1) * part, 16)
            pairs.append((wdown.at[pl.ds(k * part, part), :], dbuf.at[0, pl.ds(at, part), :]))
        for side in range(2):
            which = core if side == 0 else 1 - core
            for m in range(1, 4):
                piece = pieces[side * 3 + m - 1]
                at = pl.multiple_of((shard ^ m) * height + which * half, 16)
                g = j ^ (m >> 1)
                pairs.append((piece.at[pl.ds(g * half, half), :], ubuf.at[j, pl.ds(at, half), :]))
                if m >> 1 == j:
                    at = ((shard ^ m) & 1) * part + which * (part // 2)
                    at = pl.multiple_of(at, 16)
                    pairs.append(
                        (
                            piece.at[pl.ds(2 * half, part // 2), :],
                            dbuf.at[j, pl.ds(at, part // 2), :],
                        )
                    )
        blocks.append(run_copies(pairs, sems, 12 * j))

    @pl.when(step == 0)
    def _():
        for c in blocks[0] + blocks[1]:
            c.start()
        for c in blocks[0]:
            c.wait()

    @pl.when(step == 1)
    def _():
        for c in blocks[1]:
            c.wait()

    uw, dw = ubuf[step], dbuf[step]
    x, g = h2[...], dm[...]
    pair = 2 * ((shard >> 1) ^ step)
    bias = jnp.concatenate([sm[pl.ds(UB + pair + h, 1), take] for h in range(2)], axis=1)
    u = dot(x, uw, 1, 0) + bias
    dact = dot(g, dw, 1, 1)
    cdf = 0.5 * (1.0 + lax.erf(u * np.float32(np.sqrt(0.5))))
    act = (u * cdf).astype(BF)
    slope = cdf + u * (jnp.exp(-0.5 * u * u) * np.float32(1.0 / np.sqrt(2.0 * np.pi)))
    du = (dact * slope).astype(BF)
    bsum = jnp.sum(du.astype(F32), axis=0, keepdims=True)
    gd = dot(act, g, 0, 0).astype(BF)
    for h in range(2):
        gub[h] = bsum[:, h * part : (h + 1) * part]
        for i in range(2):
            for n in range(2):
                span = slice(n * part, (n + 1) * part)
                at = h * part + i * half
                store_halves(
                    core,
                    dn_own,
                    dn_send,
                    (h ^ (shard & 1), 2 * i + n),
                    gd[at : at + half, span],
                    gd[at + part // 2 : at + part // 2 + half, span],
                )
    gu = dot(x, du, 0, 0).astype(BF)
    for m in range(4):
        at = m * height
        for h in range(2):
            span = slice(h * part, (h + 1) * part)
            store_halves(
                core,
                up_own,
                up_send,
                (shard ^ m, h),
                gu[at : at + half, span],
                gu[at + half : at + height, span],
            )
    new_down = dot(act, dw, 1, 0)
    new_dh2 = dot(du, uw, 1, 1)

    @pl.when(step == 0)
    def _():
        if k:
            down[...] = old_down[...] + new_down
            dh2[...] = old_dh2[...] + new_dh2
        else:
            down[...] = new_down
            dh2[...] = new_dh2

    @pl.when(step > 0)
    def _():
        down[...] += new_down
        dh2[...] += new_dh2


def mlp_part(sc, h2, dm, sm, wup, wdown, pieces, k, old):
    rows, width = h2.shape
    half, part = wup.shape[0] // 2, wdown.shape[0] // 2
    once = pl.Buffered(1)
    full = lambda a: pl.BlockSpec(a.shape, lambda j, sc: (0,) * a.ndim, pipeline_mode=once)
    whole = pl.BlockSpec((rows, width), lambda j, sc: (0, 0), pipeline_mode=once)
    by_up = pl.BlockSpec((4, 2, half, part), lambda j, sc: (0, (sc[0] >> 1) ^ j, 0, 0))
    by_down = pl.BlockSpec((2, 4, half, part), lambda j, sc: (j, 0, 0, 0))
    shares = SD((4, 4, half, part), BF)
    return pl.pallas_call(
        functools.partial(mlp_kernel, k=k),
        grid_spec=pltpu.PrefetchScalarGridSpec(
            num_scalar_prefetch=1,
            grid=(2,),
            in_specs=[VM] * 3 + [ANY] * 8 + [VM] * len(old),
            out_specs=[VM] * 2
            + [by_up] * 2
            + [by_down] * 2
            + [pl.BlockSpec((2, 1, part), lambda j, sc: ((sc[0] >> 1) ^ j, 0, 0))],
            scratch_shapes=[
                pltpu.VMEM((2, width, width), BF),
                pltpu.VMEM((2, width, width), BF),
                pltpu.SemaphoreType.DMA((24,)),
            ],
        ),
        out_shape=[SD((rows, width), F32)] * 2 + [shares] * 4 + [SD((4, 1, part), F32)],
        input_output_aliases={12: 0, 13: 1} if old else {},
        compiler_params=params(36),
        cost_estimate=cost(26),
        name="mlp%d" % k,
    )(sc, h2, dm, sm, wup, wdown, *pieces, *old)


def after_kernel(sc, down, dh2, mid, cot, keep, sm, o, dm, own, *rest, slots):
    pieces = rest[:6]
    out, dmid, do, g_own, g_send, gs, wbuf, sems = rest[6:]
    images, count, width = cot.shape
    every = pl.ds(0, width)
    height = own.shape[0]
    copies = run_copies(
        place_rows(wbuf, sc, (own, every), pieces, every, pl.ds(width, width), height), sems
    )
    for c in copies:
        c.start()
    e0 = dh2[...]
    xhat, rsq = normalized(mid[...])
    gs[...] = jnp.zeros_like(gs)
    gs[1:2, :] = jnp.sum(e0 * xhat, axis=0, keepdims=True)
    gs[2:3, :] = jnp.sum(e0, axis=0, keepdims=True)
    gs[3:4, :] = jnp.sum(dm[...].astype(F32), axis=0, keepdims=True)
    dmid[...] = norm_back(e0 * sm[G2 : G2 + 1, :], xhat, rsq)
    for i in range(images):
        sl = slice(i * slots, i * slots + count)
        dmid[sl, :] += cot[i].astype(F32) * keep[sl, :]
        out[i] = (keep[sl, :] * (mid[sl, :] + down[sl, :] + sm[DB : DB + 1, :])).astype(BF)
    low = dmid[...].astype(BF)
    gs[0:1, :] = jnp.sum(low.astype(F32), axis=0, keepdims=True)
    for c in copies:
        c.wait()
    do[...] = dot(low, wbuf[...], 1, 1).astype(BF)
    gw = dot(o[...], low, 0, 0).astype(BF)
    half, part = height // 2, width // 2
    for m in range(4):
        for j in range(2):
            cols = slice(j * part, (j + 1) * part)
            at = m * height
            store_halves(
                sc[1],
                g_own,
                g_send,
                (sc[0] ^ m, j),
                gw[at : at + half, cols],
                gw[at + half : at + height, cols],
            )


def after_mlp(sc, down, dh2, mid, cot, keep, sm, o, dm, own, pieces, slots):
    rows, width = o.shape
    half, part = own.shape[0] // 2, width // 2
    full = lambda a: pl.BlockSpec(a.shape, lambda j, sc: (0,) * a.ndim)
    whole = pl.BlockSpec((rows, width), lambda j, sc: (0, 0))
    share = pl.BlockSpec((4, 2, half, part), lambda j, sc: (0, 3, 0, 0))
    return pl.pallas_call(
        functools.partial(after_kernel, slots=slots),
        grid_spec=pltpu.PrefetchScalarGridSpec(
            num_scalar_prefetch=1,
            grid=(1,),
            in_specs=[VM] * 8 + [ANY] * 7,
            out_specs=[VM] * 3 + [share] * 2 + [VM],
            scratch_shapes=[pltpu.VMEM((width, width), BF), pltpu.SemaphoreType.DMA((7,))],
        ),
        out_shape=[SD(cot.shape, BF), SD((rows, width), F32), SD((rows, width), BF)]
        + [SD((4, 8, half, part), BF)] * 2
        + [SD((8, width), F32)],
        compiler_params=params(24),
        cost_estimate=cost(15),
        name="after_mlp",
    )(sc, down, dh2, mid, cot, keep, sm, o, dm, own, *pieces)


def project_grad_kernel(sc, h1, dx, old_own, old_send, g_own, g_send, gs, *, height):
    half, part = height // 2, dx.shape[1] // 2
    low = dx[...]
    gs[0] = jnp.broadcast_to(jnp.sum(low.astype(F32), axis=0, keepdims=True), gs.shape[1:])
    gw = dot(h1[...], low, 0, 0).astype(BF)
    for m in range(4):
        for j in range(2):
            cols = slice(j * part, (j + 1) * part)
            at = m * height
            store_halves(
                sc[1],
                g_own,
                g_send,
                (sc[0] ^ m, j),
                gw[at : at + half, cols],
                gw[at + half : at + height, cols],
            )


def project_grad(sc, h1, dx, g_own, g_send, height):
    rows, width = h1.shape
    half, part = height // 2, width // 2
    share = pl.BlockSpec((4, 2, half, part), lambda j, sc: (0, j, 0, 0))
    return pl.pallas_call(
        functools.partial(project_grad_kernel, height=height),
        grid_spec=pltpu.PrefetchScalarGridSpec(
            num_scalar_prefetch=1,
            grid=(3,),
            in_specs=[
                VM,
                pl.BlockSpec((rows, width), lambda j, sc: (0, j)),
                ANY,
                ANY,
            ],
            out_specs=[share, share, pl.BlockSpec((1, 8, width), lambda j, sc: (j, 0, 0))],
        ),
        out_shape=[SD((4, 8, half, part), BF)] * 2 + [SD((3, 8, width), F32)],
        input_output_aliases={3: 0, 4: 1},
        compiler_params=params(20),
        cost_estimate=cost(10),
        name="project_grad",
    )(sc, h1, dx, g_own, g_send)


def tokens_grad_kernel(sc, dx, tok, sm, dmid, ga, gp, gu0, gu1, own, *rest, slots):
    pp, pq = rest[:6], rest[6:12]
    out, gs, wbuf, acc, sems = rest[12:]
    images, count, width = tok.shape
    height = own.shape[0]
    two, third = pl.ds(0, 2 * width), pl.ds(2 * width, width)
    pairs = place_rows(wbuf, sc, (own, two), pp, two, two, height)
    pairs += place_rows(wbuf, sc, (own, third), pq, third, pl.ds(0, width), height)
    copies = run_copies(pairs, sems)
    for c in copies:
        c.start()
    gs[...] = jnp.zeros_like(gs)
    gs[OB : OB + 4, :] = ga[0:4, :]
    gs[QB : QB + 1, :] = gp[0, 0:1, :]
    gs[VB : VB + 1, :] = gp[2, 0:1, :]
    for b in range(4):
        gs[UB + b : UB + b + 1, : width // 2] = gu0[b]
        gs[UB + b : UB + b + 1, width // 2 :] = gu1[b]
    for c in copies:
        c.wait()
    acc[...] = dot(dx[...], wbuf[...], 1, 1)
    gain = jnp.zeros((1, width), F32)
    shift = jnp.zeros((1, width), F32)
    for i in range(images):
        sl = slice(i * slots, i * slots + count)
        e0 = acc[sl, :]
        xhat, rsq = normalized(tok[i].astype(F32))
        gain += jnp.sum(e0 * xhat, axis=0, keepdims=True)
        shift += jnp.sum(e0, axis=0, keepdims=True)
        out[i] = (dmid[sl, :] + norm_back(e0 * sm[G1 : G1 + 1, :], xhat, rsq)).astype(BF)
    gs[G1 : G1 + 1, :] = gain
    gs[B1 : B1 + 1, :] = shift


def tokens_grad(sc, dx, tok, sm, dmid, ga, gp, gu0, gu1, own, pieces, slots):
    rows, width = dmid.shape
    full = lambda a: pl.BlockSpec(a.shape, lambda j, sc: (0,) * a.ndim)
    operands = (dx, tok, sm, dmid, ga, gp, gu0, gu1)
    return pl.pallas_call(
        functools.partial(tokens_grad_kernel, slots=slots),
        grid_spec=pltpu.PrefetchScalarGridSpec(
            num_scalar_prefetch=1,
            grid=(1,),
            in_specs=[VM] * len(operands) + [ANY] * 13,
            out_specs=[VM] * 2,
            scratch_shapes=[
                pltpu.VMEM((width, 3 * width), BF),
                pltpu.VMEM((rows, width), F32),
                pltpu.SemaphoreType.DMA((14,)),
            ],
        ),
        out_shape=[SD(tok.shape, BF), SD((16, width), F32)],
        compiler_params=params(24),
        cost_estimate=cost(13),
        name="tokens_grad",
    )(sc, *operands, own, *pieces)


def lay_kernel(sc, *refs, kind):
    core, odd = sc[1], sc[2] % 2
    ins, (wide, tall) = refs[:-2], refs[-2:]
    half, part = ins[0].shape[1:]

    def put(k, side, first, second):
        which = core if side == 0 else 1 - core
        rows = pl.ds(pl.multiple_of(which * half, 8), half)
        if kind == "mlp":
            for b in range(4):
                wide[rows, pl.ds((2 * b + k) * part, part)] = first[b].astype(F32)
            for i in range(2):
                at = pl.multiple_of(which * 2 * half + (k * 4 + i) * half, 8)
                for j in range(2):
                    tall[pl.ds(at, half), pl.ds(j * part, part)] = second[2 * i + j].astype(F32)
        else:
            for n in range(4):
                wide[rows, pl.ds(n * part, part)] = first[n].astype(F32)
            for n in range(2):
                wide[rows, pl.ds((4 + n) * part, part)] = second[n].astype(F32)
                tall[rows, pl.ds(n * part, part)] = second[2 + n].astype(F32)

    for k in range(len(ins) // 4):
        kept, other, skept, sother = ins[4 * k : 4 * k + 4]

        @pl.when(odd == 0)
        def _(k=k, kept=kept, other=other, skept=skept, sother=sother):
            put(k, 0, kept, other)
            put(k, 1, skept, sother)

        @pl.when(odd != 0)
        def _(k=k, kept=kept, other=other, skept=skept, sother=sother):
            put(k, 0, other, kept)
            put(k, 1, sother, skept)


def lay_out(sc, finals, kind, shapes):
    full = lambda s: pl.BlockSpec(s, lambda j, sc: (0,) * len(s))
    flat = [a for group in finals for a in group]
    return pl.pallas_call(
        functools.partial(lay_kernel, kind=kind),
        grid_spec=pltpu.PrefetchScalarGridSpec(
            num_scalar_prefetch=1,
            grid=(1,),
            in_specs=[VM] * len(flat),
            out_specs=[VM] * 2,
        ),
        out_shape=[SD(s, F32) for s in shapes],
        compiler_params=params(8),
        cost_estimate=cost(4),
        name="lay_" + kind,
    )(sc, *flat)


def hops():
    def table(move):
        pairs = []
        for dp in range(8):
            for fs in range(4):
                z, core, shard = move(dp // 2, dp % 2, fs)
                pairs.append((dp * 4 + fs, (z * 2 + core) * 4 + shard))
        return pairs

    moves = {
        "sib": lambda z, c, f: (z, 1 - c, f),
        "x": lambda z, c, f: (z, c, f ^ 1),
        "y": lambda z, c, f: (z, c, f ^ 2),
        "xy": lambda z, c, f: (z, c, f ^ 3),
        "z1": lambda z, c, f: (z ^ 1, c, f),
        "z2": lambda z, c, f: (z ^ 2, c, f),
        "z3": lambda z, c, f: (z ^ 3, c, f),
    }
    tables = {name: table(move) for name, move in moves.items()}
    return lambda value, name: lax.ppermute(value, ("dp", "fsdp"), tables[name])


class Transfer:
    def __init__(self, stages):
        self.stages = stages
        self.flying = next(stages)
        self.result = None

    def step(self, landed):
        try:
            self.flying = self.stages.send(landed)
        except StopIteration as end:
            self.flying, self.result = (), end.value


def advance(held, *transfers):
    values = lax.optimization_barrier((held, tuple(t.flying for t in transfers)))
    for t, landed in zip(transfers, values[1]):
        t.step(landed)
    return values[0]


PLANE = ("x", "y", "xy")
LINE = ("z1", "z2", "z3")


def gather_stages(hop, own):
    far = yield tuple(hop(own, name) for name in PLANE)
    near = yield tuple(hop(a, "sib") for a in far)
    return tuple(far) + tuple(near)


def small_stages(hop, own):
    return (own,) + tuple((yield tuple(hop(own, name) for name in PLANE)))


def add(a, b):
    return (a.astype(F32) + b.astype(F32)).astype(BF)


def line_stages(hop, even, total):
    parts = total.shape[0] // 2
    keep = jnp.where(even, total[:parts], total[parts:])
    give = jnp.where(even, total[parts:], total[:parts]).astype(BF)
    (got,) = yield (hop(give, "z1"),)
    half = lax.optimization_barrier((keep + got.astype(F32)).astype(BF))
    (got,) = yield (hop(half, "z2"),)
    kept = add(half, got)
    other, skept = yield (hop(kept, "z1"), hop(kept, "sib"))
    (sother,) = yield (hop(other, "sib"),)
    return kept, other, skept, sother


def plane_stages(hop, even, chip):
    got = yield tuple(hop(chip(r).astype(BF), name) for r, name in enumerate(PLANE, 1))
    total = chip(0)
    for a in got:
        total = total + a.astype(F32)
    return (yield from line_stages(hop, even, total))


def ffn_stages(hop, even, up_own, up_send, dn_own, dn_send):
    up_got, dn_got = yield (hop(up_send, "sib"), hop(dn_send, "sib"))

    def chip(r):
        return jnp.concatenate(
            [
                up_own[r].astype(F32) + up_got[r].astype(F32),
                dn_own[r].astype(F32) + dn_got[r].astype(F32),
            ]
        )

    return (yield from plane_stages(hop, even, chip))


def attn_stages(hop, even, own, send):
    (got,) = yield (hop(send, "sib"),)
    chip = lambda r: own[r].astype(F32) + got[r].astype(F32)
    return (yield from plane_stages(hop, even, chip))


def sum_stages(hop, value):
    (got,) = yield (hop(value, "sib"),)
    value = value + got
    for names in (PLANE, LINE):
        one, two, three = yield tuple(hop(value, name) for name in names)
        value = (value + one) + (two + three)
    return value


def on_device_fast(
    tokens,
    mask,
    cotangent,
    ln1_gain,
    ln1_bias,
    w_qkv,
    qv_bias,
    w_out,
    out_bias,
    ln2_gain,
    ln2_bias,
    w_up,
    up_bias,
    w_down,
    down_bias,
):
    images, count, width = tokens.shape
    slots = -(-count // 8) * 8
    height = w_out.shape[0]
    half, part = height // 2, width // 2
    hop = hops()
    shard = lax.axis_index("fsdp")
    dp = lax.axis_index("dp")
    sc = jnp.stack([shard, dp % 2, dp // 2]).astype(jnp.int32)
    even = (dp // 2) % 2 == 0

    tie = lax.optimization_barrier
    small = (ln1_gain, ln1_bias, qv_bias, out_bias, ln2_gain, ln2_bias, down_bias, up_bias)
    top, bottom = pack_attn(sc, w_qkv, w_out, small)
    px, py, qx, qy = hop(top, "x"), hop(top, "y"), hop(bottom, "x"), hop(bottom, "y")
    own0, own1 = pack(sc, pack_ffn_kernel, 10, [(2 * height, width)] * 2, w_up, w_down)
    px, py, qx, qy, own0, own1 = tie((px, py, qx, qy, own0, own1))
    pfar, qfar = hop(px, "y"), hop(qy, "x")
    near = tuple(hop(a, "sib") for a in (px, py, qx, qy))
    pfar, qfar, near, own0, own1 = tie((pfar, qfar, near, own0, own1))
    spfar, sqfar = hop(pfar, "sib"), hop(qfar, "sib")
    ffn0 = Transfer(gather_stages(hop, own0))
    sc, spfar, sqfar = tie((sc, spfar, sqfar))
    pieces_p = (px, py, pfar, near[0], near[1], spfar)
    pieces_q = (qx, qy, qfar, near[2], near[3], sqfar)
    pieces = pieces_p + pieces_q

    keep = jnp.pad(mask.astype(F32), ((0, 0), (0, slots - count)))
    mask_row = keep.reshape(images, 1, slots)
    keep_col = keep.reshape(images * slots, 1)

    h1, qkv, sm = project(sc, tokens, w_qkv, top, pieces, slots)
    o = attend(qkv, mask_row, slots)
    o, own1 = tie((o, own1))
    ffn1 = Transfer(gather_stages(hop, own1))
    mid, h2, dm = middle_part(sc, tokens, o, sm, cotangent, keep_col, w_out, pieces_q, slots)
    h2 = advance(h2, ffn0)
    sc = advance(sc, ffn0)
    down, dh2, *shares, gu0 = mlp_part(sc, h2, dm, sm, w_up, w_down, ffn0.result, 0, ())
    down, dh2, *shares = advance((down, dh2, *shares), ffn1)
    m0 = Transfer(ffn_stages(hop, even, *shares))
    sc = advance(sc, ffn1, m0)
    down, dh2, *shares, gu1 = mlp_part(
        sc, h2, dm, sm, w_up, w_down, ffn1.result, 1, (down, dh2)
    )
    down, dh2, *shares = advance((down, dh2, *shares), m0)
    m1 = Transfer(ffn_stages(hop, even, *shares))
    layer_out, dmid, do, g_own, g_send, ga = after_mlp(
        sc, down, dh2, mid, cotangent, keep_col, sm, o, dm, w_out, pieces_q, slots
    )
    do = advance(do, m0, m1)
    dx = attend_back(qkv, do, keep_col, slots)
    dx = advance(dx, m0)
    g_own, g_send, gp = project_grad(sc, h1, dx, g_own, g_send, height)
    g_own, g_send, dx = advance((g_own, g_send, dx), m0, m1)
    attn = Transfer(attn_stages(hop, even, g_own, g_send))
    sc = advance(sc, attn)
    sc = advance(sc, m1)
    grad_tokens, gs = tokens_grad(
        sc, dx, tokens, sm, dmid, ga, gp, gu0, gu1, w_qkv, pieces, slots
    )
    gs = advance(gs, m0)
    total = Transfer(sum_stages(hop, gs))
    advance((), m1)
    advance((), attn, total)
    advance((), m1)
    advance((), attn, total)
    advance((), m1)
    ffn = lay_out(
        sc, (m0.result, m1.result), "mlp", ((height, 4 * width), (4 * height, width))
    )
    ffn = advance(ffn, attn, total)
    gs = total.result

    def mine(r, n=1):
        return lax.dynamic_slice(gs[r : r + n].reshape(-1), (shard * (n * height),), (n * height,))

    rows = tuple(mine(r) for r in (G1, B1, OB, G2, B2, DB)) + (mine(QB, 2), mine(UB, 4))
    while attn.flying:
        ffn, rows = advance((ffn, rows), attn)
    g1, b1, ob, g2, b2, db, qvb, ub = rows
    grad_w_up, grad_w_down = ffn
    grad_w_qkv, grad_w_out = lay_out(
        sc, (attn.result,), "attn", ((height, 3 * width), (height, width))
    )
    return (
        layer_out,
        grad_tokens,
        g1,
        b1,
        grad_w_qkv,
        qvb,
        grad_w_out,
        ob,
        g2,
        b2,
        grad_w_up,
        ub,
        grad_w_down,
        db,
    )


def norm(values, gain, shift):
    mean_value = jnp.mean(values, axis=-1, keepdims=True)
    centred = values - mean_value
    variance = jnp.mean(centred * centred, axis=-1, keepdims=True)
    return centred * lax.rsqrt(variance + EPS) * gain + shift


def gelu_exact(values):
    return jax.nn.gelu(values, approximate=False)


def score_block(query, key_part, valid):
    scores = jnp.einsum(
        "iqhe,ikhe->ihqk", query, key_part, preferred_element_type=jnp.float32
    ) * HD ** (-0.5)
    return jnp.where(valid, scores, -1e30)


def arrange(grad, groups, copies):
    shaped = grad.reshape((groups, copies, grad.shape[0] // (groups * copies)) + grad.shape[1:])
    return jnp.swapaxes(shaped, 0, 1).reshape(grad.shape)


def reduce_six(grad_one, grad_two, grad_three, grad_four, grad_five, grad_six):
    groups = lax.axis_size("fsdp")
    copies = lax.axis_size("dp")
    pieces = (
        lax.psum_scatter(
            arrange(grad_one, groups, copies), ("dp", "fsdp"), scatter_dimension=0, tiled=True
        ),
        lax.psum_scatter(
            arrange(grad_two, groups, copies), ("dp", "fsdp"), scatter_dimension=0, tiled=True
        ),
        lax.psum_scatter(
            arrange(grad_three, groups, copies), ("dp", "fsdp"), scatter_dimension=0, tiled=True
        ),
        lax.psum_scatter(
            arrange(grad_four, groups, copies), ("dp", "fsdp"), scatter_dimension=0, tiled=True
        ),
        lax.psum_scatter(
            arrange(grad_five, groups, copies), ("dp", "fsdp"), scatter_dimension=0, tiled=True
        ),
        lax.psum_scatter(
            arrange(grad_six, groups, copies), ("dp", "fsdp"), scatter_dimension=0, tiled=True
        ),
    )
    return (
        lax.all_gather(pieces[0].astype(jnp.bfloat16), "dp", axis=0, tiled=True).astype(
            jnp.float32
        ),
        lax.all_gather(pieces[1].astype(jnp.bfloat16), "dp", axis=0, tiled=True).astype(
            jnp.float32
        ),
        lax.all_gather(pieces[2].astype(jnp.bfloat16), "dp", axis=0, tiled=True).astype(
            jnp.float32
        ),
        lax.all_gather(pieces[3].astype(jnp.bfloat16), "dp", axis=0, tiled=True).astype(
            jnp.float32
        ),
        lax.all_gather(pieces[4].astype(jnp.bfloat16), "dp", axis=0, tiled=True).astype(
            jnp.float32
        ),
        lax.all_gather(pieces[5].astype(jnp.bfloat16), "dp", axis=0, tiled=True).astype(
            jnp.float32
        ),
    )


def on_device(
    tokens,
    mask,
    cotangent,
    ln1_gain,
    ln1_bias,
    w_qkv,
    qv_bias,
    w_out,
    out_bias,
    ln2_gain,
    ln2_bias,
    w_up,
    up_bias,
    w_down,
    down_bias,
):
    image_count, slot_count, width = tokens.shape
    row_count = image_count * slot_count
    heads = width // HD
    scale = HD ** (-0.5)
    attn_full = (
        lax.all_gather(ln1_gain, "fsdp", axis=0, tiled=True),
        lax.all_gather(ln1_bias, "fsdp", axis=0, tiled=True),
        lax.all_gather(w_qkv, "fsdp", axis=0, tiled=True),
        lax.all_gather(qv_bias, "fsdp", axis=0, tiled=True),
        lax.all_gather(w_out, "fsdp", axis=0, tiled=True),
        lax.all_gather(out_bias, "fsdp", axis=0, tiled=True),
    )
    mlp_full = (
        lax.all_gather(ln2_gain, "fsdp", axis=0, tiled=True),
        lax.all_gather(ln2_bias, "fsdp", axis=0, tiled=True),
        lax.all_gather(w_up, "fsdp", axis=0, tiled=True),
        lax.all_gather(up_bias, "fsdp", axis=0, tiled=True),
        lax.all_gather(w_down, "fsdp", axis=0, tiled=True),
        lax.all_gather(down_bias, "fsdp", axis=0, tiled=True),
    )
    gain_one, shift_one, qkv_weight, qkv_shift, out_weight, out_shift = attn_full
    gain_two, shift_two, up_weight, up_shift, down_weight, down_shift = mlp_full
    keep = mask.astype(jnp.float32)
    valid = (keep > 0.5)[:, None, None, :]
    keep_rows = keep.reshape(row_count, 1)
    inputs = tokens.astype(jnp.float32).reshape(row_count, width)
    normed_one, norm_one_back = jax.vjp(
        norm, inputs, gain_one.astype(jnp.float32), shift_one.astype(jnp.float32)
    )
    normed_low = normed_one.astype(jnp.bfloat16)
    qv_float = qkv_shift.astype(jnp.float32)
    full_bias = jnp.concatenate(
        [qv_float[:width], jnp.zeros((width,), jnp.float32), qv_float[width:]]
    )
    projected = (
        jnp.dot(normed_low, qkv_weight, preferred_element_type=jnp.float32) + full_bias
    ).astype(jnp.bfloat16)
    query = projected[:, :width].reshape(image_count, slot_count, heads, HD)
    key_part = projected[:, width : 2 * width].reshape(image_count, slot_count, heads, HD)
    value = projected[:, 2 * width :].reshape(image_count, slot_count, heads, HD)
    scores = score_block(query, key_part, valid)
    top = jnp.max(scores, axis=-1, keepdims=True)
    lse = top + jnp.log(jnp.sum(jnp.exp(scores - top), axis=-1, keepdims=True))
    probs_low = jnp.exp(scores - lse).astype(jnp.bfloat16)
    mixed = jnp.einsum("ihqk,ikhe->iqhe", probs_low, value, preferred_element_type=jnp.float32)
    mixed = mixed.reshape(row_count, width).astype(jnp.bfloat16)
    middle = (
        inputs
        + jnp.dot(mixed, out_weight, preferred_element_type=jnp.float32)
        + out_shift.astype(jnp.float32)
    )
    normed_two, norm_two_back = jax.vjp(
        norm, middle, gain_two.astype(jnp.float32), shift_two.astype(jnp.float32)
    )
    normed_two_low = normed_two.astype(jnp.bfloat16)
    upward = jnp.dot(
        normed_two_low, up_weight, preferred_element_type=jnp.float32
    ) + up_shift.astype(jnp.float32)
    active, gelu_back = jax.vjp(gelu_exact, upward)
    active_low = active.astype(jnp.bfloat16)
    downward = jnp.dot(
        active_low, down_weight, preferred_element_type=jnp.float32
    ) + down_shift.astype(jnp.float32)
    layer_out = (
        (keep_rows * (middle + downward))
        .astype(jnp.bfloat16)
        .reshape(image_count, slot_count, width)
    )
    mlp_back = (
        lax.all_gather(ln2_gain, "fsdp", axis=0, tiled=True),
        lax.all_gather(ln2_bias, "fsdp", axis=0, tiled=True),
        lax.all_gather(w_up, "fsdp", axis=0, tiled=True),
        lax.all_gather(up_bias, "fsdp", axis=0, tiled=True),
        lax.all_gather(w_down, "fsdp", axis=0, tiled=True),
        lax.all_gather(down_bias, "fsdp", axis=0, tiled=True),
    )
    up_back = mlp_back[2]
    down_back = mlp_back[4]
    grad_rows = cotangent.astype(jnp.float32).reshape(row_count, width) * keep_rows
    grad_down_low = grad_rows.astype(jnp.bfloat16)
    grad_w_down = jnp.einsum(
        "rf,rd->fd", active_low, grad_down_low, preferred_element_type=jnp.float32
    )
    grad_down_bias = jnp.sum(grad_down_low, axis=0, dtype=jnp.float32)
    grad_active = jnp.einsum(
        "rd,fd->rf", grad_down_low, down_back, preferred_element_type=jnp.float32
    )
    grad_up_low = gelu_back(grad_active)[0].astype(jnp.bfloat16)
    grad_w_up = jnp.einsum(
        "rd,rf->df", normed_two_low, grad_up_low, preferred_element_type=jnp.float32
    )
    grad_up_bias = jnp.sum(grad_up_low, axis=0, dtype=jnp.float32)
    grad_normed_two = jnp.einsum(
        "rf,df->rd", grad_up_low, up_back, preferred_element_type=jnp.float32
    )
    grad_mid_norm, grad_ln2_gain, grad_ln2_bias = norm_two_back(grad_normed_two)
    grad_middle = grad_rows + grad_mid_norm
    mlp_grads = reduce_six(
        grad_ln2_gain, grad_ln2_bias, grad_w_up, grad_up_bias, grad_w_down, grad_down_bias
    )
    attn_back = (
        lax.all_gather(ln1_gain, "fsdp", axis=0, tiled=True),
        lax.all_gather(ln1_bias, "fsdp", axis=0, tiled=True),
        lax.all_gather(w_qkv, "fsdp", axis=0, tiled=True),
        lax.all_gather(qv_bias, "fsdp", axis=0, tiled=True),
        lax.all_gather(w_out, "fsdp", axis=0, tiled=True),
        lax.all_gather(out_bias, "fsdp", axis=0, tiled=True),
    )
    qkv_back = attn_back[2]
    out_back = attn_back[4]
    grad_attn_low = grad_middle.astype(jnp.bfloat16)
    grad_w_out = jnp.einsum("rd,re->de", mixed, grad_attn_low, preferred_element_type=jnp.float32)
    grad_out_bias = jnp.sum(grad_attn_low, axis=0, dtype=jnp.float32)
    grad_mixed = jnp.einsum(
        "re,de->rd", grad_attn_low, out_back, preferred_element_type=jnp.float32
    )
    grad_mixed = grad_mixed.astype(jnp.bfloat16).reshape(image_count, slot_count, heads, HD)
    probs = jnp.exp(score_block(query, key_part, valid) - lse)
    probs_again = probs.astype(jnp.bfloat16)
    grad_value = jnp.einsum(
        "ihqk,iqhe->ikhe", probs_again, grad_mixed, preferred_element_type=jnp.float32
    )
    grad_probs = jnp.einsum(
        "iqhe,ikhe->ihqk", grad_mixed, value, preferred_element_type=jnp.float32
    )
    inner = jnp.sum(grad_probs * probs, axis=-1, keepdims=True)
    grad_scores = (probs * (grad_probs - inner)).astype(jnp.bfloat16)
    grad_query = (
        jnp.einsum("ihqk,ikhe->iqhe", grad_scores, key_part, preferred_element_type=jnp.float32)
        * scale
    )
    grad_key = (
        jnp.einsum("ihqk,iqhe->ikhe", grad_scores, query, preferred_element_type=jnp.float32)
        * scale
    )
    grad_projected = jnp.concatenate(
        [
            grad_query.reshape(row_count, width),
            grad_key.reshape(row_count, width),
            grad_value.reshape(row_count, width),
        ],
        axis=1,
    ).astype(jnp.bfloat16)
    grad_w_qkv = jnp.einsum(
        "rd,re->de", normed_low, grad_projected, preferred_element_type=jnp.float32
    )
    grad_qv_bias = jnp.concatenate(
        [
            jnp.sum(grad_projected[:, :width], axis=0, dtype=jnp.float32),
            jnp.sum(grad_projected[:, 2 * width :], axis=0, dtype=jnp.float32),
        ]
    )
    grad_normed_one = jnp.einsum(
        "re,de->rd", grad_projected, qkv_back, preferred_element_type=jnp.float32
    )
    grad_in_norm, grad_ln1_gain, grad_ln1_bias = norm_one_back(grad_normed_one)
    grad_tokens = (
        (grad_middle + grad_in_norm).astype(jnp.bfloat16).reshape(image_count, slot_count, width)
    )
    attn_grads = reduce_six(
        grad_ln1_gain, grad_ln1_bias, grad_w_qkv, grad_qv_bias, grad_w_out, grad_out_bias
    )
    return (
        layer_out,
        grad_tokens,
        attn_grads[0],
        attn_grads[1],
        attn_grads[2],
        attn_grads[3],
        attn_grads[4],
        attn_grads[5],
        mlp_grads[0],
        mlp_grads[1],
        mlp_grads[2],
        mlp_grads[3],
        mlp_grads[4],
        mlp_grads[5],
    )


def solution(mesh):
    in_specs = (
        P(("dp", "fsdp"), None, None),
        P(("dp", "fsdp"), None),
        P(("dp", "fsdp"), None, None),
        P("fsdp"),
        P("fsdp"),
        P("fsdp", None),
        P("fsdp"),
        P("fsdp", None),
        P("fsdp"),
        P("fsdp"),
        P("fsdp"),
        P("fsdp", None),
        P("fsdp"),
        P("fsdp", None),
        P("fsdp"),
    )
    out_specs = (
        P(("dp", "fsdp"), None, None),
        P(("dp", "fsdp"), None, None),
        P("fsdp"),
        P("fsdp"),
        P("fsdp", None),
        P("fsdp"),
        P("fsdp", None),
        P("fsdp"),
        P("fsdp"),
        P("fsdp"),
        P("fsdp", None),
        P("fsdp"),
        P("fsdp", None),
        P("fsdp"),
    )
    fast = dict(mesh.shape) == {"dp": 8, "fsdp": 4}
    return jax.shard_map(
        on_device_fast if fast else on_device, mesh=mesh, in_specs=in_specs, out_specs=out_specs, check_vma=False
    )
```

```python
import functools

import jax
import jax.numpy as jnp
import numpy as np
from jax import lax
from jax.experimental import pallas as pl
from jax.experimental.pallas import tpu as pltpu
from jax.sharding import PartitionSpec as P

HD = 64
EPS = 1e-06
F32 = jnp.float32
BF = jnp.bfloat16
MB = 2**20
SCORE_SCALE = np.float32(np.log2(np.e) * HD ** (-0.5))
MASKED = np.float32(-1e30)
SD = jax.ShapeDtypeStruct
ANY = pl.BlockSpec(memory_space=pl.ANY)
VM = pl.BlockSpec(memory_space=pltpu.VMEM)


def dot(a, b, ca, cb):
    return lax.dot_general(a, b, (((ca,), (cb,)), ((), ())), preferred_element_type=F32)


def params(mb=58):
    return pltpu.CompilerParams(vmem_limit_bytes=mb * MB)


def cost(micros):
    return pl.CostEstimate(flops=int(micros * 1.15e9), bytes_accessed=0, transcendentals=0)


def normalized(values):
    mean = jnp.mean(values, axis=-1, keepdims=True)
    centred = values - mean
    rsq = lax.rsqrt(jnp.mean(centred * centred, axis=-1, keepdims=True) + EPS)
    return centred * rsq, rsq


def norm_back(e, xhat, rsq):
    return rsq * (
        e
        - jnp.mean(e, axis=-1, keepdims=True)
        - xhat * jnp.mean(e * xhat, axis=-1, keepdims=True)
    )


def run_copies(pairs, sems, base=0):
    copies = [
        pltpu.make_async_copy(src, dst, sems.at[base + n]) for n, (src, dst) in enumerate(pairs)
    ]
    return copies


PACK_MB = 54

G1, B1, QB, VB, OB, G2, B2, DB, UB = range(9)


def all_copies(pairs, sems):
    copies = run_copies(pairs, sems)
    for c in copies:
        c.start()
    for c in copies:
        c.wait()


def pack_attn_kernel(sc, wqkv, wout, *rest):
    small, (top, bottom, table, sems) = rest[:8], rest[8:]
    height, width = wout.shape
    half = height // 2
    rows = pl.ds(pl.multiple_of(sc[1] * half, 16), half)
    copies = run_copies(
        [
            (wqkv.at[rows, pl.ds(0, 2 * width)], top.at[pl.ds(0, half), :]),
            (wqkv.at[rows, pl.ds(2 * width, width)], bottom.at[:, pl.ds(0, width)]),
            (wout.at[rows, :], bottom.at[:, pl.ds(width, width)]),
        ],
        sems,
    )
    for c in copies:
        c.start()
    table[...] = jnp.zeros_like(table)
    row = 0
    for ref in small:
        values = ref[...].astype(F32)
        for n in range(ref.shape[0] // height):
            table[row : row + 1, :height] = values[n * height : (n + 1) * height].reshape(1, height)
            row += 1
    top[half:, : table.shape[1]] = table[...].astype(BF)
    for c in copies:
        c.wait()


def pack_attn(sc, wqkv, wout, small):
    height, width = wout.shape
    lanes = -(-height // 128) * 128
    return pl.pallas_call(
        pack_attn_kernel,
        grid_spec=pltpu.PrefetchScalarGridSpec(
            num_scalar_prefetch=1,
            in_specs=[ANY] * 2 + [VM] * 8,
            out_specs=[VM] * 2,
            scratch_shapes=[pltpu.VMEM((16, lanes), F32), pltpu.SemaphoreType.DMA((3,))],
        ),
        out_shape=[SD((height // 2 + 16, 2 * width), BF), SD((height // 2, 2 * width), BF)],
        compiler_params=params(PACK_MB),
        name="pack_attn",
    )(sc, wqkv, wout, *small)


def pack_ffn_kernel(sc, wup, wdown, ffn0, ffn1, sems):
    width = wdown.shape[1]
    half, part = wup.shape[0] // 2, wdown.shape[0] // 2
    rows = pl.ds(pl.multiple_of(sc[1] * half, 16), half)
    pairs = []
    for k, ffn in enumerate((ffn0, ffn1)):
        for g in range(2):
            for h in range(2):
                block = 2 * ((sc[0] >> 1) ^ g) + h
                at = pl.multiple_of(block * width + k * part, 128)
                pairs.append(
                    (
                        wup.at[rows, pl.ds(at, part)],
                        ffn.at[pl.ds(g * half, half), pl.ds(h * part, part)],
                    )
                )
        at = pl.multiple_of(k * part + sc[1] * (part // 2), 16)
        pairs.append((wdown.at[pl.ds(at, part // 2), :], ffn.at[pl.ds(2 * half, part // 2), :]))
    all_copies(pairs, sems)


def pack(sc, kernel, copies, shapes, *weights):
    return pl.pallas_call(
        kernel,
        grid_spec=pltpu.PrefetchScalarGridSpec(
            num_scalar_prefetch=1,
            in_specs=[ANY] * len(weights),
            out_specs=[ANY] * len(shapes),
            scratch_shapes=[pltpu.SemaphoreType.DMA((copies,))],
        ),
        out_shape=[SD(shape, BF) for shape in shapes],
        compiler_params=params(2),
        name="pack",
    )(sc, *weights)


def place_rows(dst, sc, own, pieces, cols, src_cols, height, base=0):
    half = height // 2
    shard, core = sc[0], sc[1]
    pairs = []
    if own is not None:
        src, take = own
        pairs.append((src.at[:, take], dst.at[pl.ds(pl.multiple_of(shard * height, 16), height), cols]))
    for side in range(2):
        which = core if side == 0 else 1 - core
        for r in range(1, 4):
            at = pl.multiple_of((shard ^ r) * height + which * half, 16)
            pairs.append(
                (
                    pieces[side * 3 + r - 1].at[pl.ds(base * half, half), src_cols],
                    dst.at[pl.ds(at, half), cols],
                )
            )
    return pairs


def fill_small(sc, pieces, sm, height):
    shard = sc[0]
    vals = [pieces[r].astype(F32) for r in range(4)]

    def of(j):
        got = vals[3]
        for r in range(3):
            got = jnp.where(shard == (j ^ r), vals[r], got)
        return got[:, :height]

    by = [of(j) for j in range(4)]
    sm[...] = jnp.zeros_like(sm)
    for j in range(4):
        cols = slice(j * height, (j + 1) * height)
        sm[G1 : B1 + 1, cols] = by[j][0:2]
        sm[OB : DB + 1, cols] = by[j][4:8]
        for n in range(2):
            at = (2 * j + n) % 4 * height
            row = QB if j < 2 else VB
            sm[row : row + 1, at : at + height] = by[j][2 + n : 3 + n]
        for n in range(4):
            sm[UB + j : UB + j + 1, n * height : (n + 1) * height] = by[j][8 + n : 9 + n]


def project_kernel(sc, tok, own, packed, *rest, slots):
    pp, pq = rest[:6], rest[6:12]
    h1, qkv, sm, wbuf, small, sems = rest[12:]
    images, count, width = tok.shape
    height = own.shape[0]
    step = pl.program_id(0)
    two = pl.ds(0, 2 * width)
    third = pl.ds(2 * width, width)
    first = run_copies(place_rows(wbuf, sc, (own, two), pp, two, two, height), sems)
    last = run_copies(
        place_rows(wbuf, sc, (own, third), pq, third, pl.ds(0, width), height),
        sems,
        len(first),
    )

    corner = (pl.ds(height // 2, 16), pl.ds(0, small.shape[2]))
    table = run_copies(
        [
            (ref.at[corner[0], corner[1]], small.at[r])
            for r, ref in enumerate((packed,) + pp[:3])
        ],
        sems,
        len(first) + len(last),
    )

    @pl.when(step == 0)
    def _():
        for c in table + first + last:
            c.start()
        for c in table:
            c.wait()
        fill_small(sc, small, sm, height)
        for i in range(images):
            xhat, _ = normalized(tok[i].astype(F32))
            low = (xhat * sm[G1 : G1 + 1, :] + sm[B1 : B1 + 1, :]).astype(BF)
            tail = count // 8 * 8
            h1[i * slots + tail : (i + 1) * slots, :] = jnp.zeros((slots - tail, width), BF)
            h1[i * slots : i * slots + count, :] = low
        for c in first:
            c.wait()

    @pl.when(step == 2)
    def _():
        for c in last:
            c.wait()

    row = jnp.where(step == 0, sm[QB : QB + 1, :], sm[VB : VB + 1, :])
    row = jnp.where(step == 1, jnp.zeros_like(row), row)
    weight = wbuf[:, pl.ds(pl.multiple_of(step * width, 128), width)]
    qkv[...] = (dot(h1[...], weight, 1, 0) + row).astype(BF)


def project(sc, tok, own, packed, pieces, slots):
    images, _, width = tok.shape
    rows = images * slots
    full = lambda *s: pl.BlockSpec(s, lambda j, sc: (0,) * len(s))
    return pl.pallas_call(
        functools.partial(project_kernel, slots=slots),
        grid_spec=pltpu.PrefetchScalarGridSpec(
            num_scalar_prefetch=1,
            grid=(3,),
            in_specs=[VM] + [ANY] * 14,
            out_specs=[
                VM,
                pl.BlockSpec((rows, width), lambda j, sc: (0, j)),
                VM,
            ],
            scratch_shapes=[
                pltpu.VMEM((width, 3 * width), BF),
                pltpu.VMEM((4, 16, -(-own.shape[0] // 128) * 128), BF),
                pltpu.SemaphoreType.DMA((18,)),
            ],
        ),
        out_shape=[SD((rows, width), BF), SD((rows, 3 * width), BF), SD((16, width), F32)],
        compiler_params=params(54),
        cost_estimate=cost(10),
        name="project",
    )(sc, tok, own, packed, *pieces)


def head_lanes():
    return lax.broadcasted_iota(jnp.int32, (1, 2 * HD), 1) < HD


def attend_kernel(q, k, v, mask, o, *, pairs):
    low_half = head_lanes()
    keep = mask[0] > 0
    zero = jnp.zeros((), BF)
    for p in range(pairs):
        sl = slice(p * 2 * HD, (p + 1) * 2 * HD)
        qp, kp, vp = q[:, sl], k[:, sl], v[:, sl]
        outs = []
        for a in range(2):
            mine = low_half if a == 0 else jnp.logical_not(low_half)
            s = dot(jnp.where(mine, qp, zero), kp, 1, 1)
            s = jnp.where(keep, s * SCORE_SCALE, MASKED)
            e = jnp.exp2(s - jnp.max(s, axis=-1, keepdims=True))
            prob = (e * (1.0 / jnp.sum(e, axis=-1, keepdims=True))).astype(BF)
            outs.append(dot(prob, jnp.where(mine, vp, zero), 1, 0))
        o[:, sl] = (outs[0] + outs[1]).astype(BF)


def attend(qkv, mask_row, slots):
    rows, three = qkv.shape
    width, images = three // 3, rows // slots
    block = lambda n: pl.BlockSpec((slots, width), lambda i: (i, n))
    return pl.pallas_call(
        functools.partial(attend_kernel, pairs=width // (2 * HD)),
        grid=(images,),
        in_specs=[block(0), block(1), block(2), pl.BlockSpec((1, 1, slots), lambda i: (i, 0, 0))],
        out_specs=block(0),
        out_shape=SD((rows, width), BF),
        compiler_params=params(40),
        cost_estimate=cost(11),
        name="attend",
    )(qkv, qkv, qkv, mask_row)


def attend_back_kernel(q, k, v, do, mask, dx, *, pairs):
    low_half = head_lanes()
    keep = mask[...] > 0
    zero = jnp.zeros((), BF)
    scale = np.float32(HD ** (-0.5))
    wide = pairs * 2 * HD
    for p in range(pairs):
        sl = slice(p * 2 * HD, (p + 1) * 2 * HD)
        qp, kp, vp, dop = q[:, sl], k[:, sl], v[:, sl], do[:, sl]
        gq, gk, gv = [], [], []
        for a in range(2):
            mine = low_half if a == 0 else jnp.logical_not(low_half)
            qm, km, dm = (jnp.where(mine, t, zero) for t in (qp, kp, dop))
            s = dot(km, qp, 1, 1)
            s = jnp.where(keep, s * SCORE_SCALE, MASKED)
            e = jnp.exp2(s - jnp.max(s, axis=0, keepdims=True))
            prob = e * (1.0 / jnp.sum(e, axis=0, keepdims=True))
            gv.append(dot(prob.astype(BF), dm, 1, 0))
            weighed = prob * dot(vp, dm, 1, 1)
            inner = jnp.sum(weighed, axis=0, keepdims=True)
            ds = (weighed - prob * inner).astype(BF)
            gk.append(dot(ds, qm, 1, 0))
            gq.append(dot(ds, km, 0, 0))
        at = p * 2 * HD
        dx[:, at : at + 2 * HD] = ((gq[0] + gq[1]) * scale).astype(BF)
        dx[:, wide + at : wide + at + 2 * HD] = ((gk[0] + gk[1]) * scale).astype(BF)
        dx[:, 2 * wide + at : 2 * wide + at + 2 * HD] = (gv[0] + gv[1]).astype(BF)


def attend_back(qkv, do, mask_col, slots):
    rows, three = qkv.shape
    width, images = three // 3, rows // slots
    block = lambda n: pl.BlockSpec((slots, width), lambda i: (i, n))
    return pl.pallas_call(
        functools.partial(attend_back_kernel, pairs=width // (2 * HD)),
        grid=(images,),
        in_specs=[block(0), block(1), block(2), block(0), pl.BlockSpec((slots, 1), lambda i: (i, 0))],
        out_specs=pl.BlockSpec((slots, 3 * width), lambda i: (i, 0)),
        out_shape=SD((rows, 3 * width), BF),
        compiler_params=params(16),
        cost_estimate=cost(20),
        name="attend_back",
    )(qkv, qkv, qkv, do, mask_col)


def middle_kernel(sc, tok, o, sm, cot, keep, own, *rest, slots):
    pieces = rest[:6]
    mid, h2, dm, wbuf, sems = rest[6:]
    images, count, width = tok.shape
    every = pl.ds(0, width)
    copies = run_copies(
        place_rows(wbuf, sc, (own, every), pieces, every, pl.ds(width, width), own.shape[0]),
        sems,
    )
    for c in copies:
        c.start()
    tail = count // 8 * 8
    for i in range(images):
        sl = slice(i * slots, i * slots + count)
        dm[i * slots + tail : (i + 1) * slots, :] = jnp.zeros((slots - tail, width), BF)
        dm[sl, :] = (cot[i].astype(F32) * keep[sl, :]).astype(BF)
    for c in copies:
        c.wait()
    mid[...] = dot(o[...], wbuf[...], 1, 0) + sm[OB : OB + 1, :]
    for i in range(images):
        sl = slice(i * slots, i * slots + count)
        mid[sl, :] += tok[i].astype(F32)
    xhat, _ = normalized(mid[...])
    h2[...] = (xhat * sm[G2 : G2 + 1, :] + sm[B2 : B2 + 1, :]).astype(BF)


def middle_part(sc, tok, o, sm, cot, keep, own, pieces, slots):
    rows, width = o.shape
    full = lambda a: pl.BlockSpec(a.shape, lambda j, sc: (0,) * a.ndim)
    whole = pl.BlockSpec((rows, width), lambda j, sc: (0, 0))
    return pl.pallas_call(
        functools.partial(middle_kernel, slots=slots),
        grid_spec=pltpu.PrefetchScalarGridSpec(
            num_scalar_prefetch=1,
            grid=(1,),
            in_specs=[VM] * 5 + [ANY] * 7,
            out_specs=[VM] * 3,
            scratch_shapes=[pltpu.VMEM((width, width), BF), pltpu.SemaphoreType.DMA((7,))],
        ),
        out_shape=[SD((rows, width), F32), SD((rows, width), BF), SD((rows, width), BF)],
        compiler_params=params(16),
        cost_estimate=cost(9),
        name="middle",
    )(sc, tok, o, sm, cot, keep, own, *pieces)


def store_halves(core, own_ref, send_ref, index, first, second):
    @pl.when(core == 0)
    def _():
        own_ref[index] = first
        send_ref[index] = second

    @pl.when(core != 0)
    def _():
        own_ref[index] = second
        send_ref[index] = first


def mlp_kernel(sc, h2, dm, sm, wup, wdown, *rest, k):
    pieces, rest = rest[:6], rest[6:]
    if k:
        old_down, old_dh2 = rest[:2]
        rest = rest[2:]
    down, dh2, up_own, up_send, dn_own, dn_send, gub, ubuf, dbuf, sems = rest
    shard, core = sc[0], sc[1]
    step = pl.program_id(0)
    width = h2.shape[1]
    height = wup.shape[0]
    half, part = height // 2, wdown.shape[0] // 2
    take = slice(k * part, (k + 1) * part)
    blocks = []
    for j in range(2):
        mine = pl.ds(pl.multiple_of(shard * height, 16), height)
        pairs = []
        for h in range(2):
            at = pl.multiple_of((2 * ((shard >> 1) ^ j) + h) * width + k * part, 128)
            pairs.append(
                (wup.at[:, pl.ds(at, part)], ubuf.at[j, mine, pl.ds(h * part, part)])
            )
        if j == 0:
            at = pl.multiple_of((shard & 1) * part, 16)
            pairs.append((wdown.at[pl.ds(k * part, part), :], dbuf.at[0, pl.ds(at, part), :]))
        for side in range(2):
            which = core if side == 0 else 1 - core
            for m in range(1, 4):
                piece = pieces[side * 3 + m - 1]
                at = pl.multiple_of((shard ^ m) * height + which * half, 16)
                g = j ^ (m >> 1)
                pairs.append((piece.at[pl.ds(g * half, half), :], ubuf.at[j, pl.ds(at, half), :]))
                if m >> 1 == j:
                    at = ((shard ^ m) & 1) * part + which * (part // 2)
                    at = pl.multiple_of(at, 16)
                    pairs.append(
                        (
                            piece.at[pl.ds(2 * half, part // 2), :],
                            dbuf.at[j, pl.ds(at, part // 2), :],
                        )
                    )
        blocks.append(run_copies(pairs, sems, 12 * j))

    @pl.when(step == 0)
    def _():
        for c in blocks[0] + blocks[1]:
            c.start()
        for c in blocks[0]:
            c.wait()

    @pl.when(step == 1)
    def _():
        for c in blocks[1]:
            c.wait()

    uw, dw = ubuf[step], dbuf[step]
    x, g = h2[...], dm[...]
    pair = 2 * ((shard >> 1) ^ step)
    bias = jnp.concatenate([sm[pl.ds(UB + pair + h, 1), take] for h in range(2)], axis=1)
    u = dot(x, uw, 1, 0) + bias
    dact = dot(g, dw, 1, 1)
    cdf = 0.5 * (1.0 + lax.erf(u * np.float32(np.sqrt(0.5))))
    act = (u * cdf).astype(BF)
    slope = cdf + u * (jnp.exp(-0.5 * u * u) * np.float32(1.0 / np.sqrt(2.0 * np.pi)))
    du = (dact * slope).astype(BF)
    bsum = jnp.sum(du.astype(F32), axis=0, keepdims=True)
    gd = dot(act, g, 0, 0).astype(BF)
    for h in range(2):
        gub[h] = bsum[:, h * part : (h + 1) * part]
        for i in range(2):
            for n in range(2):
                span = slice(n * part, (n + 1) * part)
                at = h * part + i * half
                store_halves(
                    core,
                    dn_own,
                    dn_send,
                    (h ^ (shard & 1), 2 * i + n),
                    gd[at : at + half, span],
                    gd[at + part // 2 : at + part // 2 + half, span],
                )
    gu = dot(x, du, 0, 0).astype(BF)
    for m in range(4):
        at = m * height
        for h in range(2):
            span = slice(h * part, (h + 1) * part)
            store_halves(
                core,
                up_own,
                up_send,
                (shard ^ m, h),
                gu[at : at + half, span],
                gu[at + half : at + height, span],
            )
    new_down = dot(act, dw, 1, 0)
    new_dh2 = dot(du, uw, 1, 1)

    @pl.when(step == 0)
    def _():
        if k:
            down[...] = old_down[...] + new_down
            dh2[...] = old_dh2[...] + new_dh2
        else:
            down[...] = new_down
            dh2[...] = new_dh2

    @pl.when(step > 0)
    def _():
        down[...] += new_down
        dh2[...] += new_dh2


def mlp_part(sc, h2, dm, sm, wup, wdown, pieces, k, old):
    rows, width = h2.shape
    half, part = wup.shape[0] // 2, wdown.shape[0] // 2
    once = pl.Buffered(1)
    full = lambda a: pl.BlockSpec(a.shape, lambda j, sc: (0,) * a.ndim, pipeline_mode=once)
    whole = pl.BlockSpec((rows, width), lambda j, sc: (0, 0), pipeline_mode=once)
    by_up = pl.BlockSpec((4, 2, half, part), lambda j, sc: (0, (sc[0] >> 1) ^ j, 0, 0))
    by_down = pl.BlockSpec((2, 4, half, part), lambda j, sc: (j, 0, 0, 0))
    shares = SD((4, 4, half, part), BF)
    return pl.pallas_call(
        functools.partial(mlp_kernel, k=k),
        grid_spec=pltpu.PrefetchScalarGridSpec(
            num_scalar_prefetch=1,
            grid=(2,),
            in_specs=[VM] * 3 + [ANY] * 8 + [VM] * len(old),
            out_specs=[VM] * 2
            + [by_up] * 2
            + [by_down] * 2
            + [pl.BlockSpec((2, 1, part), lambda j, sc: ((sc[0] >> 1) ^ j, 0, 0))],
            scratch_shapes=[
                pltpu.VMEM((2, width, width), BF),
                pltpu.VMEM((2, width, width), BF),
                pltpu.SemaphoreType.DMA((24,)),
            ],
        ),
        out_shape=[SD((rows, width), F32)] * 2 + [shares] * 4 + [SD((4, 1, part), F32)],
        input_output_aliases={12: 0, 13: 1} if old else {},
        compiler_params=params(30),
        cost_estimate=cost(26),
        name="mlp%d" % k,
    )(sc, h2, dm, sm, wup, wdown, *pieces, *old)


def after_kernel(sc, down, dh2, mid, cot, keep, sm, o, dm, own, *rest, slots):
    pieces = rest[:6]
    out, dmid, do, g_own, g_send, gs, wbuf, sems = rest[6:]
    images, count, width = cot.shape
    every = pl.ds(0, width)
    height = own.shape[0]
    copies = run_copies(
        place_rows(wbuf, sc, (own, every), pieces, every, pl.ds(width, width), height), sems
    )
    for c in copies:
        c.start()
    e0 = dh2[...]
    xhat, rsq = normalized(mid[...])
    gs[...] = jnp.zeros_like(gs)
    gs[1:2, :] = jnp.sum(e0 * xhat, axis=0, keepdims=True)
    gs[2:3, :] = jnp.sum(e0, axis=0, keepdims=True)
    gs[3:4, :] = jnp.sum(dm[...].astype(F32), axis=0, keepdims=True)
    dmid[...] = norm_back(e0 * sm[G2 : G2 + 1, :], xhat, rsq)
    for i in range(images):
        sl = slice(i * slots, i * slots + count)
        dmid[sl, :] += cot[i].astype(F32) * keep[sl, :]
        out[i] = (keep[sl, :] * (mid[sl, :] + down[sl, :] + sm[DB : DB + 1, :])).astype(BF)
    low = dmid[...].astype(BF)
    gs[0:1, :] = jnp.sum(low.astype(F32), axis=0, keepdims=True)
    for c in copies:
        c.wait()
    do[...] = dot(low, wbuf[...], 1, 1).astype(BF)
    gw = dot(o[...], low, 0, 0).astype(BF)
    half, part = height // 2, width // 2
    for m in range(4):
        for j in range(2):
            cols = slice(j * part, (j + 1) * part)
            at = m * height
            store_halves(
                sc[1],
                g_own,
                g_send,
                (sc[0] ^ m, j),
                gw[at : at + half, cols],
                gw[at + half : at + height, cols],
            )


def after_mlp(sc, down, dh2, mid, cot, keep, sm, o, dm, own, pieces, slots):
    rows, width = o.shape
    half, part = own.shape[0] // 2, width // 2
    full = lambda a: pl.BlockSpec(a.shape, lambda j, sc: (0,) * a.ndim)
    whole = pl.BlockSpec((rows, width), lambda j, sc: (0, 0))
    share = pl.BlockSpec((4, 2, half, part), lambda j, sc: (0, 3, 0, 0))
    return pl.pallas_call(
        functools.partial(after_kernel, slots=slots),
        grid_spec=pltpu.PrefetchScalarGridSpec(
            num_scalar_prefetch=1,
            grid=(1,),
            in_specs=[VM] * 8 + [ANY] * 7,
            out_specs=[VM] * 3 + [share] * 2 + [VM],
            scratch_shapes=[pltpu.VMEM((width, width), BF), pltpu.SemaphoreType.DMA((7,))],
        ),
        out_shape=[SD(cot.shape, BF), SD((rows, width), F32), SD((rows, width), BF)]
        + [SD((4, 8, half, part), BF)] * 2
        + [SD((8, width), F32)],
        compiler_params=params(24),
        cost_estimate=cost(15),
        name="after_mlp",
    )(sc, down, dh2, mid, cot, keep, sm, o, dm, own, *pieces)


def project_grad_kernel(sc, h1, dx, old_own, old_send, g_own, g_send, gs, *, height):
    half, part = height // 2, dx.shape[1] // 2
    low = dx[...]
    gs[0] = jnp.broadcast_to(jnp.sum(low.astype(F32), axis=0, keepdims=True), gs.shape[1:])
    gw = dot(h1[...], low, 0, 0).astype(BF)
    for m in range(4):
        for j in range(2):
            cols = slice(j * part, (j + 1) * part)
            at = m * height
            store_halves(
                sc[1],
                g_own,
                g_send,
                (sc[0] ^ m, j),
                gw[at : at + half, cols],
                gw[at + half : at + height, cols],
            )


def project_grad(sc, h1, dx, g_own, g_send, height):
    rows, width = h1.shape
    half, part = height // 2, width // 2
    share = pl.BlockSpec((4, 2, half, part), lambda j, sc: (0, j, 0, 0))
    return pl.pallas_call(
        functools.partial(project_grad_kernel, height=height),
        grid_spec=pltpu.PrefetchScalarGridSpec(
            num_scalar_prefetch=1,
            grid=(3,),
            in_specs=[
                VM,
                pl.BlockSpec((rows, width), lambda j, sc: (0, j)),
                ANY,
                ANY,
            ],
            out_specs=[share, share, pl.BlockSpec((1, 8, width), lambda j, sc: (j, 0, 0))],
        ),
        out_shape=[SD((4, 8, half, part), BF)] * 2 + [SD((3, 8, width), F32)],
        input_output_aliases={3: 0, 4: 1},
        compiler_params=params(20),
        cost_estimate=cost(10),
        name="project_grad",
    )(sc, h1, dx, g_own, g_send)


def tokens_grad_kernel(sc, dx, tok, sm, dmid, ga, gp, gu0, gu1, own, *rest, slots):
    pp, pq = rest[:6], rest[6:12]
    out, gs, wbuf, acc, sems = rest[12:]
    images, count, width = tok.shape
    height = own.shape[0]
    two, third = pl.ds(0, 2 * width), pl.ds(2 * width, width)
    pairs = place_rows(wbuf, sc, (own, two), pp, two, two, height)
    pairs += place_rows(wbuf, sc, (own, third), pq, third, pl.ds(0, width), height)
    copies = run_copies(pairs, sems)
    for c in copies:
        c.start()
    gs[...] = jnp.zeros_like(gs)
    gs[OB : OB + 4, :] = ga[0:4, :]
    gs[QB : QB + 1, :] = gp[0, 0:1, :]
    gs[VB : VB + 1, :] = gp[2, 0:1, :]
    for b in range(4):
        gs[UB + b : UB + b + 1, : width // 2] = gu0[b]
        gs[UB + b : UB + b + 1, width // 2 :] = gu1[b]
    for c in copies:
        c.wait()
    acc[...] = dot(dx[...], wbuf[...], 1, 1)
    gain = jnp.zeros((1, width), F32)
    shift = jnp.zeros((1, width), F32)
    for i in range(images):
        sl = slice(i * slots, i * slots + count)
        e0 = acc[sl, :]
        xhat, rsq = normalized(tok[i].astype(F32))
        gain += jnp.sum(e0 * xhat, axis=0, keepdims=True)
        shift += jnp.sum(e0, axis=0, keepdims=True)
        out[i] = (dmid[sl, :] + norm_back(e0 * sm[G1 : G1 + 1, :], xhat, rsq)).astype(BF)
    gs[G1 : G1 + 1, :] = gain
    gs[B1 : B1 + 1, :] = shift


def tokens_grad(sc, dx, tok, sm, dmid, ga, gp, gu0, gu1, own, pieces, slots):
    rows, width = dmid.shape
    full = lambda a: pl.BlockSpec(a.shape, lambda j, sc: (0,) * a.ndim)
    operands = (dx, tok, sm, dmid, ga, gp, gu0, gu1)
    return pl.pallas_call(
        functools.partial(tokens_grad_kernel, slots=slots),
        grid_spec=pltpu.PrefetchScalarGridSpec(
            num_scalar_prefetch=1,
            grid=(1,),
            in_specs=[VM] * len(operands) + [ANY] * 13,
            out_specs=[VM] * 2,
            scratch_shapes=[
                pltpu.VMEM((width, 3 * width), BF),
                pltpu.VMEM((rows, width), F32),
                pltpu.SemaphoreType.DMA((14,)),
            ],
        ),
        out_shape=[SD(tok.shape, BF), SD((16, width), F32)],
        compiler_params=params(24),
        cost_estimate=cost(13),
        name="tokens_grad",
    )(sc, *operands, own, *pieces)


def lay_kernel(sc, *refs, kind):
    core, odd = sc[1], sc[2] % 2
    ins, (wide, tall) = refs[:-2], refs[-2:]
    half, part = ins[0].shape[1:]

    def put(k, side, first, second):
        which = core if side == 0 else 1 - core
        rows = pl.ds(pl.multiple_of(which * half, 8), half)
        if kind == "mlp":
            for b in range(4):
                wide[rows, pl.ds((2 * b + k) * part, part)] = first[b].astype(F32)
            for i in range(2):
                at = pl.multiple_of(which * 2 * half + (k * 4 + i) * half, 8)
                for j in range(2):
                    tall[pl.ds(at, half), pl.ds(j * part, part)] = second[2 * i + j].astype(F32)
        else:
            for n in range(4):
                wide[rows, pl.ds(n * part, part)] = first[n].astype(F32)
            for n in range(2):
                wide[rows, pl.ds((4 + n) * part, part)] = second[n].astype(F32)
                tall[rows, pl.ds(n * part, part)] = second[2 + n].astype(F32)

    for k in range(len(ins) // 4):
        kept, other, skept, sother = ins[4 * k : 4 * k + 4]

        @pl.when(odd == 0)
        def _(k=k, kept=kept, other=other, skept=skept, sother=sother):
            put(k, 0, kept, other)
            put(k, 1, skept, sother)

        @pl.when(odd != 0)
        def _(k=k, kept=kept, other=other, skept=skept, sother=sother):
            put(k, 0, other, kept)
            put(k, 1, sother, skept)


def lay_out(sc, finals, kind, shapes):
    full = lambda s: pl.BlockSpec(s, lambda j, sc: (0,) * len(s))
    flat = [a for group in finals for a in group]
    return pl.pallas_call(
        functools.partial(lay_kernel, kind=kind),
        grid_spec=pltpu.PrefetchScalarGridSpec(
            num_scalar_prefetch=1,
            grid=(1,),
            in_specs=[VM] * len(flat),
            out_specs=[VM] * 2,
        ),
        out_shape=[SD(s, F32) for s in shapes],
        compiler_params=params(8),
        cost_estimate=cost(4),
        name="lay_" + kind,
    )(sc, *flat)


def hops():
    def table(move):
        pairs = []
        for dp in range(8):
            for fs in range(4):
                z, core, shard = move(dp // 2, dp % 2, fs)
                pairs.append((dp * 4 + fs, (z * 2 + core) * 4 + shard))
        return pairs

    moves = {
        "sib": lambda z, c, f: (z, 1 - c, f),
        "x": lambda z, c, f: (z, c, f ^ 1),
        "y": lambda z, c, f: (z, c, f ^ 2),
        "xy": lambda z, c, f: (z, c, f ^ 3),
        "z1": lambda z, c, f: (z ^ 1, c, f),
        "z2": lambda z, c, f: (z ^ 2, c, f),
        "z3": lambda z, c, f: (z ^ 3, c, f),
    }
    tables = {name: table(move) for name, move in moves.items()}
    return lambda value, name: lax.ppermute(value, ("dp", "fsdp"), tables[name])


class Transfer:
    def __init__(self, stages):
        self.stages = stages
        self.flying = next(stages)
        self.result = None

    def step(self, landed):
        try:
            self.flying = self.stages.send(landed)
        except StopIteration as end:
            self.flying, self.result = (), end.value


def advance(held, *transfers):
    values = lax.optimization_barrier((held, tuple(t.flying for t in transfers)))
    for t, landed in zip(transfers, values[1]):
        t.step(landed)
    return values[0]


PLANE = ("x", "y", "xy")
LINE = ("z1", "z2", "z3")


def gather_stages(hop, own):
    far = yield tuple(hop(own, name) for name in PLANE)
    near = yield tuple(hop(a, "sib") for a in far)
    return tuple(far) + tuple(near)


def small_stages(hop, own):
    return (own,) + tuple((yield tuple(hop(own, name) for name in PLANE)))


def add(a, b):
    return (a.astype(F32) + b.astype(F32)).astype(BF)


def line_stages(hop, even, total):
    parts = total.shape[0] // 2
    keep = jnp.where(even, total[:parts], total[parts:])
    give = jnp.where(even, total[parts:], total[:parts]).astype(BF)
    (got,) = yield (hop(give, "z1"),)
    half = lax.optimization_barrier((keep + got.astype(F32)).astype(BF))
    (got,) = yield (hop(half, "z2"),)
    kept = add(half, got)
    other, skept = yield (hop(kept, "z1"), hop(kept, "sib"))
    (sother,) = yield (hop(other, "sib"),)
    return kept, other, skept, sother


def plane_stages(hop, even, chip):
    got = yield tuple(hop(chip(r).astype(BF), name) for r, name in enumerate(PLANE, 1))
    total = chip(0)
    for a in got:
        total = total + a.astype(F32)
    return (yield from line_stages(hop, even, total))


def ffn_stages(hop, even, up_own, up_send, dn_own, dn_send):
    up_got, dn_got = yield (hop(up_send, "sib"), hop(dn_send, "sib"))

    def chip(r):
        return jnp.concatenate(
            [
                up_own[r].astype(F32) + up_got[r].astype(F32),
                dn_own[r].astype(F32) + dn_got[r].astype(F32),
            ]
        )

    return (yield from plane_stages(hop, even, chip))


def attn_stages(hop, even, own, send):
    (got,) = yield (hop(send, "sib"),)
    chip = lambda r: own[r].astype(F32) + got[r].astype(F32)
    return (yield from plane_stages(hop, even, chip))


def sum_stages(hop, value):
    (got,) = yield (hop(value, "sib"),)
    value = value + got
    for names in (PLANE, LINE):
        one, two, three = yield tuple(hop(value, name) for name in names)
        value = (value + one) + (two + three)
    return value


def on_device_fast(
    tokens,
    mask,
    cotangent,
    ln1_gain,
    ln1_bias,
    w_qkv,
    qv_bias,
    w_out,
    out_bias,
    ln2_gain,
    ln2_bias,
    w_up,
    up_bias,
    w_down,
    down_bias,
):
    images, count, width = tokens.shape
    slots = -(-count // 8) * 8
    height = w_out.shape[0]
    half, part = height // 2, width // 2
    hop = hops()
    shard = lax.axis_index("fsdp")
    dp = lax.axis_index("dp")
    sc = jnp.stack([shard, dp % 2, dp // 2]).astype(jnp.int32)
    even = (dp // 2) % 2 == 0

    tie = lax.optimization_barrier
    small = (ln1_gain, ln1_bias, qv_bias, out_bias, ln2_gain, ln2_bias, down_bias, up_bias)
    top, bottom = pack_attn(sc, w_qkv, w_out, small)
    px, py, qx, qy = hop(top, "x"), hop(top, "y"), hop(bottom, "x"), hop(bottom, "y")
    own0, own1 = pack(sc, pack_ffn_kernel, 10, [(2 * height, width)] * 2, w_up, w_down)
    px, py, qx, qy, own0, own1 = tie((px, py, qx, qy, own0, own1))
    pfar, qfar = hop(px, "y"), hop(qy, "x")
    near = tuple(hop(a, "sib") for a in (px, py, qx, qy))
    pfar, qfar, near, own0, own1 = tie((pfar, qfar, near, own0, own1))
    spfar, sqfar = hop(pfar, "sib"), hop(qfar, "sib")
    ffn0 = Transfer(gather_stages(hop, own0))
    sc, spfar, sqfar = tie((sc, spfar, sqfar))
    pieces_p = (px, py, pfar, near[0], near[1], spfar)
    pieces_q = (qx, qy, qfar, near[2], near[3], sqfar)
    pieces = pieces_p + pieces_q

    keep = jnp.pad(mask.astype(F32), ((0, 0), (0, slots - count)))
    mask_row = keep.reshape(images, 1, slots)
    keep_col = keep.reshape(images * slots, 1)

    h1, qkv, sm = project(sc, tokens, w_qkv, top, pieces, slots)
    o = attend(qkv, mask_row, slots)
    o, own1 = tie((o, own1))
    ffn1 = Transfer(gather_stages(hop, own1))
    mid, h2, dm = middle_part(sc, tokens, o, sm, cotangent, keep_col, w_out, pieces_q, slots)
    h2 = advance(h2, ffn0)
    sc = advance(sc, ffn0)
    down, dh2, *shares, gu0 = mlp_part(sc, h2, dm, sm, w_up, w_down, ffn0.result, 0, ())
    down, dh2, *shares = advance((down, dh2, *shares), ffn1)
    m0 = Transfer(ffn_stages(hop, even, *shares))
    sc = advance(sc, ffn1, m0)
    down, dh2, *shares, gu1 = mlp_part(
        sc, h2, dm, sm, w_up, w_down, ffn1.result, 1, (down, dh2)
    )
    down, dh2, *shares = advance((down, dh2, *shares), m0)
    m1 = Transfer(ffn_stages(hop, even, *shares))
    layer_out, dmid, do, g_own, g_send, ga = after_mlp(
        sc, down, dh2, mid, cotangent, keep_col, sm, o, dm, w_out, pieces_q, slots
    )
    do = advance(do, m0, m1)
    dx = attend_back(qkv, do, keep_col, slots)
    dx = advance(dx, m0)
    g_own, g_send, gp = project_grad(sc, h1, dx, g_own, g_send, height)
    g_own, g_send, dx = advance((g_own, g_send, dx), m0, m1)
    attn = Transfer(attn_stages(hop, even, g_own, g_send))
    sc = advance(sc, attn)
    sc = advance(sc, m1)
    grad_tokens, gs = tokens_grad(
        sc, dx, tokens, sm, dmid, ga, gp, gu0, gu1, w_qkv, pieces, slots
    )
    gs = advance(gs, m0)
    total = Transfer(sum_stages(hop, gs))
    advance((), m1)
    advance((), attn, total)
    advance((), m1)
    advance((), attn, total)
    advance((), m1)
    ffn = lay_out(
        sc, (m0.result, m1.result), "mlp", ((height, 4 * width), (4 * height, width))
    )
    ffn = advance(ffn, attn, total)
    gs = total.result

    def mine(r, n=1):
        return lax.dynamic_slice(gs[r : r + n].reshape(-1), (shard * (n * height),), (n * height,))

    rows = tuple(mine(r) for r in (G1, B1, OB, G2, B2, DB)) + (mine(QB, 2), mine(UB, 4))
    while attn.flying:
        ffn, rows = advance((ffn, rows), attn)
    g1, b1, ob, g2, b2, db, qvb, ub = rows
    grad_w_up, grad_w_down = ffn
    grad_w_qkv, grad_w_out = lay_out(
        sc, (attn.result,), "attn", ((height, 3 * width), (height, width))
    )
    return (
        layer_out,
        grad_tokens,
        g1,
        b1,
        grad_w_qkv,
        qvb,
        grad_w_out,
        ob,
        g2,
        b2,
        grad_w_up,
        ub,
        grad_w_down,
        db,
    )


def norm(values, gain, shift):
    mean_value = jnp.mean(values, axis=-1, keepdims=True)
    centred = values - mean_value
    variance = jnp.mean(centred * centred, axis=-1, keepdims=True)
    return centred * lax.rsqrt(variance + EPS) * gain + shift


def gelu_exact(values):
    return jax.nn.gelu(values, approximate=False)


def score_block(query, key_part, valid):
    scores = jnp.einsum(
        "iqhe,ikhe->ihqk", query, key_part, preferred_element_type=jnp.float32
    ) * HD ** (-0.5)
    return jnp.where(valid, scores, -1e30)


def arrange(grad, groups, copies):
    shaped = grad.reshape((groups, copies, grad.shape[0] // (groups * copies)) + grad.shape[1:])
    return jnp.swapaxes(shaped, 0, 1).reshape(grad.shape)


def reduce_six(grad_one, grad_two, grad_three, grad_four, grad_five, grad_six):
    groups = lax.axis_size("fsdp")
    copies = lax.axis_size("dp")
    pieces = (
        lax.psum_scatter(
            arrange(grad_one, groups, copies), ("dp", "fsdp"), scatter_dimension=0, tiled=True
        ),
        lax.psum_scatter(
            arrange(grad_two, groups, copies), ("dp", "fsdp"), scatter_dimension=0, tiled=True
        ),
        lax.psum_scatter(
            arrange(grad_three, groups, copies), ("dp", "fsdp"), scatter_dimension=0, tiled=True
        ),
        lax.psum_scatter(
            arrange(grad_four, groups, copies), ("dp", "fsdp"), scatter_dimension=0, tiled=True
        ),
        lax.psum_scatter(
            arrange(grad_five, groups, copies), ("dp", "fsdp"), scatter_dimension=0, tiled=True
        ),
        lax.psum_scatter(
            arrange(grad_six, groups, copies), ("dp", "fsdp"), scatter_dimension=0, tiled=True
        ),
    )
    return (
        lax.all_gather(pieces[0].astype(jnp.bfloat16), "dp", axis=0, tiled=True).astype(
            jnp.float32
        ),
        lax.all_gather(pieces[1].astype(jnp.bfloat16), "dp", axis=0, tiled=True).astype(
            jnp.float32
        ),
        lax.all_gather(pieces[2].astype(jnp.bfloat16), "dp", axis=0, tiled=True).astype(
            jnp.float32
        ),
        lax.all_gather(pieces[3].astype(jnp.bfloat16), "dp", axis=0, tiled=True).astype(
            jnp.float32
        ),
        lax.all_gather(pieces[4].astype(jnp.bfloat16), "dp", axis=0, tiled=True).astype(
            jnp.float32
        ),
        lax.all_gather(pieces[5].astype(jnp.bfloat16), "dp", axis=0, tiled=True).astype(
            jnp.float32
        ),
    )


def on_device(
    tokens,
    mask,
    cotangent,
    ln1_gain,
    ln1_bias,
    w_qkv,
    qv_bias,
    w_out,
    out_bias,
    ln2_gain,
    ln2_bias,
    w_up,
    up_bias,
    w_down,
    down_bias,
):
    image_count, slot_count, width = tokens.shape
    row_count = image_count * slot_count
    heads = width // HD
    scale = HD ** (-0.5)
    attn_full = (
        lax.all_gather(ln1_gain, "fsdp", axis=0, tiled=True),
        lax.all_gather(ln1_bias, "fsdp", axis=0, tiled=True),
        lax.all_gather(w_qkv, "fsdp", axis=0, tiled=True),
        lax.all_gather(qv_bias, "fsdp", axis=0, tiled=True),
        lax.all_gather(w_out, "fsdp", axis=0, tiled=True),
        lax.all_gather(out_bias, "fsdp", axis=0, tiled=True),
    )
    mlp_full = (
        lax.all_gather(ln2_gain, "fsdp", axis=0, tiled=True),
        lax.all_gather(ln2_bias, "fsdp", axis=0, tiled=True),
        lax.all_gather(w_up, "fsdp", axis=0, tiled=True),
        lax.all_gather(up_bias, "fsdp", axis=0, tiled=True),
        lax.all_gather(w_down, "fsdp", axis=0, tiled=True),
        lax.all_gather(down_bias, "fsdp", axis=0, tiled=True),
    )
    gain_one, shift_one, qkv_weight, qkv_shift, out_weight, out_shift = attn_full
    gain_two, shift_two, up_weight, up_shift, down_weight, down_shift = mlp_full
    keep = mask.astype(jnp.float32)
    valid = (keep > 0.5)[:, None, None, :]
    keep_rows = keep.reshape(row_count, 1)
    inputs = tokens.astype(jnp.float32).reshape(row_count, width)
    normed_one, norm_one_back = jax.vjp(
        norm, inputs, gain_one.astype(jnp.float32), shift_one.astype(jnp.float32)
    )
    normed_low = normed_one.astype(jnp.bfloat16)
    qv_float = qkv_shift.astype(jnp.float32)
    full_bias = jnp.concatenate(
        [qv_float[:width], jnp.zeros((width,), jnp.float32), qv_float[width:]]
    )
    projected = (
        jnp.dot(normed_low, qkv_weight, preferred_element_type=jnp.float32) + full_bias
    ).astype(jnp.bfloat16)
    query = projected[:, :width].reshape(image_count, slot_count, heads, HD)
    key_part = projected[:, width : 2 * width].reshape(image_count, slot_count, heads, HD)
    value = projected[:, 2 * width :].reshape(image_count, slot_count, heads, HD)
    scores = score_block(query, key_part, valid)
    top = jnp.max(scores, axis=-1, keepdims=True)
    lse = top + jnp.log(jnp.sum(jnp.exp(scores - top), axis=-1, keepdims=True))
    probs_low = jnp.exp(scores - lse).astype(jnp.bfloat16)
    mixed = jnp.einsum("ihqk,ikhe->iqhe", probs_low, value, preferred_element_type=jnp.float32)
    mixed = mixed.reshape(row_count, width).astype(jnp.bfloat16)
    middle = (
        inputs
        + jnp.dot(mixed, out_weight, preferred_element_type=jnp.float32)
        + out_shift.astype(jnp.float32)
    )
    normed_two, norm_two_back = jax.vjp(
        norm, middle, gain_two.astype(jnp.float32), shift_two.astype(jnp.float32)
    )
    normed_two_low = normed_two.astype(jnp.bfloat16)
    upward = jnp.dot(
        normed_two_low, up_weight, preferred_element_type=jnp.float32
    ) + up_shift.astype(jnp.float32)
    active, gelu_back = jax.vjp(gelu_exact, upward)
    active_low = active.astype(jnp.bfloat16)
    downward = jnp.dot(
        active_low, down_weight, preferred_element_type=jnp.float32
    ) + down_shift.astype(jnp.float32)
    layer_out = (
        (keep_rows * (middle + downward))
        .astype(jnp.bfloat16)
        .reshape(image_count, slot_count, width)
    )
    mlp_back = (
        lax.all_gather(ln2_gain, "fsdp", axis=0, tiled=True),
        lax.all_gather(ln2_bias, "fsdp", axis=0, tiled=True),
        lax.all_gather(w_up, "fsdp", axis=0, tiled=True),
        lax.all_gather(up_bias, "fsdp", axis=0, tiled=True),
        lax.all_gather(w_down, "fsdp", axis=0, tiled=True),
        lax.all_gather(down_bias, "fsdp", axis=0, tiled=True),
    )
    up_back = mlp_back[2]
    down_back = mlp_back[4]
    grad_rows = cotangent.astype(jnp.float32).reshape(row_count, width) * keep_rows
    grad_down_low = grad_rows.astype(jnp.bfloat16)
    grad_w_down = jnp.einsum(
        "rf,rd->fd", active_low, grad_down_low, preferred_element_type=jnp.float32
    )
    grad_down_bias = jnp.sum(grad_down_low, axis=0, dtype=jnp.float32)
    grad_active = jnp.einsum(
        "rd,fd->rf", grad_down_low, down_back, preferred_element_type=jnp.float32
    )
    grad_up_low = gelu_back(grad_active)[0].astype(jnp.bfloat16)
    grad_w_up = jnp.einsum(
        "rd,rf->df", normed_two_low, grad_up_low, preferred_element_type=jnp.float32
    )
    grad_up_bias = jnp.sum(grad_up_low, axis=0, dtype=jnp.float32)
    grad_normed_two = jnp.einsum(
        "rf,df->rd", grad_up_low, up_back, preferred_element_type=jnp.float32
    )
    grad_mid_norm, grad_ln2_gain, grad_ln2_bias = norm_two_back(grad_normed_two)
    grad_middle = grad_rows + grad_mid_norm
    mlp_grads = reduce_six(
        grad_ln2_gain, grad_ln2_bias, grad_w_up, grad_up_bias, grad_w_down, grad_down_bias
    )
    attn_back = (
        lax.all_gather(ln1_gain, "fsdp", axis=0, tiled=True),
        lax.all_gather(ln1_bias, "fsdp", axis=0, tiled=True),
        lax.all_gather(w_qkv, "fsdp", axis=0, tiled=True),
        lax.all_gather(qv_bias, "fsdp", axis=0, tiled=True),
        lax.all_gather(w_out, "fsdp", axis=0, tiled=True),
        lax.all_gather(out_bias, "fsdp", axis=0, tiled=True),
    )
    qkv_back = attn_back[2]
    out_back = attn_back[4]
    grad_attn_low = grad_middle.astype(jnp.bfloat16)
    grad_w_out = jnp.einsum("rd,re->de", mixed, grad_attn_low, preferred_element_type=jnp.float32)
    grad_out_bias = jnp.sum(grad_attn_low, axis=0, dtype=jnp.float32)
    grad_mixed = jnp.einsum(
        "re,de->rd", grad_attn_low, out_back, preferred_element_type=jnp.float32
    )
    grad_mixed = grad_mixed.astype(jnp.bfloat16).reshape(image_count, slot_count, heads, HD)
    probs = jnp.exp(score_block(query, key_part, valid) - lse)
    probs_again = probs.astype(jnp.bfloat16)
    grad_value = jnp.einsum(
        "ihqk,iqhe->ikhe", probs_again, grad_mixed, preferred_element_type=jnp.float32
    )
    grad_probs = jnp.einsum(
        "iqhe,ikhe->ihqk", grad_mixed, value, preferred_element_type=jnp.float32
    )
    inner = jnp.sum(grad_probs * probs, axis=-1, keepdims=True)
    grad_scores = (probs * (grad_probs - inner)).astype(jnp.bfloat16)
    grad_query = (
        jnp.einsum("ihqk,ikhe->iqhe", grad_scores, key_part, preferred_element_type=jnp.float32)
        * scale
    )
    grad_key = (
        jnp.einsum("ihqk,iqhe->ikhe", grad_scores, query, preferred_element_type=jnp.float32)
        * scale
    )
    grad_projected = jnp.concatenate(
        [
            grad_query.reshape(row_count, width),
            grad_key.reshape(row_count, width),
            grad_value.reshape(row_count, width),
        ],
        axis=1,
    ).astype(jnp.bfloat16)
    grad_w_qkv = jnp.einsum(
        "rd,re->de", normed_low, grad_projected, preferred_element_type=jnp.float32
    )
    grad_qv_bias = jnp.concatenate(
        [
            jnp.sum(grad_projected[:, :width], axis=0, dtype=jnp.float32),
            jnp.sum(grad_projected[:, 2 * width :], axis=0, dtype=jnp.float32),
        ]
    )
    grad_normed_one = jnp.einsum(
        "re,de->rd", grad_projected, qkv_back, preferred_element_type=jnp.float32
    )
    grad_in_norm, grad_ln1_gain, grad_ln1_bias = norm_one_back(grad_normed_one)
    grad_tokens = (
        (grad_middle + grad_in_norm).astype(jnp.bfloat16).reshape(image_count, slot_count, width)
    )
    attn_grads = reduce_six(
        grad_ln1_gain, grad_ln1_bias, grad_w_qkv, grad_qv_bias, grad_w_out, grad_out_bias
    )
    return (
        layer_out,
        grad_tokens,
        attn_grads[0],
        attn_grads[1],
        attn_grads[2],
        attn_grads[3],
        attn_grads[4],
        attn_grads[5],
        mlp_grads[0],
        mlp_grads[1],
        mlp_grads[2],
        mlp_grads[3],
        mlp_grads[4],
        mlp_grads[5],
    )


def solution(mesh):
    in_specs = (
        P(("dp", "fsdp"), None, None),
        P(("dp", "fsdp"), None),
        P(("dp", "fsdp"), None, None),
        P("fsdp"),
        P("fsdp"),
        P("fsdp", None),
        P("fsdp"),
        P("fsdp", None),
        P("fsdp"),
        P("fsdp"),
        P("fsdp"),
        P("fsdp", None),
        P("fsdp"),
        P("fsdp", None),
        P("fsdp"),
    )
    out_specs = (
        P(("dp", "fsdp"), None, None),
        P(("dp", "fsdp"), None, None),
        P("fsdp"),
        P("fsdp"),
        P("fsdp", None),
        P("fsdp"),
        P("fsdp", None),
        P("fsdp"),
        P("fsdp"),
        P("fsdp"),
        P("fsdp", None),
        P("fsdp"),
        P("fsdp", None),
        P("fsdp"),
    )
    fast = dict(mesh.shape) == {"dp": 8, "fsdp": 4}
    return jax.shard_map(
        on_device_fast if fast else on_device, mesh=mesh, in_specs=in_specs, out_specs=out_specs, check_vma=False
    )
```

```python
import functools

import jax
import jax.numpy as jnp
import numpy as np
from jax import lax
from jax.experimental import pallas as pl
from jax.experimental.pallas import tpu as pltpu
from jax.sharding import PartitionSpec as P

HD = 64
EPS = 1e-06
F32 = jnp.float32
BF = jnp.bfloat16
MB = 2**20
SCORE_SCALE = np.float32(np.log2(np.e) * HD ** (-0.5))
MASKED = np.float32(-1e30)
SD = jax.ShapeDtypeStruct
ANY = pl.BlockSpec(memory_space=pl.ANY)
VM = pl.BlockSpec(memory_space=pltpu.VMEM)


def dot(a, b, ca, cb):
    return lax.dot_general(a, b, (((ca,), (cb,)), ((), ())), preferred_element_type=F32)


def params(mb=58):
    return pltpu.CompilerParams(vmem_limit_bytes=mb * MB)


def cost(micros):
    return pl.CostEstimate(flops=int(micros * 1.15e9), bytes_accessed=0, transcendentals=0)


def normalized(values):
    mean = jnp.mean(values, axis=-1, keepdims=True)
    centred = values - mean
    rsq = lax.rsqrt(jnp.mean(centred * centred, axis=-1, keepdims=True) + EPS)
    return centred * rsq, rsq


def norm_back(e, xhat, rsq):
    return rsq * (
        e
        - jnp.mean(e, axis=-1, keepdims=True)
        - xhat * jnp.mean(e * xhat, axis=-1, keepdims=True)
    )


def run_copies(pairs, sems, base=0):
    copies = [
        pltpu.make_async_copy(src, dst, sems.at[base + n]) for n, (src, dst) in enumerate(pairs)
    ]
    return copies


PACK_MB = 54

G1, B1, QB, VB, OB, G2, B2, DB, UB = range(9)


def all_copies(pairs, sems):
    copies = run_copies(pairs, sems)
    for c in copies:
        c.start()
    for c in copies:
        c.wait()


def pack_attn_kernel(sc, wqkv, wout, *rest):
    small, (top, bottom, table, sems) = rest[:8], rest[8:]
    height, width = wout.shape
    half = height // 2
    rows = pl.ds(pl.multiple_of(sc[1] * half, 16), half)
    copies = run_copies(
        [
            (wqkv.at[rows, pl.ds(0, 2 * width)], top.at[pl.ds(0, half), :]),
            (wqkv.at[rows, pl.ds(2 * width, width)], bottom.at[:, pl.ds(0, width)]),
            (wout.at[rows, :], bottom.at[:, pl.ds(width, width)]),
        ],
        sems,
    )
    for c in copies:
        c.start()
    table[...] = jnp.zeros_like(table)
    row = 0
    for ref in small:
        values = ref[...].astype(F32)
        for n in range(ref.shape[0] // height):
            table[row : row + 1, :height] = values[n * height : (n + 1) * height].reshape(1, height)
            row += 1
    top[half:, : table.shape[1]] = table[...].astype(BF)
    for c in copies:
        c.wait()


def pack_attn(sc, wqkv, wout, small):
    height, width = wout.shape
    lanes = -(-height // 128) * 128
    return pl.pallas_call(
        pack_attn_kernel,
        grid_spec=pltpu.PrefetchScalarGridSpec(
            num_scalar_prefetch=1,
            in_specs=[ANY] * 2 + [VM] * 8,
            out_specs=[VM] * 2,
            scratch_shapes=[pltpu.VMEM((16, lanes), F32), pltpu.SemaphoreType.DMA((3,))],
        ),
        out_shape=[SD((height // 2 + 16, 2 * width), BF), SD((height // 2, 2 * width), BF)],
        compiler_params=params(PACK_MB),
        name="pack_attn",
    )(sc, wqkv, wout, *small)


def pack_ffn_kernel(sc, wup, wdown, ffn0, ffn1, sems):
    width = wdown.shape[1]
    half, part = wup.shape[0] // 2, wdown.shape[0] // 2
    rows = pl.ds(pl.multiple_of(sc[1] * half, 16), half)
    pairs = []
    for k, ffn in enumerate((ffn0, ffn1)):
        for g in range(2):
            for h in range(2):
                block = 2 * ((sc[0] >> 1) ^ g) + h
                at = pl.multiple_of(block * width + k * part, 128)
                pairs.append(
                    (
                        wup.at[rows, pl.ds(at, part)],
                        ffn.at[pl.ds(g * half, half), pl.ds(h * part, part)],
                    )
                )
        at = pl.multiple_of(k * part + sc[1] * (part // 2), 16)
        pairs.append((wdown.at[pl.ds(at, part // 2), :], ffn.at[pl.ds(2 * half, part // 2), :]))
    all_copies(pairs, sems)


def pack(sc, kernel, copies, shapes, *weights):
    return pl.pallas_call(
        kernel,
        grid_spec=pltpu.PrefetchScalarGridSpec(
            num_scalar_prefetch=1,
            in_specs=[ANY] * len(weights),
            out_specs=[ANY] * len(shapes),
            scratch_shapes=[pltpu.SemaphoreType.DMA((copies,))],
        ),
        out_shape=[SD(shape, BF) for shape in shapes],
        compiler_params=params(2),
        name="pack",
    )(sc, *weights)


def place_rows(dst, sc, own, pieces, cols, src_cols, height, base=0):
    half = height // 2
    shard, core = sc[0], sc[1]
    pairs = []
    if own is not None:
        src, take = own
        pairs.append((src.at[:, take], dst.at[pl.ds(pl.multiple_of(shard * height, 16), height), cols]))
    for side in range(2):
        which = core if side == 0 else 1 - core
        for r in range(1, 4):
            at = pl.multiple_of((shard ^ r) * height + which * half, 16)
            pairs.append(
                (
                    pieces[side * 3 + r - 1].at[pl.ds(base * half, half), src_cols],
                    dst.at[pl.ds(at, half), cols],
                )
            )
    return pairs


def fill_small(sc, pieces, sm, height):
    shard = sc[0]
    vals = [pieces[r].astype(F32) for r in range(4)]

    def of(j):
        got = vals[3]
        for r in range(3):
            got = jnp.where(shard == (j ^ r), vals[r], got)
        return got[:, :height]

    by = [of(j) for j in range(4)]
    sm[...] = jnp.zeros_like(sm)
    for j in range(4):
        cols = slice(j * height, (j + 1) * height)
        sm[G1 : B1 + 1, cols] = by[j][0:2]
        sm[OB : DB + 1, cols] = by[j][4:8]
        for n in range(2):
            at = (2 * j + n) % 4 * height
            row = QB if j < 2 else VB
            sm[row : row + 1, at : at + height] = by[j][2 + n : 3 + n]
        for n in range(4):
            sm[UB + j : UB + j + 1, n * height : (n + 1) * height] = by[j][8 + n : 9 + n]


def project_kernel(sc, tok, own, packed, *rest, slots):
    pp, pq = rest[:6], rest[6:12]
    h1, qkv, sm, wbuf, small, sems = rest[12:]
    images, count, width = tok.shape
    height = own.shape[0]
    step = pl.program_id(0)
    two = pl.ds(0, 2 * width)
    third = pl.ds(2 * width, width)
    first = run_copies(place_rows(wbuf, sc, (own, two), pp, two, two, height), sems)
    last = run_copies(
        place_rows(wbuf, sc, (own, third), pq, third, pl.ds(0, width), height),
        sems,
        len(first),
    )

    corner = (pl.ds(height // 2, 16), pl.ds(0, small.shape[2]))
    table = run_copies(
        [
            (ref.at[corner[0], corner[1]], small.at[r])
            for r, ref in enumerate((packed,) + pp[:3])
        ],
        sems,
        len(first) + len(last),
    )

    @pl.when(step == 0)
    def _():
        for c in table + first + last:
            c.start()
        for c in table:
            c.wait()
        fill_small(sc, small, sm, height)
        for i in range(images):
            xhat, _ = normalized(tok[i].astype(F32))
            low = (xhat * sm[G1 : G1 + 1, :] + sm[B1 : B1 + 1, :]).astype(BF)
            tail = count // 8 * 8
            h1[i * slots + tail : (i + 1) * slots, :] = jnp.zeros((slots - tail, width), BF)
            h1[i * slots : i * slots + count, :] = low
        for c in first:
            c.wait()

    @pl.when(step == 2)
    def _():
        for c in last:
            c.wait()

    row = jnp.where(step == 0, sm[QB : QB + 1, :], sm[VB : VB + 1, :])
    row = jnp.where(step == 1, jnp.zeros_like(row), row)
    weight = wbuf[:, pl.ds(pl.multiple_of(step * width, 128), width)]
    qkv[...] = (dot(h1[...], weight, 1, 0) + row).astype(BF)


def project(sc, tok, own, packed, pieces, slots):
    images, _, width = tok.shape
    rows = images * slots
    full = lambda *s: pl.BlockSpec(s, lambda j, sc: (0,) * len(s))
    return pl.pallas_call(
        functools.partial(project_kernel, slots=slots),
        grid_spec=pltpu.PrefetchScalarGridSpec(
            num_scalar_prefetch=1,
            grid=(3,),
            in_specs=[VM] + [ANY] * 14,
            out_specs=[
                VM,
                pl.BlockSpec((rows, width), lambda j, sc: (0, j)),
                VM,
            ],
            scratch_shapes=[
                pltpu.VMEM((width, 3 * width), BF),
                pltpu.VMEM((4, 16, -(-own.shape[0] // 128) * 128), BF),
                pltpu.SemaphoreType.DMA((18,)),
            ],
        ),
        out_shape=[SD((rows, width), BF), SD((rows, 3 * width), BF), SD((16, width), F32)],
        compiler_params=params(54),
        cost_estimate=cost(10),
        name="project",
    )(sc, tok, own, packed, *pieces)


def head_lanes():
    return lax.broadcasted_iota(jnp.int32, (1, 2 * HD), 1) < HD


def attend_kernel(q, k, v, mask, o, *, pairs):
    low_half = head_lanes()
    keep = mask[0] > 0
    zero = jnp.zeros((), BF)
    for p in range(pairs):
        sl = slice(p * 2 * HD, (p + 1) * 2 * HD)
        qp, kp, vp = q[:, sl], k[:, sl], v[:, sl]
        outs = []
        for a in range(2):
            mine = low_half if a == 0 else jnp.logical_not(low_half)
            s = dot(jnp.where(mine, qp, zero), kp, 1, 1)
            s = jnp.where(keep, s * SCORE_SCALE, MASKED)
            e = jnp.exp2(s - jnp.max(s, axis=-1, keepdims=True))
            prob = (e * (1.0 / jnp.sum(e, axis=-1, keepdims=True))).astype(BF)
            outs.append(dot(prob, jnp.where(mine, vp, zero), 1, 0))
        o[:, sl] = (outs[0] + outs[1]).astype(BF)


def attend(qkv, mask_row, slots):
    rows, three = qkv.shape
    width, images = three // 3, rows // slots
    block = lambda n: pl.BlockSpec((slots, width), lambda i: (i, n))
    return pl.pallas_call(
        functools.partial(attend_kernel, pairs=width // (2 * HD)),
        grid=(images,),
        in_specs=[block(0), block(1), block(2), pl.BlockSpec((1, 1, slots), lambda i: (i, 0, 0))],
        out_specs=block(0),
        out_shape=SD((rows, width), BF),
        compiler_params=params(40),
        cost_estimate=cost(11),
        name="attend",
    )(qkv, qkv, qkv, mask_row)


def attend_back_kernel(q, k, v, do, mask, dx, *, pairs):
    low_half = head_lanes()
    keep = mask[...] > 0
    zero = jnp.zeros((), BF)
    scale = np.float32(HD ** (-0.5))
    wide = pairs * 2 * HD
    for p in range(pairs):
        sl = slice(p * 2 * HD, (p + 1) * 2 * HD)
        qp, kp, vp, dop = q[:, sl], k[:, sl], v[:, sl], do[:, sl]
        gq, gk, gv = [], [], []
        for a in range(2):
            mine = low_half if a == 0 else jnp.logical_not(low_half)
            qm, km, dm = (jnp.where(mine, t, zero) for t in (qp, kp, dop))
            s = dot(km, qp, 1, 1)
            s = jnp.where(keep, s * SCORE_SCALE, MASKED)
            e = jnp.exp2(s - jnp.max(s, axis=0, keepdims=True))
            prob = e * (1.0 / jnp.sum(e, axis=0, keepdims=True))
            gv.append(dot(prob.astype(BF), dm, 1, 0))
            weighed = prob * dot(vp, dm, 1, 1)
            inner = jnp.sum(weighed, axis=0, keepdims=True)
            ds = (weighed - prob * inner).astype(BF)
            gk.append(dot(ds, qm, 1, 0))
            gq.append(dot(ds, km, 0, 0))
        at = p * 2 * HD
        dx[:, at : at + 2 * HD] = ((gq[0] + gq[1]) * scale).astype(BF)
        dx[:, wide + at : wide + at + 2 * HD] = ((gk[0] + gk[1]) * scale).astype(BF)
        dx[:, 2 * wide + at : 2 * wide + at + 2 * HD] = (gv[0] + gv[1]).astype(BF)


def attend_back(qkv, do, mask_col, slots):
    rows, three = qkv.shape
    width, images = three // 3, rows // slots
    block = lambda n: pl.BlockSpec((slots, width), lambda i: (i, n))
    return pl.pallas_call(
        functools.partial(attend_back_kernel, pairs=width // (2 * HD)),
        grid=(images,),
        in_specs=[block(0), block(1), block(2), block(0), pl.BlockSpec((slots, 1), lambda i: (i, 0))],
        out_specs=pl.BlockSpec((slots, 3 * width), lambda i: (i, 0)),
        out_shape=SD((rows, 3 * width), BF),
        compiler_params=params(16),
        cost_estimate=cost(20),
        name="attend_back",
    )(qkv, qkv, qkv, do, mask_col)


def middle_kernel(sc, tok, o, sm, cot, keep, own, *rest, slots):
    pieces = rest[:6]
    mid, h2, dm, wbuf, sems = rest[6:]
    images, count, width = tok.shape
    every = pl.ds(0, width)
    copies = run_copies(
        place_rows(wbuf, sc, (own, every), pieces, every, pl.ds(width, width), own.shape[0]),
        sems,
    )
    for c in copies:
        c.start()
    tail = count // 8 * 8
    for i in range(images):
        sl = slice(i * slots, i * slots + count)
        dm[i * slots + tail : (i + 1) * slots, :] = jnp.zeros((slots - tail, width), BF)
        dm[sl, :] = (cot[i].astype(F32) * keep[sl, :]).astype(BF)
    for c in copies:
        c.wait()
    mid[...] = dot(o[...], wbuf[...], 1, 0) + sm[OB : OB + 1, :]
    for i in range(images):
        sl = slice(i * slots, i * slots + count)
        mid[sl, :] += tok[i].astype(F32)
    xhat, _ = normalized(mid[...])
    h2[...] = (xhat * sm[G2 : G2 + 1, :] + sm[B2 : B2 + 1, :]).astype(BF)


def middle_part(sc, tok, o, sm, cot, keep, own, pieces, slots):
    rows, width = o.shape
    full = lambda a: pl.BlockSpec(a.shape, lambda j, sc: (0,) * a.ndim)
    whole = pl.BlockSpec((rows, width), lambda j, sc: (0, 0))
    return pl.pallas_call(
        functools.partial(middle_kernel, slots=slots),
        grid_spec=pltpu.PrefetchScalarGridSpec(
            num_scalar_prefetch=1,
            grid=(1,),
            in_specs=[VM] * 5 + [ANY] * 7,
            out_specs=[VM] * 3,
            scratch_shapes=[pltpu.VMEM((width, width), BF), pltpu.SemaphoreType.DMA((7,))],
        ),
        out_shape=[SD((rows, width), F32), SD((rows, width), BF), SD((rows, width), BF)],
        compiler_params=params(16),
        cost_estimate=cost(9),
        name="middle",
    )(sc, tok, o, sm, cot, keep, own, *pieces)


def store_halves(core, own_ref, send_ref, index, first, second):
    @pl.when(core == 0)
    def _():
        own_ref[index] = first
        send_ref[index] = second

    @pl.when(core != 0)
    def _():
        own_ref[index] = second
        send_ref[index] = first


def mlp_kernel(sc, h2, dm, sm, wup, wdown, *rest, k):
    pieces, rest = rest[:6], rest[6:]
    if k:
        old_down, old_dh2 = rest[:2]
        rest = rest[2:]
    down, dh2, up_own, up_send, dn_own, dn_send, gub, ubuf, dbuf, sems = rest
    shard, core = sc[0], sc[1]
    step = pl.program_id(0)
    width = h2.shape[1]
    height = wup.shape[0]
    half, part = height // 2, wdown.shape[0] // 2
    take = slice(k * part, (k + 1) * part)
    blocks = []
    for j in range(2):
        mine = pl.ds(pl.multiple_of(shard * height, 16), height)
        pairs = []
        for h in range(2):
            at = pl.multiple_of((2 * ((shard >> 1) ^ j) + h) * width + k * part, 128)
            pairs.append(
                (wup.at[:, pl.ds(at, part)], ubuf.at[j, mine, pl.ds(h * part, part)])
            )
        if j == 0:
            at = pl.multiple_of((shard & 1) * part, 16)
            pairs.append((wdown.at[pl.ds(k * part, part), :], dbuf.at[0, pl.ds(at, part), :]))
        for side in range(2):
            which = core if side == 0 else 1 - core
            for m in range(1, 4):
                piece = pieces[side * 3 + m - 1]
                at = pl.multiple_of((shard ^ m) * height + which * half, 16)
                g = j ^ (m >> 1)
                pairs.append((piece.at[pl.ds(g * half, half), :], ubuf.at[j, pl.ds(at, half), :]))
                if m >> 1 == j:
                    at = ((shard ^ m) & 1) * part + which * (part // 2)
                    at = pl.multiple_of(at, 16)
                    pairs.append(
                        (
                            piece.at[pl.ds(2 * half, part // 2), :],
                            dbuf.at[j, pl.ds(at, part // 2), :],
                        )
                    )
        blocks.append(run_copies(pairs, sems, 12 * j))

    @pl.when(step == 0)
    def _():
        for c in blocks[0] + blocks[1]:
            c.start()
        for c in blocks[0]:
            c.wait()

    @pl.when(step == 1)
    def _():
        for c in blocks[1]:
            c.wait()

    uw, dw = ubuf[step], dbuf[step]
    x, g = h2[...], dm[...]
    pair = 2 * ((shard >> 1) ^ step)
    bias = jnp.concatenate([sm[pl.ds(UB + pair + h, 1), take] for h in range(2)], axis=1)
    u = dot(x, uw, 1, 0) + bias
    dact = dot(g, dw, 1, 1)
    cdf = 0.5 * (1.0 + lax.erf(u * np.float32(np.sqrt(0.5))))
    act = (u * cdf).astype(BF)
    slope = cdf + u * (jnp.exp(-0.5 * u * u) * np.float32(1.0 / np.sqrt(2.0 * np.pi)))
    du = (dact * slope).astype(BF)
    bsum = jnp.sum(du.astype(F32), axis=0, keepdims=True)
    gd = dot(act, g, 0, 0).astype(BF)
    for h in range(2):
        gub[h] = bsum[:, h * part : (h + 1) * part]
        for i in range(2):
            for n in range(2):
                span = slice(n * part, (n + 1) * part)
                at = h * part + i * half
                store_halves(
                    core,
                    dn_own,
                    dn_send,
                    (h ^ (shard & 1), 2 * i + n),
                    gd[at : at + half, span],
                    gd[at + part // 2 : at + part // 2 + half, span],
                )
    gu = dot(x, du, 0, 0).astype(BF)
    for m in range(4):
        at = m * height
        for h in range(2):
            span = slice(h * part, (h + 1) * part)
            store_halves(
                core,
                up_own,
                up_send,
                (shard ^ m, h),
                gu[at : at + half, span],
                gu[at + half : at + height, span],
            )
    new_down = dot(act, dw, 1, 0)
    new_dh2 = dot(du, uw, 1, 1)

    @pl.when(step == 0)
    def _():
        if k:
            down[...] = old_down[...] + new_down
            dh2[...] = old_dh2[...] + new_dh2
        else:
            down[...] = new_down
            dh2[...] = new_dh2

    @pl.when(step > 0)
    def _():
        down[...] += new_down
        dh2[...] += new_dh2


def mlp_part(sc, h2, dm, sm, wup, wdown, pieces, k, old):
    rows, width = h2.shape
    half, part = wup.shape[0] // 2, wdown.shape[0] // 2
    once = pl.Buffered(1)
    full = lambda a: pl.BlockSpec(a.shape, lambda j, sc: (0,) * a.ndim, pipeline_mode=once)
    whole = pl.BlockSpec((rows, width), lambda j, sc: (0, 0), pipeline_mode=once)
    by_up = pl.BlockSpec((4, 2, half, part), lambda j, sc: (0, (sc[0] >> 1) ^ j, 0, 0))
    by_down = pl.BlockSpec((2, 4, half, part), lambda j, sc: (j, 0, 0, 0))
    shares = SD((4, 4, half, part), BF)
    return pl.pallas_call(
        functools.partial(mlp_kernel, k=k),
        grid_spec=pltpu.PrefetchScalarGridSpec(
            num_scalar_prefetch=1,
            grid=(2,),
            in_specs=[VM] * 3 + [ANY] * 8 + [VM] * len(old),
            out_specs=[VM] * 2
            + [by_up] * 2
            + [by_down] * 2
            + [pl.BlockSpec((2, 1, part), lambda j, sc: ((sc[0] >> 1) ^ j, 0, 0))],
            scratch_shapes=[
                pltpu.VMEM((2, width, width), BF),
                pltpu.VMEM((2, width, width), BF),
                pltpu.SemaphoreType.DMA((24,)),
            ],
        ),
        out_shape=[SD((rows, width), F32)] * 2 + [shares] * 4 + [SD((4, 1, part), F32)],
        input_output_aliases={12: 0, 13: 1} if old else {},
        compiler_params=params(30),
        cost_estimate=cost(26),
        name="mlp%d" % k,
    )(sc, h2, dm, sm, wup, wdown, *pieces, *old)


def after_kernel(sc, down, dh2, mid, cot, keep, sm, o, dm, own, *rest, slots):
    pieces = rest[:6]
    out, dmid, do, g_own, g_send, gs, wbuf, sems = rest[6:]
    images, count, width = cot.shape
    every = pl.ds(0, width)
    height = own.shape[0]
    copies = run_copies(
        place_rows(wbuf, sc, (own, every), pieces, every, pl.ds(width, width), height), sems
    )
    for c in copies:
        c.start()
    e0 = dh2[...]
    xhat, rsq = normalized(mid[...])
    gs[...] = jnp.zeros_like(gs)
    gs[1:2, :] = jnp.sum(e0 * xhat, axis=0, keepdims=True)
    gs[2:3, :] = jnp.sum(e0, axis=0, keepdims=True)
    gs[3:4, :] = jnp.sum(dm[...].astype(F32), axis=0, keepdims=True)
    dmid[...] = norm_back(e0 * sm[G2 : G2 + 1, :], xhat, rsq)
    for i in range(images):
        sl = slice(i * slots, i * slots + count)
        dmid[sl, :] += cot[i].astype(F32) * keep[sl, :]
        out[i] = (keep[sl, :] * (mid[sl, :] + down[sl, :] + sm[DB : DB + 1, :])).astype(BF)
    low = dmid[...].astype(BF)
    gs[0:1, :] = jnp.sum(low.astype(F32), axis=0, keepdims=True)
    for c in copies:
        c.wait()
    do[...] = dot(low, wbuf[...], 1, 1).astype(BF)
    gw = dot(o[...], low, 0, 0).astype(BF)
    half, part = height // 2, width // 2
    for m in range(4):
        for j in range(2):
            cols = slice(j * part, (j + 1) * part)
            at = m * height
            store_halves(
                sc[1],
                g_own,
                g_send,
                (sc[0] ^ m, j),
                gw[at : at + half, cols],
                gw[at + half : at + height, cols],
            )


def after_mlp(sc, down, dh2, mid, cot, keep, sm, o, dm, own, pieces, slots):
    rows, width = o.shape
    half, part = own.shape[0] // 2, width // 2
    full = lambda a: pl.BlockSpec(a.shape, lambda j, sc: (0,) * a.ndim)
    whole = pl.BlockSpec((rows, width), lambda j, sc: (0, 0))
    share = pl.BlockSpec((4, 2, half, part), lambda j, sc: (0, 3, 0, 0))
    return pl.pallas_call(
        functools.partial(after_kernel, slots=slots),
        grid_spec=pltpu.PrefetchScalarGridSpec(
            num_scalar_prefetch=1,
            grid=(1,),
            in_specs=[VM] * 8 + [ANY] * 7,
            out_specs=[VM] * 3 + [share] * 2 + [VM],
            scratch_shapes=[pltpu.VMEM((width, width), BF), pltpu.SemaphoreType.DMA((7,))],
        ),
        out_shape=[SD(cot.shape, BF), SD((rows, width), F32), SD((rows, width), BF)]
        + [SD((4, 8, half, part), BF)] * 2
        + [SD((8, width), F32)],
        compiler_params=params(24),
        cost_estimate=cost(15),
        name="after_mlp",
    )(sc, down, dh2, mid, cot, keep, sm, o, dm, own, *pieces)


def project_grad_kernel(sc, h1, dx, old_own, old_send, g_own, g_send, gs, *, height):
    half, part = height // 2, dx.shape[1] // 2
    low = dx[...]
    gs[0] = jnp.broadcast_to(jnp.sum(low.astype(F32), axis=0, keepdims=True), gs.shape[1:])
    gw = dot(h1[...], low, 0, 0).astype(BF)
    for m in range(4):
        for j in range(2):
            cols = slice(j * part, (j + 1) * part)
            at = m * height
            store_halves(
                sc[1],
                g_own,
                g_send,
                (sc[0] ^ m, j),
                gw[at : at + half, cols],
                gw[at + half : at + height, cols],
            )


def project_grad(sc, h1, dx, g_own, g_send, height):
    rows, width = h1.shape
    half, part = height // 2, width // 2
    share = pl.BlockSpec((4, 2, half, part), lambda j, sc: (0, j, 0, 0))
    return pl.pallas_call(
        functools.partial(project_grad_kernel, height=height),
        grid_spec=pltpu.PrefetchScalarGridSpec(
            num_scalar_prefetch=1,
            grid=(3,),
            in_specs=[
                VM,
                pl.BlockSpec((rows, width), lambda j, sc: (0, j)),
                ANY,
                ANY,
            ],
            out_specs=[share, share, pl.BlockSpec((1, 8, width), lambda j, sc: (j, 0, 0))],
        ),
        out_shape=[SD((4, 8, half, part), BF)] * 2 + [SD((3, 8, width), F32)],
        input_output_aliases={3: 0, 4: 1},
        compiler_params=params(20),
        cost_estimate=cost(10),
        name="project_grad",
    )(sc, h1, dx, g_own, g_send)


def tokens_grad_kernel(sc, dx, tok, sm, dmid, ga, gp, gu0, gu1, own, *rest, slots):
    pp, pq = rest[:6], rest[6:12]
    out, gs, wbuf, acc, sems = rest[12:]
    images, count, width = tok.shape
    height = own.shape[0]
    two, third = pl.ds(0, 2 * width), pl.ds(2 * width, width)
    pairs = place_rows(wbuf, sc, (own, two), pp, two, two, height)
    pairs += place_rows(wbuf, sc, (own, third), pq, third, pl.ds(0, width), height)
    copies = run_copies(pairs, sems)
    for c in copies:
        c.start()
    gs[...] = jnp.zeros_like(gs)
    gs[OB : OB + 4, :] = ga[0:4, :]
    gs[QB : QB + 1, :] = gp[0, 0:1, :]
    gs[VB : VB + 1, :] = gp[2, 0:1, :]
    for b in range(4):
        gs[UB + b : UB + b + 1, : width // 2] = gu0[b]
        gs[UB + b : UB + b + 1, width // 2 :] = gu1[b]
    for c in copies:
        c.wait()
    acc[...] = dot(dx[...], wbuf[...], 1, 1)
    gain = jnp.zeros((1, width), F32)
    shift = jnp.zeros((1, width), F32)
    for i in range(images):
        sl = slice(i * slots, i * slots + count)
        e0 = acc[sl, :]
        xhat, rsq = normalized(tok[i].astype(F32))
        gain += jnp.sum(e0 * xhat, axis=0, keepdims=True)
        shift += jnp.sum(e0, axis=0, keepdims=True)
        out[i] = (dmid[sl, :] + norm_back(e0 * sm[G1 : G1 + 1, :], xhat, rsq)).astype(BF)
    gs[G1 : G1 + 1, :] = gain
    gs[B1 : B1 + 1, :] = shift


def tokens_grad(sc, dx, tok, sm, dmid, ga, gp, gu0, gu1, own, pieces, slots):
    rows, width = dmid.shape
    full = lambda a: pl.BlockSpec(a.shape, lambda j, sc: (0,) * a.ndim)
    operands = (dx, tok, sm, dmid, ga, gp, gu0, gu1)
    return pl.pallas_call(
        functools.partial(tokens_grad_kernel, slots=slots),
        grid_spec=pltpu.PrefetchScalarGridSpec(
            num_scalar_prefetch=1,
            grid=(1,),
            in_specs=[VM] * len(operands) + [ANY] * 13,
            out_specs=[VM] * 2,
            scratch_shapes=[
                pltpu.VMEM((width, 3 * width), BF),
                pltpu.VMEM((rows, width), F32),
                pltpu.SemaphoreType.DMA((14,)),
            ],
        ),
        out_shape=[SD(tok.shape, BF), SD((16, width), F32)],
        compiler_params=params(24),
        cost_estimate=cost(13),
        name="tokens_grad",
    )(sc, *operands, own, *pieces)


def lay_kernel(sc, *refs, kind):
    core, odd = sc[1], sc[2] % 2
    ins, (wide, tall) = refs[:-2], refs[-2:]
    half, part = ins[0].shape[1:]

    def put(k, side, first, second):
        which = core if side == 0 else 1 - core
        rows = pl.ds(pl.multiple_of(which * half, 8), half)
        if kind == "mlp":
            for b in range(4):
                wide[rows, pl.ds((2 * b + k) * part, part)] = first[b].astype(F32)
            for i in range(2):
                at = pl.multiple_of(which * 2 * half + (k * 4 + i) * half, 8)
                for j in range(2):
                    tall[pl.ds(at, half), pl.ds(j * part, part)] = second[2 * i + j].astype(F32)
        else:
            for n in range(4):
                wide[rows, pl.ds(n * part, part)] = first[n].astype(F32)
            for n in range(2):
                wide[rows, pl.ds((4 + n) * part, part)] = second[n].astype(F32)
                tall[rows, pl.ds(n * part, part)] = second[2 + n].astype(F32)

    for k in range(len(ins) // 4):
        kept, other, skept, sother = ins[4 * k : 4 * k + 4]

        @pl.when(odd == 0)
        def _(k=k, kept=kept, other=other, skept=skept, sother=sother):
            put(k, 0, kept, other)
            put(k, 1, skept, sother)

        @pl.when(odd != 0)
        def _(k=k, kept=kept, other=other, skept=skept, sother=sother):
            put(k, 0, other, kept)
            put(k, 1, sother, skept)


def lay_out(sc, finals, kind, shapes):
    full = lambda s: pl.BlockSpec(s, lambda j, sc: (0,) * len(s))
    flat = [a for group in finals for a in group]
    return pl.pallas_call(
        functools.partial(lay_kernel, kind=kind),
        grid_spec=pltpu.PrefetchScalarGridSpec(
            num_scalar_prefetch=1,
            grid=(1,),
            in_specs=[VM] * len(flat),
            out_specs=[VM] * 2,
        ),
        out_shape=[SD(s, F32) for s in shapes],
        compiler_params=params(8),
        cost_estimate=cost(4),
        name="lay_" + kind,
    )(sc, *flat)


def hops():
    def table(move):
        pairs = []
        for dp in range(8):
            for fs in range(4):
                z, core, shard = move(dp // 2, dp % 2, fs)
                pairs.append((dp * 4 + fs, (z * 2 + core) * 4 + shard))
        return pairs

    moves = {
        "sib": lambda z, c, f: (z, 1 - c, f),
        "x": lambda z, c, f: (z, c, f ^ 1),
        "y": lambda z, c, f: (z, c, f ^ 2),
        "xy": lambda z, c, f: (z, c, f ^ 3),
        "z1": lambda z, c, f: (z ^ 1, c, f),
        "z2": lambda z, c, f: (z ^ 2, c, f),
        "z3": lambda z, c, f: (z ^ 3, c, f),
    }
    tables = {name: table(move) for name, move in moves.items()}
    return lambda value, name: lax.ppermute(value, ("dp", "fsdp"), tables[name])


class Transfer:
    def __init__(self, stages):
        self.stages = stages
        self.flying = next(stages)
        self.result = None

    def step(self, landed):
        try:
            self.flying = self.stages.send(landed)
        except StopIteration as end:
            self.flying, self.result = (), end.value


def advance(held, *transfers):
    values = lax.optimization_barrier((held, tuple(t.flying for t in transfers)))
    for t, landed in zip(transfers, values[1]):
        t.step(landed)
    return values[0]


def follow(lead, *transfers):
    landed = lax.optimization_barrier(tuple(lead.flying))
    lead.step(landed)
    values = lax.optimization_barrier((landed, tuple(t.flying for t in transfers)))
    for t, got in zip(transfers, values[1]):
        t.step(got)


PLANE = ("x", "y", "xy")
LINE = ("z1", "z2", "z3")


def gather_stages(hop, own):
    far = yield tuple(hop(own, name) for name in PLANE)
    near = yield tuple(hop(a, "sib") for a in far)
    return tuple(far) + tuple(near)


def small_stages(hop, own):
    return (own,) + tuple((yield tuple(hop(own, name) for name in PLANE)))


def add(a, b):
    return (a.astype(F32) + b.astype(F32)).astype(BF)


def line_stages(hop, even, total):
    parts = total.shape[0] // 2
    keep = jnp.where(even, total[:parts], total[parts:])
    give = jnp.where(even, total[parts:], total[:parts]).astype(BF)
    (got,) = yield (hop(give, "z1"),)
    half = lax.optimization_barrier((keep + got.astype(F32)).astype(BF))
    (got,) = yield (hop(half, "z2"),)
    kept = add(half, got)
    other, skept = yield (hop(kept, "z1"), hop(kept, "sib"))
    (sother,) = yield (hop(other, "sib"),)
    return kept, other, skept, sother


def plane_stages(hop, even, chip):
    got = yield tuple(hop(chip(r).astype(BF), name) for r, name in enumerate(PLANE, 1))
    total = chip(0)
    for a in got:
        total = total + a.astype(F32)
    return (yield from line_stages(hop, even, total))


def ffn_stages(hop, even, up_own, up_send, dn_own, dn_send):
    up_got, dn_got = yield (hop(up_send, "sib"), hop(dn_send, "sib"))

    def chip(r):
        return jnp.concatenate(
            [
                up_own[r].astype(F32) + up_got[r].astype(F32),
                dn_own[r].astype(F32) + dn_got[r].astype(F32),
            ]
        )

    return (yield from plane_stages(hop, even, chip))


def attn_stages(hop, even, own, send):
    (got,) = yield (hop(send, "sib"),)
    chip = lambda r: own[r].astype(F32) + got[r].astype(F32)
    return (yield from plane_stages(hop, even, chip))


def sum_stages(hop, value):
    (got,) = yield (hop(value, "sib"),)
    value = value + got
    for names in (PLANE, LINE):
        one, two, three = yield tuple(hop(value, name) for name in names)
        value = (value + one) + (two + three)
    return value


def on_device_fast(
    tokens,
    mask,
    cotangent,
    ln1_gain,
    ln1_bias,
    w_qkv,
    qv_bias,
    w_out,
    out_bias,
    ln2_gain,
    ln2_bias,
    w_up,
    up_bias,
    w_down,
    down_bias,
):
    images, count, width = tokens.shape
    slots = -(-count // 8) * 8
    height = w_out.shape[0]
    half, part = height // 2, width // 2
    hop = hops()
    shard = lax.axis_index("fsdp")
    dp = lax.axis_index("dp")
    sc = jnp.stack([shard, dp % 2, dp // 2]).astype(jnp.int32)
    even = (dp // 2) % 2 == 0

    tie = lax.optimization_barrier
    small = (ln1_gain, ln1_bias, qv_bias, out_bias, ln2_gain, ln2_bias, down_bias, up_bias)
    top, bottom = pack_attn(sc, w_qkv, w_out, small)
    px, py, qx, qy = hop(top, "x"), hop(top, "y"), hop(bottom, "x"), hop(bottom, "y")
    own0, own1 = pack(sc, pack_ffn_kernel, 10, [(2 * height, width)] * 2, w_up, w_down)
    px, py, qx, qy, own0, own1 = tie((px, py, qx, qy, own0, own1))
    pfar, qfar = hop(px, "y"), hop(qy, "x")
    near = tuple(hop(a, "sib") for a in (px, py, qx, qy))
    pfar, qfar, near, own0, own1 = tie((pfar, qfar, near, own0, own1))
    spfar, sqfar = hop(pfar, "sib"), hop(qfar, "sib")
    ffn0 = Transfer(gather_stages(hop, own0))
    sc, spfar, sqfar = tie((sc, spfar, sqfar))
    pieces_p = (px, py, pfar, near[0], near[1], spfar)
    pieces_q = (qx, qy, qfar, near[2], near[3], sqfar)
    pieces = pieces_p + pieces_q

    keep = jnp.pad(mask.astype(F32), ((0, 0), (0, slots - count)))
    mask_row = keep.reshape(images, 1, slots)
    keep_col = keep.reshape(images * slots, 1)

    h1, qkv, sm = project(sc, tokens, w_qkv, top, pieces, slots)
    o = attend(qkv, mask_row, slots)
    o, own1 = tie((o, own1))
    ffn1 = Transfer(gather_stages(hop, own1))
    mid, h2, dm = middle_part(sc, tokens, o, sm, cotangent, keep_col, w_out, pieces_q, slots)
    h2 = advance(h2, ffn0)
    sc = advance(sc, ffn0)
    down, dh2, *shares, gu0 = mlp_part(sc, h2, dm, sm, w_up, w_down, ffn0.result, 0, ())
    down, dh2, *shares = advance((down, dh2, *shares), ffn1)
    m0 = Transfer(ffn_stages(hop, even, *shares))
    sc = advance(sc, ffn1, m0)
    down, dh2, *shares, gu1 = mlp_part(
        sc, h2, dm, sm, w_up, w_down, ffn1.result, 1, (down, dh2)
    )
    down, dh2, *shares = advance((down, dh2, *shares), m0)
    m1 = Transfer(ffn_stages(hop, even, *shares))
    layer_out, dmid, do, g_own, g_send, ga = after_mlp(
        sc, down, dh2, mid, cotangent, keep_col, sm, o, dm, w_out, pieces_q, slots
    )
    do = advance(do, m0, m1)
    dx = attend_back(qkv, do, keep_col, slots)
    dx = advance(dx, m0)
    g_own, g_send, gp = project_grad(sc, h1, dx, g_own, g_send, height)
    g_own, g_send, dx = advance((g_own, g_send, dx), m0, m1)
    attn = Transfer(attn_stages(hop, even, g_own, g_send))
    sc = advance(sc, attn)
    sc = advance(sc, m1)
    grad_tokens, gs = tokens_grad(
        sc, dx, tokens, sm, dmid, ga, gp, gu0, gu1, w_qkv, pieces, slots
    )
    gs = advance(gs, m0, m1, attn)
    total = Transfer(sum_stages(hop, gs))
    advance((), total)
    follow(attn, m1, total)
    ffn = advance((), m1)
    ffn = lay_out(
        sc, (m0.result, m1.result), "mlp", ((height, 4 * width), (4 * height, width))
    )
    follow(attn, total)
    gs = total.result

    def mine(r, n=1):
        return lax.dynamic_slice(gs[r : r + n].reshape(-1), (shard * (n * height),), (n * height,))

    rows = tuple(mine(r) for r in (G1, B1, OB, G2, B2, DB)) + (mine(QB, 2), mine(UB, 4))
    while attn.flying:
        ffn, rows = advance((ffn, rows), attn)
    g1, b1, ob, g2, b2, db, qvb, ub = rows
    grad_w_up, grad_w_down = ffn
    grad_w_qkv, grad_w_out = lay_out(
        sc, (attn.result,), "attn", ((height, 3 * width), (height, width))
    )
    return (
        layer_out,
        grad_tokens,
        g1,
        b1,
        grad_w_qkv,
        qvb,
        grad_w_out,
        ob,
        g2,
        b2,
        grad_w_up,
        ub,
        grad_w_down,
        db,
    )


def norm(values, gain, shift):
    mean_value = jnp.mean(values, axis=-1, keepdims=True)
    centred = values - mean_value
    variance = jnp.mean(centred * centred, axis=-1, keepdims=True)
    return centred * lax.rsqrt(variance + EPS) * gain + shift


def gelu_exact(values):
    return jax.nn.gelu(values, approximate=False)


def score_block(query, key_part, valid):
    scores = jnp.einsum(
        "iqhe,ikhe->ihqk", query, key_part, preferred_element_type=jnp.float32
    ) * HD ** (-0.5)
    return jnp.where(valid, scores, -1e30)


def arrange(grad, groups, copies):
    shaped = grad.reshape((groups, copies, grad.shape[0] // (groups * copies)) + grad.shape[1:])
    return jnp.swapaxes(shaped, 0, 1).reshape(grad.shape)


def reduce_six(grad_one, grad_two, grad_three, grad_four, grad_five, grad_six):
    groups = lax.axis_size("fsdp")
    copies = lax.axis_size("dp")
    pieces = (
        lax.psum_scatter(
            arrange(grad_one, groups, copies), ("dp", "fsdp"), scatter_dimension=0, tiled=True
        ),
        lax.psum_scatter(
            arrange(grad_two, groups, copies), ("dp", "fsdp"), scatter_dimension=0, tiled=True
        ),
        lax.psum_scatter(
            arrange(grad_three, groups, copies), ("dp", "fsdp"), scatter_dimension=0, tiled=True
        ),
        lax.psum_scatter(
            arrange(grad_four, groups, copies), ("dp", "fsdp"), scatter_dimension=0, tiled=True
        ),
        lax.psum_scatter(
            arrange(grad_five, groups, copies), ("dp", "fsdp"), scatter_dimension=0, tiled=True
        ),
        lax.psum_scatter(
            arrange(grad_six, groups, copies), ("dp", "fsdp"), scatter_dimension=0, tiled=True
        ),
    )
    return (
        lax.all_gather(pieces[0].astype(jnp.bfloat16), "dp", axis=0, tiled=True).astype(
            jnp.float32
        ),
        lax.all_gather(pieces[1].astype(jnp.bfloat16), "dp", axis=0, tiled=True).astype(
            jnp.float32
        ),
        lax.all_gather(pieces[2].astype(jnp.bfloat16), "dp", axis=0, tiled=True).astype(
            jnp.float32
        ),
        lax.all_gather(pieces[3].astype(jnp.bfloat16), "dp", axis=0, tiled=True).astype(
            jnp.float32
        ),
        lax.all_gather(pieces[4].astype(jnp.bfloat16), "dp", axis=0, tiled=True).astype(
            jnp.float32
        ),
        lax.all_gather(pieces[5].astype(jnp.bfloat16), "dp", axis=0, tiled=True).astype(
            jnp.float32
        ),
    )


def on_device(
    tokens,
    mask,
    cotangent,
    ln1_gain,
    ln1_bias,
    w_qkv,
    qv_bias,
    w_out,
    out_bias,
    ln2_gain,
    ln2_bias,
    w_up,
    up_bias,
    w_down,
    down_bias,
):
    image_count, slot_count, width = tokens.shape
    row_count = image_count * slot_count
    heads = width // HD
    scale = HD ** (-0.5)
    attn_full = (
        lax.all_gather(ln1_gain, "fsdp", axis=0, tiled=True),
        lax.all_gather(ln1_bias, "fsdp", axis=0, tiled=True),
        lax.all_gather(w_qkv, "fsdp", axis=0, tiled=True),
        lax.all_gather(qv_bias, "fsdp", axis=0, tiled=True),
        lax.all_gather(w_out, "fsdp", axis=0, tiled=True),
        lax.all_gather(out_bias, "fsdp", axis=0, tiled=True),
    )
    mlp_full = (
        lax.all_gather(ln2_gain, "fsdp", axis=0, tiled=True),
        lax.all_gather(ln2_bias, "fsdp", axis=0, tiled=True),
        lax.all_gather(w_up, "fsdp", axis=0, tiled=True),
        lax.all_gather(up_bias, "fsdp", axis=0, tiled=True),
        lax.all_gather(w_down, "fsdp", axis=0, tiled=True),
        lax.all_gather(down_bias, "fsdp", axis=0, tiled=True),
    )
    gain_one, shift_one, qkv_weight, qkv_shift, out_weight, out_shift = attn_full
    gain_two, shift_two, up_weight, up_shift, down_weight, down_shift = mlp_full
    keep = mask.astype(jnp.float32)
    valid = (keep > 0.5)[:, None, None, :]
    keep_rows = keep.reshape(row_count, 1)
    inputs = tokens.astype(jnp.float32).reshape(row_count, width)
    normed_one, norm_one_back = jax.vjp(
        norm, inputs, gain_one.astype(jnp.float32), shift_one.astype(jnp.float32)
    )
    normed_low = normed_one.astype(jnp.bfloat16)
    qv_float = qkv_shift.astype(jnp.float32)
    full_bias = jnp.concatenate(
        [qv_float[:width], jnp.zeros((width,), jnp.float32), qv_float[width:]]
    )
    projected = (
        jnp.dot(normed_low, qkv_weight, preferred_element_type=jnp.float32) + full_bias
    ).astype(jnp.bfloat16)
    query = projected[:, :width].reshape(image_count, slot_count, heads, HD)
    key_part = projected[:, width : 2 * width].reshape(image_count, slot_count, heads, HD)
    value = projected[:, 2 * width :].reshape(image_count, slot_count, heads, HD)
    scores = score_block(query, key_part, valid)
    top = jnp.max(scores, axis=-1, keepdims=True)
    lse = top + jnp.log(jnp.sum(jnp.exp(scores - top), axis=-1, keepdims=True))
    probs_low = jnp.exp(scores - lse).astype(jnp.bfloat16)
    mixed = jnp.einsum("ihqk,ikhe->iqhe", probs_low, value, preferred_element_type=jnp.float32)
    mixed = mixed.reshape(row_count, width).astype(jnp.bfloat16)
    middle = (
        inputs
        + jnp.dot(mixed, out_weight, preferred_element_type=jnp.float32)
        + out_shift.astype(jnp.float32)
    )
    normed_two, norm_two_back = jax.vjp(
        norm, middle, gain_two.astype(jnp.float32), shift_two.astype(jnp.float32)
    )
    normed_two_low = normed_two.astype(jnp.bfloat16)
    upward = jnp.dot(
        normed_two_low, up_weight, preferred_element_type=jnp.float32
    ) + up_shift.astype(jnp.float32)
    active, gelu_back = jax.vjp(gelu_exact, upward)
    active_low = active.astype(jnp.bfloat16)
    downward = jnp.dot(
        active_low, down_weight, preferred_element_type=jnp.float32
    ) + down_shift.astype(jnp.float32)
    layer_out = (
        (keep_rows * (middle + downward))
        .astype(jnp.bfloat16)
        .reshape(image_count, slot_count, width)
    )
    mlp_back = (
        lax.all_gather(ln2_gain, "fsdp", axis=0, tiled=True),
        lax.all_gather(ln2_bias, "fsdp", axis=0, tiled=True),
        lax.all_gather(w_up, "fsdp", axis=0, tiled=True),
        lax.all_gather(up_bias, "fsdp", axis=0, tiled=True),
        lax.all_gather(w_down, "fsdp", axis=0, tiled=True),
        lax.all_gather(down_bias, "fsdp", axis=0, tiled=True),
    )
    up_back = mlp_back[2]
    down_back = mlp_back[4]
    grad_rows = cotangent.astype(jnp.float32).reshape(row_count, width) * keep_rows
    grad_down_low = grad_rows.astype(jnp.bfloat16)
    grad_w_down = jnp.einsum(
        "rf,rd->fd", active_low, grad_down_low, preferred_element_type=jnp.float32
    )
    grad_down_bias = jnp.sum(grad_down_low, axis=0, dtype=jnp.float32)
    grad_active = jnp.einsum(
        "rd,fd->rf", grad_down_low, down_back, preferred_element_type=jnp.float32
    )
    grad_up_low = gelu_back(grad_active)[0].astype(jnp.bfloat16)
    grad_w_up = jnp.einsum(
        "rd,rf->df", normed_two_low, grad_up_low, preferred_element_type=jnp.float32
    )
    grad_up_bias = jnp.sum(grad_up_low, axis=0, dtype=jnp.float32)
    grad_normed_two = jnp.einsum(
        "rf,df->rd", grad_up_low, up_back, preferred_element_type=jnp.float32
    )
    grad_mid_norm, grad_ln2_gain, grad_ln2_bias = norm_two_back(grad_normed_two)
    grad_middle = grad_rows + grad_mid_norm
    mlp_grads = reduce_six(
        grad_ln2_gain, grad_ln2_bias, grad_w_up, grad_up_bias, grad_w_down, grad_down_bias
    )
    attn_back = (
        lax.all_gather(ln1_gain, "fsdp", axis=0, tiled=True),
        lax.all_gather(ln1_bias, "fsdp", axis=0, tiled=True),
        lax.all_gather(w_qkv, "fsdp", axis=0, tiled=True),
        lax.all_gather(qv_bias, "fsdp", axis=0, tiled=True),
        lax.all_gather(w_out, "fsdp", axis=0, tiled=True),
        lax.all_gather(out_bias, "fsdp", axis=0, tiled=True),
    )
    qkv_back = attn_back[2]
    out_back = attn_back[4]
    grad_attn_low = grad_middle.astype(jnp.bfloat16)
    grad_w_out = jnp.einsum("rd,re->de", mixed, grad_attn_low, preferred_element_type=jnp.float32)
    grad_out_bias = jnp.sum(grad_attn_low, axis=0, dtype=jnp.float32)
    grad_mixed = jnp.einsum(
        "re,de->rd", grad_attn_low, out_back, preferred_element_type=jnp.float32
    )
    grad_mixed = grad_mixed.astype(jnp.bfloat16).reshape(image_count, slot_count, heads, HD)
    probs = jnp.exp(score_block(query, key_part, valid) - lse)
    probs_again = probs.astype(jnp.bfloat16)
    grad_value = jnp.einsum(
        "ihqk,iqhe->ikhe", probs_again, grad_mixed, preferred_element_type=jnp.float32
    )
    grad_probs = jnp.einsum(
        "iqhe,ikhe->ihqk", grad_mixed, value, preferred_element_type=jnp.float32
    )
    inner = jnp.sum(grad_probs * probs, axis=-1, keepdims=True)
    grad_scores = (probs * (grad_probs - inner)).astype(jnp.bfloat16)
    grad_query = (
        jnp.einsum("ihqk,ikhe->iqhe", grad_scores, key_part, preferred_element_type=jnp.float32)
        * scale
    )
    grad_key = (
        jnp.einsum("ihqk,iqhe->ikhe", grad_scores, query, preferred_element_type=jnp.float32)
        * scale
    )
    grad_projected = jnp.concatenate(
        [
            grad_query.reshape(row_count, width),
            grad_key.reshape(row_count, width),
            grad_value.reshape(row_count, width),
        ],
        axis=1,
    ).astype(jnp.bfloat16)
    grad_w_qkv = jnp.einsum(
        "rd,re->de", normed_low, grad_projected, preferred_element_type=jnp.float32
    )
    grad_qv_bias = jnp.concatenate(
        [
            jnp.sum(grad_projected[:, :width], axis=0, dtype=jnp.float32),
            jnp.sum(grad_projected[:, 2 * width :], axis=0, dtype=jnp.float32),
        ]
    )
    grad_normed_one = jnp.einsum(
        "re,de->rd", grad_projected, qkv_back, preferred_element_type=jnp.float32
    )
    grad_in_norm, grad_ln1_gain, grad_ln1_bias = norm_one_back(grad_normed_one)
    grad_tokens = (
        (grad_middle + grad_in_norm).astype(jnp.bfloat16).reshape(image_count, slot_count, width)
    )
    attn_grads = reduce_six(
        grad_ln1_gain, grad_ln1_bias, grad_w_qkv, grad_qv_bias, grad_w_out, grad_out_bias
    )
    return (
        layer_out,
        grad_tokens,
        attn_grads[0],
        attn_grads[1],
        attn_grads[2],
        attn_grads[3],
        attn_grads[4],
        attn_grads[5],
        mlp_grads[0],
        mlp_grads[1],
        mlp_grads[2],
        mlp_grads[3],
        mlp_grads[4],
        mlp_grads[5],
    )


def solution(mesh):
    in_specs = (
        P(("dp", "fsdp"), None, None),
        P(("dp", "fsdp"), None),
        P(("dp", "fsdp"), None, None),
        P("fsdp"),
        P("fsdp"),
        P("fsdp", None),
        P("fsdp"),
        P("fsdp", None),
        P("fsdp"),
        P("fsdp"),
        P("fsdp"),
        P("fsdp", None),
        P("fsdp"),
        P("fsdp", None),
        P("fsdp"),
    )
    out_specs = (
        P(("dp", "fsdp"), None, None),
        P(("dp", "fsdp"), None, None),
        P("fsdp"),
        P("fsdp"),
        P("fsdp", None),
        P("fsdp"),
        P("fsdp", None),
        P("fsdp"),
        P("fsdp"),
        P("fsdp"),
        P("fsdp", None),
        P("fsdp"),
        P("fsdp", None),
        P("fsdp"),
    )
    fast = dict(mesh.shape) == {"dp": 8, "fsdp": 4}
    return jax.shard_map(
        on_device_fast if fast else on_device, mesh=mesh, in_specs=in_specs, out_specs=out_specs, check_vma=False
    )
```

```python
import functools

import jax
import jax.numpy as jnp
import numpy as np
from jax import lax
from jax.experimental import pallas as pl
from jax.experimental.pallas import tpu as pltpu
from jax.sharding import PartitionSpec as P

HD = 64
EPS = 1e-06
F32 = jnp.float32
BF = jnp.bfloat16
MB = 2**20
SCORE_SCALE = np.float32(np.log2(np.e) * HD ** (-0.5))
MASKED = np.float32(-1e30)
SD = jax.ShapeDtypeStruct
ANY = pl.BlockSpec(memory_space=pl.ANY)
VM = pl.BlockSpec(memory_space=pltpu.VMEM)


def dot(a, b, ca, cb):
    return lax.dot_general(a, b, (((ca,), (cb,)), ((), ())), preferred_element_type=F32)


def params(mb=58):
    return pltpu.CompilerParams(vmem_limit_bytes=mb * MB)


def cost(micros):
    return pl.CostEstimate(flops=int(micros * 1.15e9), bytes_accessed=0, transcendentals=0)


def normalized(values):
    mean = jnp.mean(values, axis=-1, keepdims=True)
    centred = values - mean
    rsq = lax.rsqrt(jnp.mean(centred * centred, axis=-1, keepdims=True) + EPS)
    return centred * rsq, rsq


def norm_back(e, xhat, rsq):
    return rsq * (
        e
        - jnp.mean(e, axis=-1, keepdims=True)
        - xhat * jnp.mean(e * xhat, axis=-1, keepdims=True)
    )


def run_copies(pairs, sems, base=0):
    copies = [
        pltpu.make_async_copy(src, dst, sems.at[base + n]) for n, (src, dst) in enumerate(pairs)
    ]
    return copies


PACK_MB = 54

G1, B1, QB, VB, OB, G2, B2, DB, UB = range(9)


def all_copies(pairs, sems):
    copies = run_copies(pairs, sems)
    for c in copies:
        c.start()
    for c in copies:
        c.wait()


def pack_attn_kernel(sc, wqkv, wout, *rest):
    small, (top, bottom, table, sems) = rest[:8], rest[8:]
    height, width = wout.shape
    half = height // 2
    rows = pl.ds(pl.multiple_of(sc[1] * half, 16), half)
    copies = run_copies(
        [
            (wqkv.at[rows, pl.ds(0, 2 * width)], top.at[pl.ds(0, half), :]),
            (wqkv.at[rows, pl.ds(2 * width, width)], bottom.at[:, pl.ds(0, width)]),
            (wout.at[rows, :], bottom.at[:, pl.ds(width, width)]),
        ],
        sems,
    )
    for c in copies:
        c.start()
    table[...] = jnp.zeros_like(table)
    row = 0
    for ref in small:
        values = ref[...].astype(F32)
        for n in range(ref.shape[0] // height):
            table[row : row + 1, :height] = values[n * height : (n + 1) * height].reshape(1, height)
            row += 1
    top[half:, : table.shape[1]] = table[...].astype(BF)
    for c in copies:
        c.wait()


def pack_attn(sc, wqkv, wout, small):
    height, width = wout.shape
    lanes = -(-height // 128) * 128
    return pl.pallas_call(
        pack_attn_kernel,
        grid_spec=pltpu.PrefetchScalarGridSpec(
            num_scalar_prefetch=1,
            in_specs=[ANY] * 2 + [VM] * 8,
            out_specs=[VM] * 2,
            scratch_shapes=[pltpu.VMEM((16, lanes), F32), pltpu.SemaphoreType.DMA((3,))],
        ),
        out_shape=[SD((height // 2 + 16, 2 * width), BF), SD((height // 2, 2 * width), BF)],
        compiler_params=params(PACK_MB),
        name="pack_attn",
    )(sc, wqkv, wout, *small)


def pack_ffn_kernel(sc, wup, wdown, ffn0, ffn1, sems):
    width = wdown.shape[1]
    half, part = wup.shape[0] // 2, wdown.shape[0] // 2
    rows = pl.ds(pl.multiple_of(sc[1] * half, 16), half)
    pairs = []
    for k, ffn in enumerate((ffn0, ffn1)):
        for g in range(2):
            for h in range(2):
                block = 2 * ((sc[0] >> 1) ^ g) + h
                at = pl.multiple_of(block * width + k * part, 128)
                pairs.append(
                    (
                        wup.at[rows, pl.ds(at, part)],
                        ffn.at[pl.ds(g * half, half), pl.ds(h * part, part)],
                    )
                )
        at = pl.multiple_of(k * part + sc[1] * (part // 2), 16)
        pairs.append((wdown.at[pl.ds(at, part // 2), :], ffn.at[pl.ds(2 * half, part // 2), :]))
    all_copies(pairs, sems)


def pack(sc, kernel, copies, shapes, *weights):
    return pl.pallas_call(
        kernel,
        grid_spec=pltpu.PrefetchScalarGridSpec(
            num_scalar_prefetch=1,
            in_specs=[ANY] * len(weights),
            out_specs=[ANY] * len(shapes),
            scratch_shapes=[pltpu.SemaphoreType.DMA((copies,))],
        ),
        out_shape=[SD(shape, BF) for shape in shapes],
        compiler_params=params(2),
        name="pack",
    )(sc, *weights)


def place_rows(dst, sc, own, pieces, cols, src_cols, height, base=0):
    half = height // 2
    shard, core = sc[0], sc[1]
    pairs = []
    if own is not None:
        src, take = own
        pairs.append((src.at[:, take], dst.at[pl.ds(pl.multiple_of(shard * height, 16), height), cols]))
    for side in range(2):
        which = core if side == 0 else 1 - core
        for r in range(1, 4):
            at = pl.multiple_of((shard ^ r) * height + which * half, 16)
            pairs.append(
                (
                    pieces[side * 3 + r - 1].at[pl.ds(base * half, half), src_cols],
                    dst.at[pl.ds(at, half), cols],
                )
            )
    return pairs


def fill_small(sc, pieces, sm, height):
    shard = sc[0]
    vals = [pieces[r].astype(F32) for r in range(4)]

    def of(j):
        got = vals[3]
        for r in range(3):
            got = jnp.where(shard == (j ^ r), vals[r], got)
        return got[:, :height]

    by = [of(j) for j in range(4)]
    sm[...] = jnp.zeros_like(sm)
    for j in range(4):
        cols = slice(j * height, (j + 1) * height)
        sm[G1 : B1 + 1, cols] = by[j][0:2]
        sm[OB : DB + 1, cols] = by[j][4:8]
        for n in range(2):
            at = (2 * j + n) % 4 * height
            row = QB if j < 2 else VB
            sm[row : row + 1, at : at + height] = by[j][2 + n : 3 + n]
        for n in range(4):
            sm[UB + j : UB + j + 1, n * height : (n + 1) * height] = by[j][8 + n : 9 + n]


def project_kernel(sc, tok, own, packed, *rest, slots):
    pp, pq = rest[:6], rest[6:12]
    h1, qkv, sm, wbuf, small, sems = rest[12:]
    images, count, width = tok.shape
    height = own.shape[0]
    step = pl.program_id(0)
    two = pl.ds(0, 2 * width)
    third = pl.ds(2 * width, width)
    first = run_copies(place_rows(wbuf, sc, (own, two), pp, two, two, height), sems)
    last = run_copies(
        place_rows(wbuf, sc, (own, third), pq, third, pl.ds(0, width), height),
        sems,
        len(first),
    )

    corner = (pl.ds(height // 2, 16), pl.ds(0, small.shape[2]))
    table = run_copies(
        [
            (ref.at[corner[0], corner[1]], small.at[r])
            for r, ref in enumerate((packed,) + pp[:3])
        ],
        sems,
        len(first) + len(last),
    )

    @pl.when(step == 0)
    def _():
        for c in table + first + last:
            c.start()
        for c in table:
            c.wait()
        fill_small(sc, small, sm, height)
        for i in range(images):
            xhat, _ = normalized(tok[i].astype(F32))
            low = (xhat * sm[G1 : G1 + 1, :] + sm[B1 : B1 + 1, :]).astype(BF)
            tail = count // 8 * 8
            h1[i * slots + tail : (i + 1) * slots, :] = jnp.zeros((slots - tail, width), BF)
            h1[i * slots : i * slots + count, :] = low
        for c in first:
            c.wait()

    @pl.when(step == 2)
    def _():
        for c in last:
            c.wait()

    row = jnp.where(step == 0, sm[QB : QB + 1, :], sm[VB : VB + 1, :])
    row = jnp.where(step == 1, jnp.zeros_like(row), row)
    weight = wbuf[:, pl.ds(pl.multiple_of(step * width, 128), width)]
    qkv[...] = (dot(h1[...], weight, 1, 0) + row).astype(BF)


def project(sc, tok, own, packed, pieces, slots):
    images, _, width = tok.shape
    rows = images * slots
    full = lambda *s: pl.BlockSpec(s, lambda j, sc: (0,) * len(s))
    return pl.pallas_call(
        functools.partial(project_kernel, slots=slots),
        grid_spec=pltpu.PrefetchScalarGridSpec(
            num_scalar_prefetch=1,
            grid=(3,),
            in_specs=[VM] + [ANY] * 14,
            out_specs=[
                VM,
                pl.BlockSpec((rows, width), lambda j, sc: (0, j)),
                VM,
            ],
            scratch_shapes=[
                pltpu.VMEM((width, 3 * width), BF),
                pltpu.VMEM((4, 16, -(-own.shape[0] // 128) * 128), BF),
                pltpu.SemaphoreType.DMA((18,)),
            ],
        ),
        out_shape=[SD((rows, width), BF), SD((rows, 3 * width), BF), SD((16, width), F32)],
        compiler_params=params(54),
        cost_estimate=cost(10),
        name="project",
    )(sc, tok, own, packed, *pieces)


def head_lanes():
    return lax.broadcasted_iota(jnp.int32, (1, 2 * HD), 1) < HD


def attend_kernel(q, k, v, mask, o, *, pairs):
    low_half = head_lanes()
    keep = mask[0] > 0
    zero = jnp.zeros((), BF)
    for p in range(pairs):
        sl = slice(p * 2 * HD, (p + 1) * 2 * HD)
        qp, kp, vp = q[:, sl], k[:, sl], v[:, sl]
        outs = []
        for a in range(2):
            mine = low_half if a == 0 else jnp.logical_not(low_half)
            s = dot(jnp.where(mine, qp, zero), kp, 1, 1)
            s = jnp.where(keep, s * SCORE_SCALE, MASKED)
            e = jnp.exp2(s - jnp.max(s, axis=-1, keepdims=True))
            prob = (e * (1.0 / jnp.sum(e, axis=-1, keepdims=True))).astype(BF)
            outs.append(dot(prob, jnp.where(mine, vp, zero), 1, 0))
        o[:, sl] = (outs[0] + outs[1]).astype(BF)


def attend(qkv, mask_row, slots):
    rows, three = qkv.shape
    width, images = three // 3, rows // slots
    block = lambda n: pl.BlockSpec((slots, width), lambda i: (i, n))
    return pl.pallas_call(
        functools.partial(attend_kernel, pairs=width // (2 * HD)),
        grid=(images,),
        in_specs=[block(0), block(1), block(2), pl.BlockSpec((1, 1, slots), lambda i: (i, 0, 0))],
        out_specs=block(0),
        out_shape=SD((rows, width), BF),
        compiler_params=params(40),
        cost_estimate=cost(11),
        name="attend",
    )(qkv, qkv, qkv, mask_row)


def attend_back_kernel(q, k, v, do, mask, dx, *, pairs):
    low_half = head_lanes()
    keep = mask[...] > 0
    zero = jnp.zeros((), BF)
    scale = np.float32(HD ** (-0.5))
    wide = pairs * 2 * HD
    for p in range(pairs):
        sl = slice(p * 2 * HD, (p + 1) * 2 * HD)
        qp, kp, vp, dop = q[:, sl], k[:, sl], v[:, sl], do[:, sl]
        gq, gk, gv = [], [], []
        for a in range(2):
            mine = low_half if a == 0 else jnp.logical_not(low_half)
            qm, km, dm = (jnp.where(mine, t, zero) for t in (qp, kp, dop))
            s = dot(km, qp, 1, 1)
            s = jnp.where(keep, s * SCORE_SCALE, MASKED)
            e = jnp.exp2(s - jnp.max(s, axis=0, keepdims=True))
            prob = e * (1.0 / jnp.sum(e, axis=0, keepdims=True))
            gv.append(dot(prob.astype(BF), dm, 1, 0))
            weighed = prob * dot(vp, dm, 1, 1)
            inner = jnp.sum(weighed, axis=0, keepdims=True)
            ds = (weighed - prob * inner).astype(BF)
            gk.append(dot(ds, qm, 1, 0))
            gq.append(dot(ds, km, 0, 0))
        at = p * 2 * HD
        dx[:, at : at + 2 * HD] = ((gq[0] + gq[1]) * scale).astype(BF)
        dx[:, wide + at : wide + at + 2 * HD] = ((gk[0] + gk[1]) * scale).astype(BF)
        dx[:, 2 * wide + at : 2 * wide + at + 2 * HD] = (gv[0] + gv[1]).astype(BF)


def attend_back(qkv, do, mask_col, slots):
    rows, three = qkv.shape
    width, images = three // 3, rows // slots
    block = lambda n: pl.BlockSpec((slots, width), lambda i: (i, n))
    return pl.pallas_call(
        functools.partial(attend_back_kernel, pairs=width // (2 * HD)),
        grid=(images,),
        in_specs=[block(0), block(1), block(2), block(0), pl.BlockSpec((slots, 1), lambda i: (i, 0))],
        out_specs=pl.BlockSpec((slots, 3 * width), lambda i: (i, 0)),
        out_shape=SD((rows, 3 * width), BF),
        compiler_params=params(16),
        cost_estimate=cost(20),
        name="attend_back",
    )(qkv, qkv, qkv, do, mask_col)


def middle_kernel(sc, tok, o, sm, cot, keep, own, *rest, slots):
    pieces = rest[:6]
    mid, h2, dm, wbuf, sems = rest[6:]
    images, count, width = tok.shape
    every = pl.ds(0, width)
    copies = run_copies(
        place_rows(wbuf, sc, (own, every), pieces, every, pl.ds(width, width), own.shape[0]),
        sems,
    )
    for c in copies:
        c.start()
    tail = count // 8 * 8
    for i in range(images):
        sl = slice(i * slots, i * slots + count)
        dm[i * slots + tail : (i + 1) * slots, :] = jnp.zeros((slots - tail, width), BF)
        dm[sl, :] = (cot[i].astype(F32) * keep[sl, :]).astype(BF)
    for c in copies:
        c.wait()
    mid[...] = dot(o[...], wbuf[...], 1, 0) + sm[OB : OB + 1, :]
    for i in range(images):
        sl = slice(i * slots, i * slots + count)
        mid[sl, :] += tok[i].astype(F32)
    xhat, _ = normalized(mid[...])
    h2[...] = (xhat * sm[G2 : G2 + 1, :] + sm[B2 : B2 + 1, :]).astype(BF)


def middle_part(sc, tok, o, sm, cot, keep, own, pieces, slots):
    rows, width = o.shape
    full = lambda a: pl.BlockSpec(a.shape, lambda j, sc: (0,) * a.ndim)
    whole = pl.BlockSpec((rows, width), lambda j, sc: (0, 0))
    return pl.pallas_call(
        functools.partial(middle_kernel, slots=slots),
        grid_spec=pltpu.PrefetchScalarGridSpec(
            num_scalar_prefetch=1,
            grid=(1,),
            in_specs=[VM] * 5 + [ANY] * 7,
            out_specs=[VM] * 3,
            scratch_shapes=[pltpu.VMEM((width, width), BF), pltpu.SemaphoreType.DMA((7,))],
        ),
        out_shape=[SD((rows, width), F32), SD((rows, width), BF), SD((rows, width), BF)],
        compiler_params=params(16),
        cost_estimate=cost(9),
        name="middle",
    )(sc, tok, o, sm, cot, keep, own, *pieces)


def store_halves(core, own_ref, send_ref, index, first, second):
    @pl.when(core == 0)
    def _():
        own_ref[index] = first
        send_ref[index] = second

    @pl.when(core != 0)
    def _():
        own_ref[index] = second
        send_ref[index] = first


def mlp_kernel(sc, h2, dm, sm, wup, wdown, *rest, k):
    pieces, rest = rest[:6], rest[6:]
    if k:
        old_down, old_dh2 = rest[:2]
        rest = rest[2:]
    down, dh2, up_own, up_send, dn_own, dn_send, gub, ubuf, dbuf, sems = rest
    shard, core = sc[0], sc[1]
    step = pl.program_id(0)
    width = h2.shape[1]
    height = wup.shape[0]
    half, part = height // 2, wdown.shape[0] // 2
    take = slice(k * part, (k + 1) * part)
    blocks = []
    for j in range(2):
        mine = pl.ds(pl.multiple_of(shard * height, 16), height)
        pairs = []
        for h in range(2):
            at = pl.multiple_of((2 * ((shard >> 1) ^ j) + h) * width + k * part, 128)
            pairs.append(
                (wup.at[:, pl.ds(at, part)], ubuf.at[j, mine, pl.ds(h * part, part)])
            )
        if j == 0:
            at = pl.multiple_of((shard & 1) * part, 16)
            pairs.append((wdown.at[pl.ds(k * part, part), :], dbuf.at[0, pl.ds(at, part), :]))
        for side in range(2):
            which = core if side == 0 else 1 - core
            for m in range(1, 4):
                piece = pieces[side * 3 + m - 1]
                at = pl.multiple_of((shard ^ m) * height + which * half, 16)
                g = j ^ (m >> 1)
                pairs.append((piece.at[pl.ds(g * half, half), :], ubuf.at[j, pl.ds(at, half), :]))
                if m >> 1 == j:
                    at = ((shard ^ m) & 1) * part + which * (part // 2)
                    at = pl.multiple_of(at, 16)
                    pairs.append(
                        (
                            piece.at[pl.ds(2 * half, part // 2), :],
                            dbuf.at[j, pl.ds(at, part // 2), :],
                        )
                    )
        blocks.append(run_copies(pairs, sems, 12 * j))

    @pl.when(step == 0)
    def _():
        for c in blocks[0] + blocks[1]:
            c.start()
        for c in blocks[0]:
            c.wait()

    @pl.when(step == 1)
    def _():
        for c in blocks[1]:
            c.wait()

    uw, dw = ubuf[step], dbuf[step]
    x, g = h2[...], dm[...]
    pair = 2 * ((shard >> 1) ^ step)
    bias = jnp.concatenate([sm[pl.ds(UB + pair + h, 1), take] for h in range(2)], axis=1)
    u = dot(x, uw, 1, 0) + bias
    dact = dot(g, dw, 1, 1)
    cdf = 0.5 * (1.0 + lax.erf(u * np.float32(np.sqrt(0.5))))
    act = (u * cdf).astype(BF)
    slope = cdf + u * (jnp.exp(-0.5 * u * u) * np.float32(1.0 / np.sqrt(2.0 * np.pi)))
    du = (dact * slope).astype(BF)
    bsum = jnp.sum(du.astype(F32), axis=0, keepdims=True)
    gd = dot(act, g, 0, 0).astype(BF)
    for h in range(2):
        gub[h] = bsum[:, h * part : (h + 1) * part]
        for i in range(2):
            for n in range(2):
                span = slice(n * part, (n + 1) * part)
                at = h * part + i * half
                store_halves(
                    core,
                    dn_own,
                    dn_send,
                    (h ^ (shard & 1), 2 * i + n),
                    gd[at : at + half, span],
                    gd[at + part // 2 : at + part // 2 + half, span],
                )
    gu = dot(x, du, 0, 0).astype(BF)
    for m in range(4):
        at = m * height
        for h in range(2):
            span = slice(h * part, (h + 1) * part)
            store_halves(
                core,
                up_own,
                up_send,
                (shard ^ m, h),
                gu[at : at + half, span],
                gu[at + half : at + height, span],
            )
    new_down = dot(act, dw, 1, 0)
    new_dh2 = dot(du, uw, 1, 1)

    @pl.when(step == 0)
    def _():
        if k:
            down[...] = old_down[...] + new_down
            dh2[...] = old_dh2[...] + new_dh2
        else:
            down[...] = new_down
            dh2[...] = new_dh2

    @pl.when(step > 0)
    def _():
        down[...] += new_down
        dh2[...] += new_dh2


def mlp_part(sc, h2, dm, sm, wup, wdown, pieces, k, old):
    rows, width = h2.shape
    half, part = wup.shape[0] // 2, wdown.shape[0] // 2
    once = pl.Buffered(1)
    full = lambda a: pl.BlockSpec(a.shape, lambda j, sc: (0,) * a.ndim, pipeline_mode=once)
    whole = pl.BlockSpec((rows, width), lambda j, sc: (0, 0), pipeline_mode=once)
    by_up = pl.BlockSpec((4, 2, half, part), lambda j, sc: (0, (sc[0] >> 1) ^ j, 0, 0))
    by_down = pl.BlockSpec((2, 4, half, part), lambda j, sc: (j, 0, 0, 0))
    shares = SD((4, 4, half, part), BF)
    return pl.pallas_call(
        functools.partial(mlp_kernel, k=k),
        grid_spec=pltpu.PrefetchScalarGridSpec(
            num_scalar_prefetch=1,
            grid=(2,),
            in_specs=[VM] * 3 + [ANY] * 8 + [VM] * len(old),
            out_specs=[VM] * 2
            + [by_up] * 2
            + [by_down] * 2
            + [pl.BlockSpec((2, 1, part), lambda j, sc: ((sc[0] >> 1) ^ j, 0, 0))],
            scratch_shapes=[
                pltpu.VMEM((2, width, width), BF),
                pltpu.VMEM((2, width, width), BF),
                pltpu.SemaphoreType.DMA((24,)),
            ],
        ),
        out_shape=[SD((rows, width), F32)] * 2 + [shares] * 4 + [SD((4, 1, part), F32)],
        input_output_aliases={12: 0, 13: 1} if old else {},
        compiler_params=params(30),
        cost_estimate=cost(26),
        name="mlp%d" % k,
    )(sc, h2, dm, sm, wup, wdown, *pieces, *old)


def after_kernel(sc, down, dh2, mid, cot, keep, sm, o, dm, own, *rest, slots):
    pieces = rest[:6]
    out, dmid, do, g_own, g_send, gs, wbuf, sems = rest[6:]
    images, count, width = cot.shape
    every = pl.ds(0, width)
    height = own.shape[0]
    copies = run_copies(
        place_rows(wbuf, sc, (own, every), pieces, every, pl.ds(width, width), height), sems
    )
    for c in copies:
        c.start()
    e0 = dh2[...]
    xhat, rsq = normalized(mid[...])
    gs[...] = jnp.zeros_like(gs)
    gs[1:2, :] = jnp.sum(e0 * xhat, axis=0, keepdims=True)
    gs[2:3, :] = jnp.sum(e0, axis=0, keepdims=True)
    gs[3:4, :] = jnp.sum(dm[...].astype(F32), axis=0, keepdims=True)
    dmid[...] = norm_back(e0 * sm[G2 : G2 + 1, :], xhat, rsq)
    for i in range(images):
        sl = slice(i * slots, i * slots + count)
        dmid[sl, :] += cot[i].astype(F32) * keep[sl, :]
        out[i] = (keep[sl, :] * (mid[sl, :] + down[sl, :] + sm[DB : DB + 1, :])).astype(BF)
    low = dmid[...].astype(BF)
    gs[0:1, :] = jnp.sum(low.astype(F32), axis=0, keepdims=True)
    for c in copies:
        c.wait()
    do[...] = dot(low, wbuf[...], 1, 1).astype(BF)
    gw = dot(o[...], low, 0, 0).astype(BF)
    half, part = height // 2, width // 2
    for m in range(4):
        for j in range(2):
            cols = slice(j * part, (j + 1) * part)
            at = m * height
            store_halves(
                sc[1],
                g_own,
                g_send,
                (sc[0] ^ m, j),
                gw[at : at + half, cols],
                gw[at + half : at + height, cols],
            )


def after_mlp(sc, down, dh2, mid, cot, keep, sm, o, dm, own, pieces, slots):
    rows, width = o.shape
    half, part = own.shape[0] // 2, width // 2
    full = lambda a: pl.BlockSpec(a.shape, lambda j, sc: (0,) * a.ndim)
    whole = pl.BlockSpec((rows, width), lambda j, sc: (0, 0))
    share = pl.BlockSpec((4, 2, half, part), lambda j, sc: (0, 3, 0, 0))
    return pl.pallas_call(
        functools.partial(after_kernel, slots=slots),
        grid_spec=pltpu.PrefetchScalarGridSpec(
            num_scalar_prefetch=1,
            grid=(1,),
            in_specs=[VM] * 8 + [ANY] * 7,
            out_specs=[VM] * 3 + [share] * 2 + [VM],
            scratch_shapes=[pltpu.VMEM((width, width), BF), pltpu.SemaphoreType.DMA((7,))],
        ),
        out_shape=[SD(cot.shape, BF), SD((rows, width), F32), SD((rows, width), BF)]
        + [SD((4, 8, half, part), BF)] * 2
        + [SD((8, width), F32)],
        compiler_params=params(24),
        cost_estimate=cost(15),
        name="after_mlp",
    )(sc, down, dh2, mid, cot, keep, sm, o, dm, own, *pieces)


def project_grad_kernel(sc, h1, dx, old_own, old_send, g_own, g_send, gs, *, height):
    half, part = height // 2, dx.shape[1] // 2
    low = dx[...]
    gs[0] = jnp.broadcast_to(jnp.sum(low.astype(F32), axis=0, keepdims=True), gs.shape[1:])
    gw = dot(h1[...], low, 0, 0).astype(BF)
    for m in range(4):
        for j in range(2):
            cols = slice(j * part, (j + 1) * part)
            at = m * height
            store_halves(
                sc[1],
                g_own,
                g_send,
                (sc[0] ^ m, j),
                gw[at : at + half, cols],
                gw[at + half : at + height, cols],
            )


def project_grad(sc, h1, dx, g_own, g_send, height):
    rows, width = h1.shape
    half, part = height // 2, width // 2
    share = pl.BlockSpec((4, 2, half, part), lambda j, sc: (0, j, 0, 0))
    return pl.pallas_call(
        functools.partial(project_grad_kernel, height=height),
        grid_spec=pltpu.PrefetchScalarGridSpec(
            num_scalar_prefetch=1,
            grid=(3,),
            in_specs=[
                VM,
                pl.BlockSpec((rows, width), lambda j, sc: (0, j)),
                ANY,
                ANY,
            ],
            out_specs=[share, share, pl.BlockSpec((1, 8, width), lambda j, sc: (j, 0, 0))],
        ),
        out_shape=[SD((4, 8, half, part), BF)] * 2 + [SD((3, 8, width), F32)],
        input_output_aliases={3: 0, 4: 1},
        compiler_params=params(20),
        cost_estimate=cost(10),
        name="project_grad",
    )(sc, h1, dx, g_own, g_send)


def tokens_grad_kernel(sc, dx, tok, sm, dmid, ga, gp, gu0, gu1, own, *rest, slots):
    pp, pq = rest[:6], rest[6:12]
    out, gs, wbuf, acc, sems = rest[12:]
    images, count, width = tok.shape
    height = own.shape[0]
    two, third = pl.ds(0, 2 * width), pl.ds(2 * width, width)
    pairs = place_rows(wbuf, sc, (own, two), pp, two, two, height)
    pairs += place_rows(wbuf, sc, (own, third), pq, third, pl.ds(0, width), height)
    copies = run_copies(pairs, sems)
    for c in copies:
        c.start()
    gs[...] = jnp.zeros_like(gs)
    gs[OB : OB + 4, :] = ga[0:4, :]
    gs[QB : QB + 1, :] = gp[0, 0:1, :]
    gs[VB : VB + 1, :] = gp[2, 0:1, :]
    for b in range(4):
        gs[UB + b : UB + b + 1, : width // 2] = gu0[b]
        gs[UB + b : UB + b + 1, width // 2 :] = gu1[b]
    for c in copies:
        c.wait()
    acc[...] = dot(dx[...], wbuf[...], 1, 1)
    gain = jnp.zeros((1, width), F32)
    shift = jnp.zeros((1, width), F32)
    for i in range(images):
        sl = slice(i * slots, i * slots + count)
        e0 = acc[sl, :]
        xhat, rsq = normalized(tok[i].astype(F32))
        gain += jnp.sum(e0 * xhat, axis=0, keepdims=True)
        shift += jnp.sum(e0, axis=0, keepdims=True)
        out[i] = (dmid[sl, :] + norm_back(e0 * sm[G1 : G1 + 1, :], xhat, rsq)).astype(BF)
    gs[G1 : G1 + 1, :] = gain
    gs[B1 : B1 + 1, :] = shift


def tokens_grad(sc, dx, tok, sm, dmid, ga, gp, gu0, gu1, own, pieces, slots):
    rows, width = dmid.shape
    full = lambda a: pl.BlockSpec(a.shape, lambda j, sc: (0,) * a.ndim)
    operands = (dx, tok, sm, dmid, ga, gp, gu0, gu1)
    return pl.pallas_call(
        functools.partial(tokens_grad_kernel, slots=slots),
        grid_spec=pltpu.PrefetchScalarGridSpec(
            num_scalar_prefetch=1,
            grid=(1,),
            in_specs=[VM] * len(operands) + [ANY] * 13,
            out_specs=[VM] * 2,
            scratch_shapes=[
                pltpu.VMEM((width, 3 * width), BF),
                pltpu.VMEM((rows, width), F32),
                pltpu.SemaphoreType.DMA((14,)),
            ],
        ),
        out_shape=[SD(tok.shape, BF), SD((16, width), F32)],
        compiler_params=params(24),
        cost_estimate=cost(13),
        name="tokens_grad",
    )(sc, *operands, own, *pieces)


def lay_kernel(sc, *refs, kind):
    core, odd = sc[1], sc[2] % 2
    ins, (wide, tall) = refs[:-2], refs[-2:]
    half, part = ins[0].shape[1:]

    def put(k, side, first, second):
        which = core if side == 0 else 1 - core
        rows = pl.ds(pl.multiple_of(which * half, 8), half)
        if kind == "mlp":
            for b in range(4):
                wide[rows, pl.ds((2 * b + k) * part, part)] = first[b].astype(F32)
            for i in range(2):
                at = pl.multiple_of(which * 2 * half + (k * 4 + i) * half, 8)
                for j in range(2):
                    tall[pl.ds(at, half), pl.ds(j * part, part)] = second[2 * i + j].astype(F32)
        else:
            for n in range(4):
                wide[rows, pl.ds(n * part, part)] = first[n].astype(F32)
            for n in range(2):
                wide[rows, pl.ds((4 + n) * part, part)] = second[n].astype(F32)
                tall[rows, pl.ds(n * part, part)] = second[2 + n].astype(F32)

    for k in range(len(ins) // 4):
        kept, other, skept, sother = ins[4 * k : 4 * k + 4]

        @pl.when(odd == 0)
        def _(k=k, kept=kept, other=other, skept=skept, sother=sother):
            put(k, 0, kept, other)
            put(k, 1, skept, sother)

        @pl.when(odd != 0)
        def _(k=k, kept=kept, other=other, skept=skept, sother=sother):
            put(k, 0, other, kept)
            put(k, 1, sother, skept)


def lay_out(sc, finals, kind, shapes):
    full = lambda s: pl.BlockSpec(s, lambda j, sc: (0,) * len(s))
    flat = [a for group in finals for a in group]
    return pl.pallas_call(
        functools.partial(lay_kernel, kind=kind),
        grid_spec=pltpu.PrefetchScalarGridSpec(
            num_scalar_prefetch=1,
            grid=(1,),
            in_specs=[VM] * len(flat),
            out_specs=[VM] * 2,
        ),
        out_shape=[SD(s, F32) for s in shapes],
        compiler_params=params(8),
        cost_estimate=cost(4),
        name="lay_" + kind,
    )(sc, *flat)


def hops():
    def table(move):
        pairs = []
        for dp in range(8):
            for fs in range(4):
                z, core, shard = move(dp // 2, dp % 2, fs)
                pairs.append((dp * 4 + fs, (z * 2 + core) * 4 + shard))
        return pairs

    moves = {
        "sib": lambda z, c, f: (z, 1 - c, f),
        "x": lambda z, c, f: (z, c, f ^ 1),
        "y": lambda z, c, f: (z, c, f ^ 2),
        "xy": lambda z, c, f: (z, c, f ^ 3),
        "z1": lambda z, c, f: (z ^ 1, c, f),
        "z2": lambda z, c, f: (z ^ 2, c, f),
        "z3": lambda z, c, f: (z ^ 3, c, f),
    }
    tables = {name: table(move) for name, move in moves.items()}
    return lambda value, name: lax.ppermute(value, ("dp", "fsdp"), tables[name])


class Transfer:
    def __init__(self, stages):
        self.stages = stages
        self.flying = next(stages)
        self.result = None

    def step(self, landed):
        try:
            self.flying = self.stages.send(landed)
        except StopIteration as end:
            self.flying, self.result = (), end.value


def advance(held, *transfers):
    values = lax.optimization_barrier((held, tuple(t.flying for t in transfers)))
    for t, landed in zip(transfers, values[1]):
        t.step(landed)
    return values[0]


def follow(lead, *transfers):
    landed = lax.optimization_barrier(tuple(lead.flying))
    lead.step(landed)
    values = lax.optimization_barrier((landed, tuple(t.flying for t in transfers)))
    for t, got in zip(transfers, values[1]):
        t.step(got)


PLANE = ("x", "y", "xy")
LINE = ("z1", "z2", "z3")


def gather_stages(hop, own):
    far = yield tuple(hop(own, name) for name in PLANE)
    near = yield tuple(hop(a, "sib") for a in far)
    return tuple(far) + tuple(near)


def small_stages(hop, own):
    return (own,) + tuple((yield tuple(hop(own, name) for name in PLANE)))


def add(a, b):
    return (a.astype(F32) + b.astype(F32)).astype(BF)


def line_stages(hop, even, total):
    parts = total.shape[0] // 2
    keep = jnp.where(even, total[:parts], total[parts:])
    give = jnp.where(even, total[parts:], total[:parts]).astype(BF)
    (got,) = yield (hop(give, "z1"),)
    half = lax.optimization_barrier((keep + got.astype(F32)).astype(BF))
    (got,) = yield (hop(half, "z2"),)
    kept = add(half, got)
    other, skept = yield (hop(kept, "z1"), hop(kept, "sib"))
    (sother,) = yield (hop(other, "sib"),)
    return kept, other, skept, sother


def plane_stages(hop, even, chip):
    got = yield tuple(hop(chip(r).astype(BF), name) for r, name in enumerate(PLANE, 1))
    total = chip(0)
    for a in got:
        total = total + a.astype(F32)
    return (yield from line_stages(hop, even, total))


def ffn_stages(hop, even, up_own, up_send, dn_own, dn_send):
    up_got, dn_got = yield (hop(up_send, "sib"), hop(dn_send, "sib"))

    def chip(r):
        return jnp.concatenate(
            [
                up_own[r].astype(F32) + up_got[r].astype(F32),
                dn_own[r].astype(F32) + dn_got[r].astype(F32),
            ]
        )

    return (yield from plane_stages(hop, even, chip))


def attn_stages(hop, even, own, send):
    (got,) = yield (hop(send, "sib"),)
    chip = lambda r: own[r].astype(F32) + got[r].astype(F32)
    return (yield from plane_stages(hop, even, chip))


def sum_stages(hop, value):
    (got,) = yield (hop(value, "sib"),)
    value = value + got
    for names in (PLANE, LINE):
        one, two, three = yield tuple(hop(value, name) for name in names)
        value = (value + one) + (two + three)
    return value


def on_device_fast(
    tokens,
    mask,
    cotangent,
    ln1_gain,
    ln1_bias,
    w_qkv,
    qv_bias,
    w_out,
    out_bias,
    ln2_gain,
    ln2_bias,
    w_up,
    up_bias,
    w_down,
    down_bias,
):
    images, count, width = tokens.shape
    slots = -(-count // 8) * 8
    height = w_out.shape[0]
    half, part = height // 2, width // 2
    hop = hops()
    shard = lax.axis_index("fsdp")
    dp = lax.axis_index("dp")
    sc = jnp.stack([shard, dp % 2, dp // 2]).astype(jnp.int32)
    even = (dp // 2) % 2 == 0

    tie = lax.optimization_barrier
    small = (ln1_gain, ln1_bias, qv_bias, out_bias, ln2_gain, ln2_bias, down_bias, up_bias)
    top, bottom = pack_attn(sc, w_qkv, w_out, small)
    px, py, qx, qy = hop(top, "x"), hop(top, "y"), hop(bottom, "x"), hop(bottom, "y")
    own0, own1 = pack(sc, pack_ffn_kernel, 10, [(2 * height, width)] * 2, w_up, w_down)
    px, py, qx, qy, own0, own1 = tie((px, py, qx, qy, own0, own1))
    pfar, qfar = hop(px, "y"), hop(qy, "x")
    near = tuple(hop(a, "sib") for a in (px, py, qx, qy))
    pfar, qfar, near, own0, own1 = tie((pfar, qfar, near, own0, own1))
    spfar, sqfar = hop(pfar, "sib"), hop(qfar, "sib")
    ffn0 = Transfer(gather_stages(hop, own0))
    sc, spfar, sqfar = tie((sc, spfar, sqfar))
    pieces_p = (px, py, pfar, near[0], near[1], spfar)
    pieces_q = (qx, qy, qfar, near[2], near[3], sqfar)
    pieces = pieces_p + pieces_q

    keep = jnp.pad(mask.astype(F32), ((0, 0), (0, slots - count)))
    mask_row = keep.reshape(images, 1, slots)
    keep_col = keep.reshape(images * slots, 1)

    h1, qkv, sm = project(sc, tokens, w_qkv, top, pieces, slots)
    o = attend(qkv, mask_row, slots)
    o, own1 = tie((o, own1))
    ffn1 = Transfer(gather_stages(hop, own1))
    mid, h2, dm = middle_part(sc, tokens, o, sm, cotangent, keep_col, w_out, pieces_q, slots)
    h2 = advance(h2, ffn0)
    sc = advance(sc, ffn0)
    down, dh2, *shares, gu0 = mlp_part(sc, h2, dm, sm, w_up, w_down, ffn0.result, 0, ())
    down, dh2, *shares = advance((down, dh2, *shares), ffn1)
    m0 = Transfer(ffn_stages(hop, even, *shares))
    sc = advance(sc, ffn1, m0)
    down, dh2, *shares, gu1 = mlp_part(
        sc, h2, dm, sm, w_up, w_down, ffn1.result, 1, (down, dh2)
    )
    down, dh2, *shares = advance((down, dh2, *shares), m0)
    m1 = Transfer(ffn_stages(hop, even, *shares))
    layer_out, dmid, do, g_own, g_send, ga = after_mlp(
        sc, down, dh2, mid, cotangent, keep_col, sm, o, dm, w_out, pieces_q, slots
    )
    do = advance(do, m0, m1)
    dx = attend_back(qkv, do, keep_col, slots)
    dx = advance(dx, m0)
    g_own, g_send, gp = project_grad(sc, h1, dx, g_own, g_send, height)
    g_own, g_send, dx = advance((g_own, g_send, dx), m0, m1)
    attn = Transfer(attn_stages(hop, even, g_own, g_send))
    sc = advance(sc, attn)
    sc = advance(sc, m1)
    grad_tokens, gs = tokens_grad(
        sc, dx, tokens, sm, dmid, ga, gp, gu0, gu1, w_qkv, pieces, slots
    )
    gs = advance(gs, m0, m1, attn)
    total = Transfer(sum_stages(hop, gs))
    advance((), total)
    follow(attn, m1, total)
    ffn = advance((), m1)
    ffn = lay_out(
        sc, (m0.result, m1.result), "mlp", ((height, 4 * width), (4 * height, width))
    )
    follow(attn, total)
    gs = total.result

    def mine(r, n=1):
        return lax.dynamic_slice(gs[r : r + n].reshape(-1), (shard * (n * height),), (n * height,))

    rows = tuple(mine(r) for r in (G1, B1, OB, G2, B2, DB)) + (mine(QB, 2), mine(UB, 4))
    rows = advance(rows, attn)
    ffn, rows = advance((ffn, rows), attn)
    g1, b1, ob, g2, b2, db, qvb, ub = rows
    grad_w_up, grad_w_down = ffn
    grad_w_qkv, grad_w_out = lay_out(
        sc, (attn.result,), "attn", ((height, 3 * width), (height, width))
    )
    return (
        layer_out,
        grad_tokens,
        g1,
        b1,
        grad_w_qkv,
        qvb,
        grad_w_out,
        ob,
        g2,
        b2,
        grad_w_up,
        ub,
        grad_w_down,
        db,
    )


def norm(values, gain, shift):
    mean_value = jnp.mean(values, axis=-1, keepdims=True)
    centred = values - mean_value
    variance = jnp.mean(centred * centred, axis=-1, keepdims=True)
    return centred * lax.rsqrt(variance + EPS) * gain + shift


def gelu_exact(values):
    return jax.nn.gelu(values, approximate=False)


def score_block(query, key_part, valid):
    scores = jnp.einsum(
        "iqhe,ikhe->ihqk", query, key_part, preferred_element_type=jnp.float32
    ) * HD ** (-0.5)
    return jnp.where(valid, scores, -1e30)


def arrange(grad, groups, copies):
    shaped = grad.reshape((groups, copies, grad.shape[0] // (groups * copies)) + grad.shape[1:])
    return jnp.swapaxes(shaped, 0, 1).reshape(grad.shape)


def reduce_six(grad_one, grad_two, grad_three, grad_four, grad_five, grad_six):
    groups = lax.axis_size("fsdp")
    copies = lax.axis_size("dp")
    pieces = (
        lax.psum_scatter(
            arrange(grad_one, groups, copies), ("dp", "fsdp"), scatter_dimension=0, tiled=True
        ),
        lax.psum_scatter(
            arrange(grad_two, groups, copies), ("dp", "fsdp"), scatter_dimension=0, tiled=True
        ),
        lax.psum_scatter(
            arrange(grad_three, groups, copies), ("dp", "fsdp"), scatter_dimension=0, tiled=True
        ),
        lax.psum_scatter(
            arrange(grad_four, groups, copies), ("dp", "fsdp"), scatter_dimension=0, tiled=True
        ),
        lax.psum_scatter(
            arrange(grad_five, groups, copies), ("dp", "fsdp"), scatter_dimension=0, tiled=True
        ),
        lax.psum_scatter(
            arrange(grad_six, groups, copies), ("dp", "fsdp"), scatter_dimension=0, tiled=True
        ),
    )
    return (
        lax.all_gather(pieces[0].astype(jnp.bfloat16), "dp", axis=0, tiled=True).astype(
            jnp.float32
        ),
        lax.all_gather(pieces[1].astype(jnp.bfloat16), "dp", axis=0, tiled=True).astype(
            jnp.float32
        ),
        lax.all_gather(pieces[2].astype(jnp.bfloat16), "dp", axis=0, tiled=True).astype(
            jnp.float32
        ),
        lax.all_gather(pieces[3].astype(jnp.bfloat16), "dp", axis=0, tiled=True).astype(
            jnp.float32
        ),
        lax.all_gather(pieces[4].astype(jnp.bfloat16), "dp", axis=0, tiled=True).astype(
            jnp.float32
        ),
        lax.all_gather(pieces[5].astype(jnp.bfloat16), "dp", axis=0, tiled=True).astype(
            jnp.float32
        ),
    )


def on_device(
    tokens,
    mask,
    cotangent,
    ln1_gain,
    ln1_bias,
    w_qkv,
    qv_bias,
    w_out,
    out_bias,
    ln2_gain,
    ln2_bias,
    w_up,
    up_bias,
    w_down,
    down_bias,
):
    image_count, slot_count, width = tokens.shape
    row_count = image_count * slot_count
    heads = width // HD
    scale = HD ** (-0.5)
    attn_full = (
        lax.all_gather(ln1_gain, "fsdp", axis=0, tiled=True),
        lax.all_gather(ln1_bias, "fsdp", axis=0, tiled=True),
        lax.all_gather(w_qkv, "fsdp", axis=0, tiled=True),
        lax.all_gather(qv_bias, "fsdp", axis=0, tiled=True),
        lax.all_gather(w_out, "fsdp", axis=0, tiled=True),
        lax.all_gather(out_bias, "fsdp", axis=0, tiled=True),
    )
    mlp_full = (
        lax.all_gather(ln2_gain, "fsdp", axis=0, tiled=True),
        lax.all_gather(ln2_bias, "fsdp", axis=0, tiled=True),
        lax.all_gather(w_up, "fsdp", axis=0, tiled=True),
        lax.all_gather(up_bias, "fsdp", axis=0, tiled=True),
        lax.all_gather(w_down, "fsdp", axis=0, tiled=True),
        lax.all_gather(down_bias, "fsdp", axis=0, tiled=True),
    )
    gain_one, shift_one, qkv_weight, qkv_shift, out_weight, out_shift = attn_full
    gain_two, shift_two, up_weight, up_shift, down_weight, down_shift = mlp_full
    keep = mask.astype(jnp.float32)
    valid = (keep > 0.5)[:, None, None, :]
    keep_rows = keep.reshape(row_count, 1)
    inputs = tokens.astype(jnp.float32).reshape(row_count, width)
    normed_one, norm_one_back = jax.vjp(
        norm, inputs, gain_one.astype(jnp.float32), shift_one.astype(jnp.float32)
    )
    normed_low = normed_one.astype(jnp.bfloat16)
    qv_float = qkv_shift.astype(jnp.float32)
    full_bias = jnp.concatenate(
        [qv_float[:width], jnp.zeros((width,), jnp.float32), qv_float[width:]]
    )
    projected = (
        jnp.dot(normed_low, qkv_weight, preferred_element_type=jnp.float32) + full_bias
    ).astype(jnp.bfloat16)
    query = projected[:, :width].reshape(image_count, slot_count, heads, HD)
    key_part = projected[:, width : 2 * width].reshape(image_count, slot_count, heads, HD)
    value = projected[:, 2 * width :].reshape(image_count, slot_count, heads, HD)
    scores = score_block(query, key_part, valid)
    top = jnp.max(scores, axis=-1, keepdims=True)
    lse = top + jnp.log(jnp.sum(jnp.exp(scores - top), axis=-1, keepdims=True))
    probs_low = jnp.exp(scores - lse).astype(jnp.bfloat16)
    mixed = jnp.einsum("ihqk,ikhe->iqhe", probs_low, value, preferred_element_type=jnp.float32)
    mixed = mixed.reshape(row_count, width).astype(jnp.bfloat16)
    middle = (
        inputs
        + jnp.dot(mixed, out_weight, preferred_element_type=jnp.float32)
        + out_shift.astype(jnp.float32)
    )
    normed_two, norm_two_back = jax.vjp(
        norm, middle, gain_two.astype(jnp.float32), shift_two.astype(jnp.float32)
    )
    normed_two_low = normed_two.astype(jnp.bfloat16)
    upward = jnp.dot(
        normed_two_low, up_weight, preferred_element_type=jnp.float32
    ) + up_shift.astype(jnp.float32)
    active, gelu_back = jax.vjp(gelu_exact, upward)
    active_low = active.astype(jnp.bfloat16)
    downward = jnp.dot(
        active_low, down_weight, preferred_element_type=jnp.float32
    ) + down_shift.astype(jnp.float32)
    layer_out = (
        (keep_rows * (middle + downward))
        .astype(jnp.bfloat16)
        .reshape(image_count, slot_count, width)
    )
    mlp_back = (
        lax.all_gather(ln2_gain, "fsdp", axis=0, tiled=True),
        lax.all_gather(ln2_bias, "fsdp", axis=0, tiled=True),
        lax.all_gather(w_up, "fsdp", axis=0, tiled=True),
        lax.all_gather(up_bias, "fsdp", axis=0, tiled=True),
        lax.all_gather(w_down, "fsdp", axis=0, tiled=True),
        lax.all_gather(down_bias, "fsdp", axis=0, tiled=True),
    )
    up_back = mlp_back[2]
    down_back = mlp_back[4]
    grad_rows = cotangent.astype(jnp.float32).reshape(row_count, width) * keep_rows
    grad_down_low = grad_rows.astype(jnp.bfloat16)
    grad_w_down = jnp.einsum(
        "rf,rd->fd", active_low, grad_down_low, preferred_element_type=jnp.float32
    )
    grad_down_bias = jnp.sum(grad_down_low, axis=0, dtype=jnp.float32)
    grad_active = jnp.einsum(
        "rd,fd->rf", grad_down_low, down_back, preferred_element_type=jnp.float32
    )
    grad_up_low = gelu_back(grad_active)[0].astype(jnp.bfloat16)
    grad_w_up = jnp.einsum(
        "rd,rf->df", normed_two_low, grad_up_low, preferred_element_type=jnp.float32
    )
    grad_up_bias = jnp.sum(grad_up_low, axis=0, dtype=jnp.float32)
    grad_normed_two = jnp.einsum(
        "rf,df->rd", grad_up_low, up_back, preferred_element_type=jnp.float32
    )
    grad_mid_norm, grad_ln2_gain, grad_ln2_bias = norm_two_back(grad_normed_two)
    grad_middle = grad_rows + grad_mid_norm
    mlp_grads = reduce_six(
        grad_ln2_gain, grad_ln2_bias, grad_w_up, grad_up_bias, grad_w_down, grad_down_bias
    )
    attn_back = (
        lax.all_gather(ln1_gain, "fsdp", axis=0, tiled=True),
        lax.all_gather(ln1_bias, "fsdp", axis=0, tiled=True),
        lax.all_gather(w_qkv, "fsdp", axis=0, tiled=True),
        lax.all_gather(qv_bias, "fsdp", axis=0, tiled=True),
        lax.all_gather(w_out, "fsdp", axis=0, tiled=True),
        lax.all_gather(out_bias, "fsdp", axis=0, tiled=True),
    )
    qkv_back = attn_back[2]
    out_back = attn_back[4]
    grad_attn_low = grad_middle.astype(jnp.bfloat16)
    grad_w_out = jnp.einsum("rd,re->de", mixed, grad_attn_low, preferred_element_type=jnp.float32)
    grad_out_bias = jnp.sum(grad_attn_low, axis=0, dtype=jnp.float32)
    grad_mixed = jnp.einsum(
        "re,de->rd", grad_attn_low, out_back, preferred_element_type=jnp.float32
    )
    grad_mixed = grad_mixed.astype(jnp.bfloat16).reshape(image_count, slot_count, heads, HD)
    probs = jnp.exp(score_block(query, key_part, valid) - lse)
    probs_again = probs.astype(jnp.bfloat16)
    grad_value = jnp.einsum(
        "ihqk,iqhe->ikhe", probs_again, grad_mixed, preferred_element_type=jnp.float32
    )
    grad_probs = jnp.einsum(
        "iqhe,ikhe->ihqk", grad_mixed, value, preferred_element_type=jnp.float32
    )
    inner = jnp.sum(grad_probs * probs, axis=-1, keepdims=True)
    grad_scores = (probs * (grad_probs - inner)).astype(jnp.bfloat16)
    grad_query = (
        jnp.einsum("ihqk,ikhe->iqhe", grad_scores, key_part, preferred_element_type=jnp.float32)
        * scale
    )
    grad_key = (
        jnp.einsum("ihqk,iqhe->ikhe", grad_scores, query, preferred_element_type=jnp.float32)
        * scale
    )
    grad_projected = jnp.concatenate(
        [
            grad_query.reshape(row_count, width),
            grad_key.reshape(row_count, width),
            grad_value.reshape(row_count, width),
        ],
        axis=1,
    ).astype(jnp.bfloat16)
    grad_w_qkv = jnp.einsum(
        "rd,re->de", normed_low, grad_projected, preferred_element_type=jnp.float32
    )
    grad_qv_bias = jnp.concatenate(
        [
            jnp.sum(grad_projected[:, :width], axis=0, dtype=jnp.float32),
            jnp.sum(grad_projected[:, 2 * width :], axis=0, dtype=jnp.float32),
        ]
    )
    grad_normed_one = jnp.einsum(
        "re,de->rd", grad_projected, qkv_back, preferred_element_type=jnp.float32
    )
    grad_in_norm, grad_ln1_gain, grad_ln1_bias = norm_one_back(grad_normed_one)
    grad_tokens = (
        (grad_middle + grad_in_norm).astype(jnp.bfloat16).reshape(image_count, slot_count, width)
    )
    attn_grads = reduce_six(
        grad_ln1_gain, grad_ln1_bias, grad_w_qkv, grad_qv_bias, grad_w_out, grad_out_bias
    )
    return (
        layer_out,
        grad_tokens,
        attn_grads[0],
        attn_grads[1],
        attn_grads[2],
        attn_grads[3],
        attn_grads[4],
        attn_grads[5],
        mlp_grads[0],
        mlp_grads[1],
        mlp_grads[2],
        mlp_grads[3],
        mlp_grads[4],
        mlp_grads[5],
    )


def solution(mesh):
    in_specs = (
        P(("dp", "fsdp"), None, None),
        P(("dp", "fsdp"), None),
        P(("dp", "fsdp"), None, None),
        P("fsdp"),
        P("fsdp"),
        P("fsdp", None),
        P("fsdp"),
        P("fsdp", None),
        P("fsdp"),
        P("fsdp"),
        P("fsdp"),
        P("fsdp", None),
        P("fsdp"),
        P("fsdp", None),
        P("fsdp"),
    )
    out_specs = (
        P(("dp", "fsdp"), None, None),
        P(("dp", "fsdp"), None, None),
        P("fsdp"),
        P("fsdp"),
        P("fsdp", None),
        P("fsdp"),
        P("fsdp", None),
        P("fsdp"),
        P("fsdp"),
        P("fsdp"),
        P("fsdp", None),
        P("fsdp"),
        P("fsdp", None),
        P("fsdp"),
    )
    fast = dict(mesh.shape) == {"dp": 8, "fsdp": 4}
    return jax.shard_map(
        on_device_fast if fast else on_device, mesh=mesh, in_specs=in_specs, out_specs=out_specs, check_vma=False
    )
```
